32 devices in a mesh: wide: 8 (over z, y), narrow: 4 (over x, core).
Axes of the slice: x: 2, y: 2, z: 4, core: 2. Of those that a mesh axis runs over, the one named last changes fastest.
Arguments:
- tokens: bfloat16 [4096, 768], P(('wide', 'narrow')), may hold values from -6 to 6
- cotangent: bfloat16 [4096, 768], P(('wide', 'narrow')), may hold values from -6 to 6
- w_qkv: bfloat16 [768, 2304], P(('wide', 'narrow')), may hold values from -0.21875 to 0.21875
- w_attn: bfloat16 [768, 768], P(('wide', 'narrow')), may hold values from -0.21875 to 0.21875
- w_in: bfloat16 [768, 3072], P(('wide', 'narrow')), may hold values from -0.21875 to 0.21875
- w_out: bfloat16 [3072, 768], P(('wide', 'narrow')), may hold values from -0.109375 to 0.109375
- gains_model: bfloat16 [3, 768], P(None, ('wide', 'narrow')), may hold values from 0.5 to 1.5
- biases_model: bfloat16 [7, 768], P(None, ('wide', 'narrow')), may hold values from -2 to 2
- gain_ffn: bfloat16 [3072], P(('wide', 'narrow')), may hold values from 0.5 to 1.5
- biases_ffn: bfloat16 [2, 3072], P(None, ('wide', 'narrow')), may hold values from -2 to 2
- offsets: int32 [3, 12], replicated, may hold values from 0 to 3, as said below
Outputs:
- out_tokens: bfloat16 [4096, 768], P(('wide', 'narrow'))
- grad_tokens: float32 [4096, 768], P(('wide', 'narrow'))
- grad_w_qkv: float32 [768, 2304], P(('wide', 'narrow'))
- grad_w_attn: float32 [768, 768], P(('wide', 'narrow'))
- grad_w_in: float32 [768, 3072], P(('wide', 'narrow'))
- grad_w_out: float32 [3072, 768], P(('wide', 'narrow'))
- grad_gains_model: float32 [3, 768], P(None, ('wide', 'narrow'))
- grad_biases_model: float32 [7, 768], P(None, ('wide', 'narrow'))
- grad_gain_ffn: float32 [3072], P(('wide', 'narrow'))
- grad_biases_ffn: float32 [2, 3072], P(None, ('wide', 'narrow'))
The draws below stay inside these ranges and needn't reach their ends.
Inputs may be any that keep to these rules, and one draw needn't show every extreme that they name: offsets[p, h] is below pattern p's rate (1, 2, 4); in every pattern each offset below its rate is taken by some head.
All inputs are finite; a program needn't handle non-finite values.
Results may differ from the reference program's by a relative error of at most 0.013.
Values may be sent and summed in bfloat16 or wider, within the bound.
No kernel may reach another device: no remote copies, remote signals or barrier semaphores. Data moves between devices by JAX's collectives and lax.ppermute only.
A program may use at most 192 MiB of HBM per device.

```python
import jax
import jax.numpy as jnp
from jax import lax

D = 768
HEADS = 12
HEAD_DIM = 64
FF = 3072
PATTERNS = 3
RATE0 = 1
RATE1 = 2
RATE2 = 4
SEG0 = 512
SEG1 = 512
SEG2 = 512
TOKENS = 4096
N_WIDE = 8


def draw_offsets(key, part):
    dilations = jnp.array([RATE0, RATE1, RATE2], dtype=jnp.int32)
    orders = jnp.stack([jax.random.permutation(jax.random.fold_in(key, pattern + 17), HEADS) for pattern in range(PATTERNS)])
    return (orders.astype(jnp.int32) % dilations[:, None]).astype(jnp.int32)


def block_scale(key, extent, pieces, low, top_value):
    def one(dim, shards_of):
        steps = jax.random.uniform(jax.random.fold_in(jax.random.fold_in(key, 6), dim), (shards_of,), jnp.float32, low / len(pieces), top_value / len(pieces))
        return jnp.repeat(jnp.exp(steps), extent[dim] // shards_of).reshape((-1,) + (1,) * (len(extent) - dim - 1))

    factor_of = one(*pieces[0])
    for cut in pieces[1:]:
        factor_of = factor_of * one(*cut)
    return factor_of


def normal_values(rng, shape, scale, bound, pieces=(), kind=jnp.bfloat16):
    loudness = block_scale(rng, shape, pieces, -0.22, 0.18) if pieces else 1.0
    values = jax.random.normal(rng, shape, jnp.float32) * scale * loudness
    return jnp.minimum(jnp.maximum(values, -bound), bound).astype(kind)


def setup_inputs(seed: int = 0) -> dict:
    key_of = jax.random.split(jax.random.key(seed), 12)
    return {
        "tokens": normal_values(key_of[0], (TOKENS, D), 1.0, 6.0, ((0, 32),)),
        "cotangent": normal_values(key_of[1], (TOKENS, D), 1.0, 6.0, ((0, 32),)),
        "w_qkv": normal_values(key_of[2], (D, 3 * D), D ** -0.5, 0.21875, ((0, 32),)),
        "w_attn": normal_values(key_of[3], (D, D), D ** -0.5, 0.21875, ((0, 32),)),
        "w_in": normal_values(key_of[4], (D, FF), D ** -0.5, 0.21875, ((0, 32),)),
        "w_out": normal_values(key_of[5], (FF, D), FF ** -0.5, 0.109375, ((0, 32),)),
        "gains_model": jnp.clip(1.0 + 0.1 * jax.random.normal(key_of[6], (3, D), jnp.float32), 0.5, 1.5).astype(jnp.bfloat16),
        "biases_model": normal_values(key_of[7], (7, D), 0.3, 2.0, ((1, 32),)),
        "gain_ffn": jnp.clip(1.0 + 0.1 * jax.random.normal(key_of[8], (FF,), jnp.float32), 0.5, 1.5).astype(jnp.bfloat16),
        "biases_ffn": normal_values(key_of[9], (2, FF), 0.3, 2.0, ((1, 32),)),
        "offsets": draw_offsets(jax.random.fold_in(key_of[11], 71), 0),
    }


EPSILON = 1e-05
SCORE_SCALE = 0.125
MASKED = -1e+30
HIGH = lax.Precision.HIGHEST

@jax.custom_vjp
def low(v):
    return lax.optimization_barrier(v.astype(jnp.bfloat16)).astype(jnp.float32)

@jax.custom_vjp
def low_back(v):
    return v

def low_keep(v):
    return (low(v), None)

def low_pass(kept, grad):
    return (grad,)

def back_keep(v):
    return (v, None)

def back_low(kept, grad):
    return (low(grad),)
low.defvjp(low_keep, low_pass)
low_back.defvjp(back_keep, back_low)

def layer_norm(values, norm_gain, norm_shift):
    average = lax.optimization_barrier(jnp.mean(values, axis=-1, keepdims=True))
    centred = values - average
    spread = lax.optimization_barrier(jnp.mean(centred * centred, axis=-1, keepdims=True))
    return centred * lax.rsqrt(spread + EPSILON) * norm_gain + norm_shift

def dense(former, latter):
    return jnp.dot(former, latter, precision=HIGH, preferred_element_type=jnp.float32)

def head_attention(operands):
    head_q, head_k, head_v, head_offsets = operands
    length = head_q.shape[0]
    settings = ((SEG0, RATE0), (SEG1, RATE1), (SEG2, RATE2))
    kept = []
    partial_value = []
    for pattern in range(3):
        segment, dilation = settings[pattern]
        selector = (jnp.arange(dilation) == head_offsets[pattern]).astype(jnp.float32)
        members = segment // dilation

        def pick_rows(values):
            shaped = values.reshape(length // dilation, dilation, HEAD_DIM)
            picked = lax.optimization_barrier(jnp.sum(shaped * selector[None, :, None], axis=1))
            return picked.reshape(length // segment, members, HEAD_DIM)
        allowed = jnp.arange(members)[None, :] <= jnp.arange(members)[:, None]
        scores = low_back(jnp.einsum('gqd,gkd->gqk', pick_rows(head_q), pick_rows(head_k), precision=HIGH) * SCORE_SCALE)
        scores = jnp.where(allowed[None], scores, MASKED)
        seg_lse = jax.nn.logsumexp(scores, axis=2)
        dense_lse = jnp.where(selector[None, :] > 0, seg_lse.reshape(length // dilation)[:, None], MASKED)
        partial_value.append(dense_lse.reshape(length))
        kept.append((selector, dilation, segment, members, allowed, scores, pick_rows(head_v)))
    totals = jax.nn.logsumexp(jnp.stack(partial_value), axis=0)
    result = jnp.zeros((length, HEAD_DIM), jnp.float32)
    for selector, dilation, segment, members, allowed, scores, picked_v in kept:
        seg_totals = lax.optimization_barrier(jnp.sum(totals.reshape(length // dilation, dilation) * selector[None, :], axis=1))
        seg_totals = seg_totals.reshape(length // segment, members)
        probability = low(jnp.where(allowed[None], jnp.exp(scores - seg_totals[:, :, None]), 0.0))
        seg_out = jnp.einsum('gqk,gkd->gqd', probability, picked_v, precision=HIGH)
        placed = seg_out.reshape(length // dilation, 1, HEAD_DIM) * selector[None, :, None]
        result = result + placed.reshape(length, HEAD_DIM)
    return result

def attention(queries, keys, values, offsets):
    length = queries.shape[0]

    def head_major(array):
        return array.reshape(length, HEADS, HEAD_DIM).transpose(1, 0, 2)
    heads_out = lax.map(jax.checkpoint(head_attention), (head_major(queries), head_major(keys), head_major(values), offsets.T))
    return heads_out.transpose(1, 0, 2).reshape(length, HEADS * HEAD_DIM)

def layer(inputs, w_qkv, w_attn, w_in, w_out, gains_model, biases_model, gain_ffn, biases_ffn, offsets):
    width = inputs.shape[1]
    normed_one = layer_norm(inputs, gains_model[0], biases_model[0])
    projected = dense(low(normed_one), w_qkv)
    queries = low(low_back(projected[:, :width] + biases_model[1]))
    keys = low(low_back(projected[:, width:2 * width]))
    values = low(low_back(projected[:, 2 * width:] + biases_model[2]))
    attended = low_back(attention(queries, keys, values, offsets))
    sub_normed = layer_norm(attended, gains_model[1], biases_model[3])
    branch = low_back(dense(low(sub_normed), w_attn) + biases_model[4])
    middle = inputs + branch
    normed_two = layer_norm(middle, gains_model[2], biases_model[5])
    pre_act = low_back(dense(low(normed_two), w_in) + biases_ffn[0])
    activated = jax.nn.gelu(pre_act, approximate=False)
    ffn_normed = layer_norm(activated, gain_ffn, biases_ffn[1])
    ffn_branch = low_back(dense(low(ffn_normed), w_out) + biases_model[6])
    return middle + ffn_branch

def reference(tokens, cotangent, w_qkv, w_attn, w_in, w_out, gains_model, biases_model, gain_ffn, biases_ffn, offsets):
    params = (w_qkv.astype(jnp.float32), w_attn.astype(jnp.float32), w_in.astype(jnp.float32), w_out.astype(jnp.float32), gains_model.astype(jnp.float32), biases_model.astype(jnp.float32), gain_ffn.astype(jnp.float32), biases_ffn.astype(jnp.float32))
    group_inputs = tokens.astype(jnp.float32).reshape(N_WIDE, SEG2, D)
    group_cots = cotangent.astype(jnp.float32).reshape(N_WIDE, SEG2, D)

    def forward(inputs, *weights):
        return layer(inputs, *weights, offsets)

    def one_group(totals, item):
        inputs, cots = item
        result, pull = jax.vjp(forward, inputs, *params)
        grads = pull(cots)
        totals = tuple((total + grad for total, grad in zip(totals, grads[1:])))
        return (totals, (result, grads[0]))
    start = tuple((jnp.zeros(param.shape, jnp.float32) for param in params))
    sums, (results, input_grads) = lax.scan(one_group, start, (group_inputs, group_cots))
    return (results.reshape(TOKENS, D).astype(jnp.bfloat16), input_grads.reshape(TOKENS, D), sums[0], sums[1], sums[2], sums[3], sums[4], sums[5], sums[6], sums[7])
```

```python
import jax
import jax.numpy as jnp
from jax import lax
from jax.experimental import pallas as pl
from jax.experimental.pallas import tpu as pltpu
from jax.sharding import PartitionSpec as P

HEADS = 12
HEAD_DIM = 64
RATE0 = 1
RATE1 = 2
RATE2 = 4


EPSILON = 1e-05
SCORE_SCALE = 0.125
MASKED = -1e30


def layer_norm(values, norm_gain, norm_shift):
    average = jnp.mean(values, axis=-1, keepdims=True)
    centred = values - average
    spread = jnp.mean(centred * centred, axis=-1, keepdims=True)
    return centred * lax.rsqrt(spread + EPSILON) * norm_gain + norm_shift


def gelu_exact(values):
    return jax.nn.gelu(values, approximate=False)


def product(former, latter):
    return jnp.dot(former, latter, preferred_element_type=jnp.float32)


def product_tn(former, latter):
    return lax.dot_general(
        former, latter, (((0,), (0,)), ((), ())), preferred_element_type=jnp.float32
    )


def product_nt(former, latter):
    return lax.dot_general(
        former, latter, (((1,), (1,)), ((), ())), preferred_element_type=jnp.float32
    )


def one_hot(offset_row, dilation):
    return (jnp.arange(dilation)[:, None] == offset_row[None, :]).astype(jnp.float32)


def select_rows(dense_rows, selector, dilation):
    picked_rows = dense_rows.shape[0] // dilation
    shaped = dense_rows.reshape(picked_rows, dilation, HEADS, HEAD_DIM)
    picked = jnp.einsum(
        "trhd,rh->thd",
        shaped,
        selector.astype(dense_rows.dtype),
        preferred_element_type=jnp.float32,
    )
    return picked.reshape(picked_rows, HEADS * HEAD_DIM)


def spread_rows(sparse_rows, selector, dilation):
    shaped = sparse_rows.reshape(sparse_rows.shape[0], 1, HEADS, HEAD_DIM)
    placed = shaped * selector[None, :, :, None]
    return placed.reshape(sparse_rows.shape[0] * dilation, HEADS * HEAD_DIM)


def select_heads(dense_heads, selector, dilation):
    shaped = dense_heads.reshape(dense_heads.shape[0] // dilation, dilation, HEADS)
    return jnp.sum(shaped * selector[None], axis=1)


def spread_heads(sparse_heads, selector, dilation):
    placed = jnp.where(selector[None] > 0, sparse_heads[:, None, :], MASKED)
    return placed.reshape(sparse_heads.shape[0] * dilation, HEADS)


def head_major(values):
    return values.reshape(values.shape[0], HEADS, HEAD_DIM).transpose(1, 0, 2)


def row_major(values):
    return values.transpose(1, 0, 2).reshape(values.shape[1], HEADS * HEAD_DIM)


def key_mask(row_count, block_count, own_block):
    query_pos = jnp.arange(row_count)[:, None]
    position = jnp.arange(row_count * block_count)[None, :]
    key_block = position // row_count
    within = position % row_count
    return (key_block < own_block) | (key_block == own_block) & (within <= query_pos)


def masked_scores(head_query, head_keys, allowed):
    return jnp.where(allowed, product_nt(head_query, head_keys) * SCORE_SCALE, MASKED)


def pattern_lse(queries, keys, allowed):

    def one_head(operands):
        scores = masked_scores(operands[0], operands[1], allowed)
        peak_rows = jnp.max(scores, axis=1, keepdims=True)
        return peak_rows[:, 0] + jnp.log(jnp.sum(jnp.exp(scores - peak_rows), axis=1))

    return lax.map(one_head, (head_major(queries), head_major(keys))).T


def pattern_out(queries, keys, values, allowed, totals):

    def one_head(operands):
        head_query, head_keys, head_values, head_total = operands
        scores = masked_scores(head_query, head_keys, allowed)
        probability = jnp.where(allowed, jnp.exp(scores - head_total[:, None]), 0.0).astype(
            jnp.bfloat16
        )
        return product(probability, head_values)

    return row_major(
        lax.map(one_head, (head_major(queries), head_major(keys), head_major(values), totals.T))
    )


def pattern_back(queries, keys, values, allowed, totals, deltas, grad_out):

    def one_head(operands):
        head_query, head_keys, head_values, head_total, head_delta, head_grad = operands
        scores = masked_scores(head_query, head_keys, allowed)
        probability = jnp.where(allowed, jnp.exp(scores - head_total[:, None]), 0.0)
        grad_probs = product_nt(head_grad, head_values)
        grad_scores = (probability * (grad_probs - head_delta[:, None])).astype(jnp.bfloat16)
        grad_query = product(grad_scores, head_keys) * SCORE_SCALE
        grad_keys = product_tn(grad_scores, head_query) * SCORE_SCALE
        grad_values = product_tn(probability.astype(jnp.bfloat16), head_grad)
        return (grad_query, grad_keys, grad_values)

    results = lax.map(
        one_head,
        (
            head_major(queries),
            head_major(keys),
            head_major(values),
            totals.T,
            deltas.T,
            head_major(grad_out),
        ),
    )
    return (row_major(results[0]), row_major(results[1]), row_major(results[2]))


def body(
    tokens,
    cotangent,
    w_qkv,
    w_attn,
    w_in,
    w_out,
    gains_model,
    biases_model,
    gain_ffn,
    biases_ffn,
    offsets,
):
    gathered = (
        lax.all_gather(w_qkv, ("wide", "narrow"), axis=0, tiled=True),
        lax.all_gather(w_attn, ("wide", "narrow"), axis=0, tiled=True),
        lax.all_gather(w_in, ("wide", "narrow"), axis=0, tiled=True),
        lax.all_gather(w_out, ("wide", "narrow"), axis=0, tiled=True),
        lax.all_gather(gains_model, ("wide", "narrow"), axis=1, tiled=True),
        lax.all_gather(biases_model, ("wide", "narrow"), axis=1, tiled=True),
        lax.all_gather(gain_ffn, ("wide", "narrow"), axis=0, tiled=True),
        lax.all_gather(biases_ffn, ("wide", "narrow"), axis=1, tiled=True),
    )
    qkv_full, attn_full, in_full, out_full = (gathered[0], gathered[1], gathered[2], gathered[3])
    model_gains = gathered[4].astype(jnp.float32)
    model_biases = gathered[5].astype(jnp.float32)
    ffn_gain = gathered[6].astype(jnp.float32)
    ffn_biases = gathered[7].astype(jnp.float32)
    local_rows = tokens.shape[0]
    width = tokens.shape[1]
    inputs = tokens.astype(jnp.float32)
    normed_one, pull_one = jax.vjp(layer_norm, inputs, model_gains[0], model_biases[0])
    normed_low = normed_one.astype(jnp.bfloat16)
    projected = product(normed_low, qkv_full)
    queries = (projected[:, :width] + model_biases[1]).astype(jnp.bfloat16)
    keys = projected[:, width : 2 * width].astype(jnp.bfloat16)
    values = (projected[:, 2 * width :] + model_biases[2]).astype(jnp.bfloat16)
    size_narrow = lax.axis_size("narrow")
    narrow_place = lax.axis_index("narrow")
    dilations = (RATE0, RATE1, RATE2)
    selectors = (one_hot(offsets[0], RATE0), one_hot(offsets[1], RATE1), one_hot(offsets[2], RATE2))
    picked_q = [
        select_rows(queries, selectors[pattern], dilations[pattern]).astype(jnp.bfloat16)
        for pattern in range(3)
    ]
    picked_k = [
        select_rows(keys, selectors[pattern], dilations[pattern]).astype(jnp.bfloat16)
        for pattern in range(3)
    ]
    picked_v = [
        select_rows(values, selectors[pattern], dilations[pattern]).astype(jnp.bfloat16)
        for pattern in range(3)
    ]
    arrived = (
        lax.all_gather(picked_k[0], "narrow", axis=0, tiled=True),
        lax.all_gather(picked_v[0], "narrow", axis=0, tiled=True),
        lax.all_gather(picked_k[1], "narrow", axis=0, tiled=True),
        lax.all_gather(picked_v[1], "narrow", axis=0, tiled=True),
        lax.all_gather(picked_k[2], "narrow", axis=0, tiled=True),
        lax.all_gather(picked_v[2], "narrow", axis=0, tiled=True),
    )
    key_sets = (arrived[0], arrived[2], arrived[4])
    value_sets = (arrived[1], arrived[3], arrived[5])
    allowed_sets = tuple(
        (
            key_mask(local_rows // dilations[pattern], size_narrow, narrow_place)
            for pattern in range(3)
        )
    )
    partial_value = jnp.stack(
        [
            spread_heads(
                pattern_lse(picked_q[pattern], key_sets[pattern], allowed_sets[pattern]),
                selectors[pattern],
                dilations[pattern],
            )
            for pattern in range(3)
        ]
    )
    peak_rows = jnp.max(partial_value, axis=0)
    totals = peak_rows + jnp.log(jnp.sum(jnp.exp(partial_value - peak_rows), axis=0))
    attended = jnp.zeros((local_rows, width), jnp.float32)
    for pattern in range(3):
        pattern_totals = select_heads(totals, selectors[pattern], dilations[pattern])
        result_rows = pattern_out(
            picked_q[pattern],
            key_sets[pattern],
            value_sets[pattern],
            allowed_sets[pattern],
            pattern_totals,
        )
        attended = attended + spread_rows(result_rows, selectors[pattern], dilations[pattern])
    sub_normed, pull_sub = jax.vjp(layer_norm, attended, model_gains[1], model_biases[3])
    sub_low = sub_normed.astype(jnp.bfloat16)
    middle = inputs + product(sub_low, attn_full) + model_biases[4]
    normed_two, pull_two = jax.vjp(layer_norm, middle, model_gains[2], model_biases[5])
    normed_two_low = normed_two.astype(jnp.bfloat16)
    pre_act = product(normed_two_low, in_full) + ffn_biases[0]
    activated, pull_gelu = jax.vjp(gelu_exact, pre_act)
    ffn_normed, pull_ffn = jax.vjp(layer_norm, activated, ffn_gain, ffn_biases[1])
    ffn_low = ffn_normed.astype(jnp.bfloat16)
    outputs = (middle + product(ffn_low, out_full) + model_biases[6]).astype(jnp.bfloat16)
    regathered = (
        lax.all_gather(w_qkv, ("wide", "narrow"), axis=0, tiled=True),
        lax.all_gather(w_attn, ("wide", "narrow"), axis=0, tiled=True),
        lax.all_gather(w_in, ("wide", "narrow"), axis=0, tiled=True),
        lax.all_gather(w_out, ("wide", "narrow"), axis=0, tiled=True),
    )
    qkv_back, attn_back, in_back, out_back = (
        regathered[0],
        regathered[1],
        regathered[2],
        regathered[3],
    )
    grad_out_f = cotangent.astype(jnp.float32)
    grad_w_out = product_tn(ffn_low, cotangent)
    grad_bias_ffo = jnp.sum(cotangent.astype(jnp.float32), axis=0)
    grad_act, grad_gain_ffn, grad_bias_ffn_norm = pull_ffn(product_nt(cotangent, out_back))
    grad_pre = pull_gelu(grad_act)[0].astype(jnp.bfloat16)
    grad_w_in = product_tn(normed_two_low, grad_pre)
    grad_bias_pre = jnp.sum(grad_pre.astype(jnp.float32), axis=0)
    grad_mid_norm, grad_gain_two, grad_bias_two = pull_two(product_nt(grad_pre, in_back))
    grad_middle = grad_out_f + grad_mid_norm
    grad_branch = grad_middle.astype(jnp.bfloat16)
    grad_w_attn = product_tn(sub_low, grad_branch)
    grad_bias_branch = jnp.sum(grad_branch.astype(jnp.float32), axis=0)
    grad_att, grad_gain_sub, grad_bias_sub = pull_sub(product_nt(grad_branch, attn_back))
    grad_att_low = grad_att.astype(jnp.bfloat16)
    deltas = jnp.sum(
        (grad_att_low.astype(jnp.float32) * attended).reshape(local_rows, HEADS, HEAD_DIM), axis=2
    )
    backward_parts = []
    for pattern in range(3):
        backward_parts.append(
            pattern_back(
                picked_q[pattern],
                key_sets[pattern],
                value_sets[pattern],
                allowed_sets[pattern],
                select_heads(totals, selectors[pattern], dilations[pattern]),
                select_heads(deltas, selectors[pattern], dilations[pattern]),
                select_rows(grad_att_low, selectors[pattern], dilations[pattern]).astype(
                    jnp.bfloat16
                ),
            )
        )
    returned = (
        lax.psum_scatter(
            backward_parts[0][1].astype(jnp.bfloat16), "narrow", scatter_dimension=0, tiled=True
        ).astype(jnp.float32),
        lax.psum_scatter(
            backward_parts[0][2].astype(jnp.bfloat16), "narrow", scatter_dimension=0, tiled=True
        ).astype(jnp.float32),
        lax.psum_scatter(
            backward_parts[1][1].astype(jnp.bfloat16), "narrow", scatter_dimension=0, tiled=True
        ).astype(jnp.float32),
        lax.psum_scatter(
            backward_parts[1][2].astype(jnp.bfloat16), "narrow", scatter_dimension=0, tiled=True
        ).astype(jnp.float32),
        lax.psum_scatter(
            backward_parts[2][1].astype(jnp.bfloat16), "narrow", scatter_dimension=0, tiled=True
        ).astype(jnp.float32),
        lax.psum_scatter(
            backward_parts[2][2].astype(jnp.bfloat16), "narrow", scatter_dimension=0, tiled=True
        ).astype(jnp.float32),
    )
    key_grads = (returned[0], returned[2], returned[4])
    value_grads = (returned[1], returned[3], returned[5])
    grad_q = jnp.zeros((local_rows, width), jnp.float32)
    grad_k = jnp.zeros((local_rows, width), jnp.float32)
    grad_v = jnp.zeros((local_rows, width), jnp.float32)
    for pattern in range(3):
        grad_q = grad_q + spread_rows(
            backward_parts[pattern][0], selectors[pattern], dilations[pattern]
        )
        grad_k = grad_k + spread_rows(key_grads[pattern], selectors[pattern], dilations[pattern])
        grad_v = grad_v + spread_rows(value_grads[pattern], selectors[pattern], dilations[pattern])
    grad_q_low = grad_q.astype(jnp.bfloat16)
    grad_v_low = grad_v.astype(jnp.bfloat16)
    grad_qkv = jnp.concatenate([grad_q_low, grad_k.astype(jnp.bfloat16), grad_v_low], axis=1)
    grad_w_qkv = product_tn(normed_low, grad_qkv)
    grad_bias_q = jnp.sum(grad_q_low.astype(jnp.float32), axis=0)
    grad_bias_v = jnp.sum(grad_v_low.astype(jnp.float32), axis=0)
    grad_first, grad_gain_one, grad_bias_one = pull_one(product_nt(grad_qkv, qkv_back))
    grad_inputs = grad_middle + grad_first
    grad_gains = jnp.stack([grad_gain_one, grad_gain_sub, grad_gain_two])
    grad_biases = jnp.stack(
        [
            grad_bias_one,
            grad_bias_q,
            grad_bias_v,
            grad_bias_sub,
            grad_bias_branch,
            grad_bias_two,
            grad_bias_ffo,
        ]
    )
    grad_ffn_biases = jnp.stack([grad_bias_pre, grad_bias_ffn_norm])
    reduced = (
        lax.psum_scatter(grad_w_qkv, ("wide", "narrow"), scatter_dimension=0, tiled=True),
        lax.psum_scatter(grad_w_attn, ("wide", "narrow"), scatter_dimension=0, tiled=True),
        lax.psum_scatter(grad_w_in, ("wide", "narrow"), scatter_dimension=0, tiled=True),
        lax.psum_scatter(grad_w_out, ("wide", "narrow"), scatter_dimension=0, tiled=True),
        lax.psum_scatter(grad_gains, ("wide", "narrow"), scatter_dimension=1, tiled=True),
        lax.psum_scatter(grad_biases, ("wide", "narrow"), scatter_dimension=1, tiled=True),
        lax.psum_scatter(grad_gain_ffn, ("wide", "narrow"), scatter_dimension=0, tiled=True),
        lax.psum_scatter(grad_ffn_biases, ("wide", "narrow"), scatter_dimension=1, tiled=True),
    )
    return (
        outputs,
        grad_inputs,
        reduced[0],
        reduced[1],
        reduced[2],
        reduced[3],
        reduced[4],
        reduced[5],
        reduced[6],
        reduced[7],
    )


BF16 = jnp.bfloat16
F32 = jnp.float32
ALPHA = (
    -2.72614225801306e-10,
    2.77068142495902e-08,
    -2.10102402082508e-06,
    -5.69250639462346e-05,
    -7.34990630326855e-04,
    -2.95459980854025e-03,
    -1.60960333262415e-02,
)
BETA = (
    -1.45660718464996e-05,
    -2.13374055278905e-04,
    -1.68282697438203e-03,
    -7.37332916720468e-03,
    -1.42647390514189e-02,
)


def nn(a, b):
    return lax.dot_general(a, b, (((1,), (0,)), ((), ())), preferred_element_type=F32)


def nt(a, b):
    return lax.dot_general(a, b, (((1,), (1,)), ((), ())), preferred_element_type=F32)


def tn(a, b):
    return lax.dot_general(a, b, (((0,), (0,)), ((), ())), preferred_element_type=F32)


def erf(v):
    v = jnp.clip(v, -4.0, 4.0)
    s = v * v
    top = jnp.full_like(s, ALPHA[0])
    for term in ALPHA[1:]:
        top = top * s + term
    low = jnp.full_like(s, BETA[0])
    for term in BETA[1:]:
        low = low * s + term
    return v * top / low


def normed(v):
    centred = v - jnp.mean(v, axis=-1, keepdims=True)
    rate = lax.rsqrt(jnp.mean(centred * centred, axis=-1, keepdims=True) + EPSILON)
    return centred * rate, rate


def norm_back(e, n, rate, gain):
    t = e * gain
    return rate * (
        t - jnp.mean(t, axis=-1, keepdims=True) - n * jnp.mean(t * n, axis=-1, keepdims=True)
    )


def colsum(v):
    return jnp.sum(v, axis=0, keepdims=True)


def lanes(shape):
    return lax.broadcasted_iota(jnp.int32, shape, len(shape) - 1)


def sublanes(shape):
    return lax.broadcasted_iota(jnp.int32, shape, len(shape) - 2)


def rows_of(parts, count):
    shape = (count, next(part for part in parts if part is not None).shape[1])
    at = sublanes(shape)
    out = jnp.zeros(shape, F32)
    for i, part in enumerate(parts):
        if part is not None:
            out = jnp.where(at == i, part, out)
    return out


def to_rows(columns):
    shape = (columns[0].shape[0], 128)
    at = lanes(shape)
    out = jnp.zeros(shape, F32)
    for i, column in enumerate(columns):
        out = jnp.where(at == i, column, out)
    return out.T[0:8]


def to_columns(rows):
    wide = rows_of(rows, 128).T
    return [wide[:, i : i + 1] for i in range(len(rows))]


def left(v, amount, width):
    return pltpu.roll(v, lax.rem(width - amount, width), 1)


def call(kernel, outs, *operands, scratch=()):
    specs = [
        pl.BlockSpec(memory_space=pltpu.SMEM if a.dtype == jnp.int32 else pltpu.VMEM)
        for a in operands
    ]
    return pl.pallas_call(
        kernel,
        out_shape=[jax.ShapeDtypeStruct(s, d) for s, d in outs],
        in_specs=specs,
        out_specs=[pl.BlockSpec(memory_space=pltpu.VMEM) for _ in outs],
        scratch_shapes=[pltpu.VMEM(s, d) for s, d in scratch],
        compiler_params=pltpu.CompilerParams(vmem_limit_bytes=56 << 20),
        name=kernel.__name__,
    )(*operands)


def prep_kernel(
    idx, wqkv, win, wattn, gains, biases, gffn, bffn,
    q0, q1, q2, q3, i0, i1, i2, i3, small, qs, is_,
):
    n = idx[1]
    small[...] = jnp.zeros_like(small)
    small[0:3, 0:24] = gains[...].astype(F32)
    small[3:10, 0:24] = biases[...].astype(F32)
    ffn_g = gffn[...].astype(F32)
    ffn_b = bffn[...].astype(F32)
    for k in range(4):
        small[16 + 8 * k : 17 + 8 * k, 0:24] = ffn_g[:, k * 24 : k * 24 + 24]
        small[17 + 8 * k : 19 + 8 * k, 0:24] = ffn_b[:, k * 24 : k * 24 + 24]
    eye = (sublanes((24, 128)) == lanes((24, 128))).astype(BF16)
    params = nt(eye, small[...].astype(BF16))
    weights = wqkv[...].astype(F32)
    for m in range(4):
        for part in range(3):
            at = part * 768 + m * 192
            qs[m, :, part * 192 : part * 192 + 192] = weights[:, at : at + 192]
        qs[m, :, 576:640] = params
    inner = win[...].astype(F32)
    for m in range(4):
        for w in range(8):
            at = (w * 4 + m) * 96
            is_[m, :, w * 96 : w * 96 + 96] = inner[:, at : at + 96]
    for k, out in enumerate((q0, q1, q2, q3)):
        out[...] = qs[n ^ k].astype(BF16)
    for k, out in enumerate((i0, i1, i2, i3)):
        if k % 2 == 0:
            out[0:24] = is_[n ^ k].astype(BF16)
            out[24:48] = wattn[...]
        else:
            out[...] = is_[n ^ k].astype(BF16)


def pack_q_kernel(idx, q0, q1, q2, q3, out, buf):
    n = idx[1]
    for k, q in enumerate((q0, q1, q2, q3)):
        buf[n ^ k] = q[...].astype(F32)
    out[...] = buf[...].reshape(96, 640).astype(BF16)


def pack_i_kernel(idx, i0, i1, i2, i3, out, buf, two):
    n = idx[1]
    for k, i in enumerate((i0, i1, i2, i3)):
        buf[n ^ k] = i[0:24].astype(F32)
        if k % 2 == 0:
            two[(n ^ k) // 2] = i[24:48].astype(F32)
    out[0:96] = buf[...].reshape(96, 768).astype(BF16)
    out[96:144] = two[...].reshape(48, 768).astype(BF16)


def pack_a_kernel(idx, r0, r1, r2, r3, r4, r5, r6, r7, out):
    w = idx[0]
    for j, r in enumerate((r0, r1, r2, r3, r4, r5, r6, r7)):
        out[w ^ j] = r[96:144]


def attend_kernel(
    idx, off, t0, t1, t2, t3, q0, q1, q2, q3, q4, q5, q6, q7,
    x_out, w_out, p_out, a_out, qkv_out, o_t_out, lse_out, o_out,
):
    w, n = idx[0], idx[1]
    for j, q in enumerate((q0, q1, q2, q3, q4, q5, q6, q7)):
        w_out[pl.ds(pl.multiple_of((w ^ j) * 96, 32), 96), :] = q[...]
    for k, t in enumerate((t0, t1, t2, t3)):
        x_out[pl.ds(pl.multiple_of((n ^ k) * 128, 128), 128), :] = t[...]
    pick = (sublanes((64, 128)) + 64 == lanes((64, 128))).astype(BF16)
    table = nt(pick, w_out[:, 512:640])
    model = table[0:16]
    ffn = jnp.zeros((8, 768), F32)
    inside = lax.rem(lanes((8, 768)), 96) // 24
    for k in range(4):
        turned = pltpu.roll(table[16 + 8 * k : 24 + 8 * k], lax.rem(768 + (k - n) * 24, 768), 1)
        ffn = jnp.where(inside == k, turned, ffn)
    p_out[0:16] = model
    p_out[16:24] = ffn
    n1, _ = normed(x_out[...].astype(F32))
    a1 = (n1 * model[0:1] + model[3:4]).astype(BF16)
    a_out[...] = a1
    qkv = nn(a1, w_out[...])
    lane = lanes((8, 768))
    bias_q = left(jnp.broadcast_to(model[4:5], (8, 768)), n * 192, 768)
    bias_v = pltpu.roll(
        jnp.broadcast_to(model[5:6], (8, 768)), lax.rem(768 + 384 - n * 192, 768), 1
    )
    bias = jnp.where(
        lane < 192, bias_q, jnp.where((lane >= 384) & (lane < 576), bias_v, 0.0)
    )[0:1, 0:640]
    qkv = jnp.where(lanes((1, 640)) < 576, qkv + bias, 0.0).astype(BF16)
    qkv_out[...] = qkv
    v_t = qkv[:, 384:576].astype(F32).T
    o_parts, lse_rows = [], []
    for h in range(3):
        head = n * 3 + h
        o1, o2 = off[1, head], off[2, head]
        at = lanes((1, 512))
        r1 = (lax.rem(at, 2) == o1).astype(F32)
        r2 = (lax.rem(at, 4) == o2).astype(F32)
        head_v = v_t[h * 64 : h * 64 + 64]
        ones = rows_of([jnp.ones((1, 512), F32), r1, r2], 8)
        left_side = jnp.concatenate([head_v, head_v * r1, head_v * r2, ones], axis=0).astype(BF16)
        head_q = qkv[:, h * 64 : h * 64 + 64] * jnp.asarray(SCORE_SCALE, BF16)
        head_k = qkv[:, 192 + h * 64 : 256 + h * 64]
        blocks, lses = [], []
        for i in range(2):
            keys = 256 * (i + 1)
            scores = nt(head_k[0:keys], head_q[i * 256 : i * 256 + 256])
            shape = (keys, 256)
            scores = jnp.where(sublanes(shape) <= lanes(shape) + i * 256, scores, MASKED)
            peak = jnp.max(scores, axis=0, keepdims=True)
            weight = jnp.exp(scores - peak).astype(BF16)
            both = nn(left_side[:, 0:keys], weight)
            s1, s2 = r1[:, i * 256 : i * 256 + 256], r2[:, i * 256 : i * 256 + 256]
            total = both[192:193] + s1 * both[193:194] + s2 * both[194:195]
            blocks.append((both[0:64] + s1 * both[64:128] + s2 * both[128:192]) / total)
            lses.append(peak + jnp.log(total))
        o_parts.append(jnp.concatenate(blocks, axis=1))
        lse_rows.append(jnp.concatenate(lses, axis=1))
    o_t = jnp.concatenate(o_parts, axis=0)
    o_t_out[...] = o_t
    lse_out[...] = rows_of(lse_rows, 8)
    o_out[...] = o_t.T.astype(BF16)


def middle_kernel(
    idx, x, p, o0, o1, o2, o3, a0, a1, g0, g1, g2, g3,
    i0, i1, i2, i3, i4, i5, i6, i7, c0, c1, c2, c3, c4, c5, c6, c7,
    o_out, u_out, x2_out, h2_out, f_out, dg_out, e_out, gy_out, win_out, wout_out, wattn_out,
    stat_out, o_buf, a_buf,
):
    w, n = idx[0], idx[1]
    core = lax.rem(n, 2)
    for j, i in enumerate((i0, i1, i2, i3, i4, i5, i6, i7)):
        win_out[pl.ds(pl.multiple_of((w ^ j) * 96, 32), 96), :] = i[0:96]
    for j, c in enumerate((c0, c1, c2, c3, c4, c5, c6, c7)):
        wout_out[pl.ds(pl.multiple_of((w ^ j) * 96, 32), 96), :] = c[...]
    for k, g in enumerate((g0, g1, g2, g3)):
        gy_out[pl.ds(pl.multiple_of((n ^ k) * 128, 128), 128), :] = g[...]
    for k, o in enumerate((o0, o1, o2, o3)):
        o_buf[n ^ k] = o[...].astype(F32)
    for side, a in ((core, a0), (1 - core, a1)):
        for w_ in range(8):
            for x_ in range(2):
                a_buf[w_, x_ * 2 + side] = a[w_, x_ * 24 : x_ * 24 + 24].astype(F32)
    wattn_out[...] = a_buf[...].reshape(768, 768).astype(BF16)
    o = jnp.concatenate([o_buf[m] for m in range(4)], axis=1)
    o_out[...] = o
    n_o, _ = normed(o)
    u = (n_o * p[1:2] + p[6:7]).astype(BF16)
    u_out[...] = u
    x2 = x[...].astype(F32) + nn(u, wattn_out[...]) + p[7:8]
    x2_out[...] = x2
    n2, _ = normed(x2)
    h2 = (n2 * p[2:3] + p[8:9]).astype(BF16)
    h2_out[...] = h2
    c = nn(h2, win_out[...]) + p[17:18]
    half = 0.5 + 0.5 * erf(c * 0.7071067811865476)
    f = c * half
    f_out[...] = f
    dg_out[...] = half + c * jnp.exp(c * c * -0.5) * 0.3989422804014327
    e = nt(gy_out[...], wout_out[...])
    e_out[...] = e
    t = e * p[16:17]
    mean = jnp.mean(f, axis=1, keepdims=True)
    centred = f - mean
    stat_out[...] = to_rows(
        [
            mean,
            jnp.sum(centred * centred, axis=1, keepdims=True),
            jnp.sum(t, axis=1, keepdims=True),
            jnp.sum(t * centred, axis=1, keepdims=True),
        ]
    )


def ffn_columns(s0, s1, s2, s3):
    parts = [s[...] for s in (s0, s1, s2, s3)]
    count = 768.0 * 4
    mean = sum(s[0:1] for s in parts) * 0.25
    spread = sum(s[1:2] + 768.0 * (s[0:1] - mean) * (s[0:1] - mean) for s in parts) / count
    rate = lax.rsqrt(spread + EPSILON)
    mean_t = sum(s[2:3] for s in parts) / count
    mean_tn = rate * sum(s[3:4] + (s[0:1] - mean) * s[2:3] for s in parts) / count
    return to_columns([mean, rate, mean_t, mean_tn])


def core_halves(value, keep, send, core, buf):
    buf[...] = value
    for x_ in range(2):
        mine = pl.ds(pl.multiple_of((x_ * 2 + core) * 128, 128), 128)
        other = pl.ds(pl.multiple_of((x_ * 2 + 1 - core) * 128, 128), 128)
        keep[x_ * 128 : x_ * 128 + 128, :] = buf[mine, :].astype(keep.dtype)
        send[x_ * 128 : x_ * 128 + 128, :] = buf[other, :].astype(send.dtype)


def ffn_back_kernel(idx, p, s0, s1, s2, s3, f, dg, e, win, gc_out, keep, send, buf):
    core = lax.rem(idx[1], 2)
    mean, rate, mean_t, mean_tn = ffn_columns(s0, s1, s2, s3)
    n_f = (f[...] - mean) * rate
    df = rate * (e[...] * p[16:17] - mean_t - n_f * mean_tn)
    gc = (df * dg[...]).astype(BF16)
    gc_out[...] = gc
    core_halves(nt(gc, win[...]), keep, send, core, buf)


def ffn_grad_kernel(
    idx, p, s0, s1, s2, s3, f, e, gc, gy, h2, wout,
    keep, send, op_keep, op_send, gin_out, sums, buf, prod,
):
    w, core = idx[0], lax.rem(idx[1], 2)
    mean, rate, _, _ = ffn_columns(s0, s1, s2, s3)
    n_f = (f[...] - mean) * rate
    z = (n_f * p[16:17] + p[18:19]).astype(BF16)
    prod[...] = tn(z, gy[...])
    for i in range(4):
        keep[i] = prod[pl.ds(pl.multiple_of((w ^ (2 * i)) * 96, 32), 96), :].astype(BF16)
        send[i] = prod[pl.ds(pl.multiple_of((w ^ (2 * i + 1)) * 96, 32), 96), :].astype(BF16)
    core_halves(nn(z, wout[...]), op_keep, op_send, core, buf)
    gin_out[...] = tn(h2[...], gc[...]).astype(BF16)
    sums[...] = rows_of(
        [
            colsum(e[...] * n_f),
            colsum(gc[...].astype(F32)),
            colsum(e[...]),
            colsum(gy[...].astype(F32)),
        ],
        8,
    )


def add_kernel(keep, got, out):
    out[...] = (keep[...].astype(F32) + got[...].astype(F32)).astype(out.dtype)


def add_four_kernel(keep, got, s0, s1, s2, s3):
    for i, out in enumerate((s0, s1, s2, s3)):
        out[...] = (keep[i].astype(F32) + got[i].astype(F32)).astype(out.dtype)


def attn_back_kernel(
    idx, p, own, own_x, sib, sib_x, x2, gy, u, o, wattn, gin, sums,
    dx2_out, do_out, keep, send, dh, prod, gat,
):
    w, n = idx[0], idx[1]
    core = lax.rem(n, 2)
    for x_ in range(2):
        at = slice(x_ * 128, x_ * 128 + 128)
        mine = pl.ds(pl.multiple_of((x_ * 2 + core) * 128, 128), 128)
        other = pl.ds(pl.multiple_of((x_ * 2 + 1 - core) * 128, 128), 128)
        dh[mine, :] = own[at].astype(F32) + own_x[at].astype(F32)
        dh[other, :] = sib[at].astype(F32) + sib_x[at].astype(F32)
    e2 = dh[...]
    n2, rate2 = normed(x2[...])
    dx2 = gy[...].astype(F32) + norm_back(e2, n2, rate2, p[2:3])
    dx2_out[...] = dx2
    ga = dx2.astype(BF16)
    eo = nt(ga, wattn[...])
    n_o, rate_o = normed(o[...])
    d_o = norm_back(eo, n_o, rate_o, p[1:2])
    for m in range(4):
        @pl.when(n == m)
        def _():
            do_out[...] = d_o[:, m * 192 : m * 192 + 192].astype(BF16)
    model = rows_of(
        [
            None,
            colsum(eo * n_o),
            colsum(e2 * n2),
            None,
            None,
            None,
            colsum(eo),
            colsum(ga.astype(F32)),
            colsum(e2),
            sums[3:4],
        ],
        16,
    )
    gat[...] = tn(u[...], ga).reshape(8, 4, 24, 768)
    for i in range(8):
        to = w ^ i
        block = (keep if i % 2 == 0 else send).at[i // 2]
        block[0:96] = gin[pl.ds(pl.multiple_of(to * 96, 32), 96), :]
        mine = left(model, to * 96 + n * 24, 768)
        ffn = left(sums[...], to * 96, 768)
        extra = jnp.concatenate(
            [mine[0:8, 0:128], mine[8:16, 0:128], ffn[:, 0:128], jnp.zeros((8, 384), F32)], axis=1
        )
        block[96:128] = jnp.concatenate([gat[to, n], extra], axis=0).astype(BF16)


def head_back_kernel(
    idx, off, p, qkv, o_t, lse, do, a1, wqkv, x,
    keep, send, d_keep, d_send, buf, prod,
):
    w, n = idx[0], idx[1]
    core = lax.rem(n, 2)
    do_t = do[...].astype(F32).T
    k_t = qkv[:, 192:384].astype(F32).T
    row = lanes((1, 512))
    column = sublanes((512, 1))
    dq_parts, dk_parts, dv_parts = [], [], []
    for h in range(3):
        head = n * 3 + h
        o1, o2 = off[1, head], off[2, head]
        r1 = (lax.rem(row, 2) == o1).astype(F32)
        r2 = (lax.rem(row, 4) == o2).astype(F32)
        c1 = (lax.rem(column, 2) == o1).astype(F32)
        c2 = (lax.rem(column, 4) == o2).astype(F32)
        span = slice(h * 64, h * 64 + 64)
        delta = colsum(do_t[span] * o_t[span, :])
        total = lse[h : h + 1, :]
        head_q = qkv[:, h * 64 : h * 64 + 64].astype(F32) * SCORE_SCALE
        head_k = qkv[:, 192 + h * 64 : 256 + h * 64]
        head_v = qkv[:, 384 + h * 64 : 448 + h * 64]
        head_do = do[:, h * 64 : h * 64 + 64]
        do_f = head_do.astype(F32)
        low_q = head_q.astype(BF16)
        q_all = jnp.concatenate([head_q, head_q * c1, head_q * c2], axis=1).astype(BF16)
        do_all = jnp.concatenate([do_f, do_f * c1, do_f * c2], axis=1).astype(BF16)
        kt = k_t[span]
        k_all = jnp.concatenate([kt, kt * r1, kt * r2], axis=0).astype(BF16)
        dk = jnp.zeros((512, 192), F32)
        dv = jnp.zeros((512, 192), F32)
        dq_blocks = []
        for i in range(2):
            keys = 256 * (i + 1)
            here = slice(i * 256, i * 256 + 256)
            shape = (keys, 256)
            scores = nt(head_k[0:keys], low_q[here])
            prob = jnp.where(
                sublanes(shape) <= lanes(shape) + i * 256, jnp.exp(scores - total[:, here]), 0.0
            )
            grad_p = nt(head_v[0:keys], head_do[here])
            grad_s = (prob * (grad_p - delta[:, here])).astype(BF16)
            dv_i = nn(prob.astype(BF16), do_all[here])
            dk_i = nn(grad_s, q_all[here])
            if keys < 512:
                zero = jnp.zeros((512 - keys, 192), F32)
                dv_i = jnp.concatenate([dv_i, zero], axis=0)
                dk_i = jnp.concatenate([dk_i, zero], axis=0)
            dv = dv + dv_i
            dk = dk + dk_i
            dq_i = nn(k_all[:, 0:keys], grad_s)
            dq_blocks.append(dq_i[0:64] + r1[:, here] * dq_i[64:128] + r2[:, here] * dq_i[128:192])
        dq_parts.append(jnp.concatenate(dq_blocks, axis=1) * SCORE_SCALE)
        dk_parts.append(dk[:, 0:64] + c1 * dk[:, 64:128] + c2 * dk[:, 128:192])
        dv_parts.append(dv[:, 0:64] + c1 * dv[:, 64:128] + c2 * dv[:, 128:192])
    dq = jnp.concatenate(dq_parts, axis=0).T
    g = jnp.concatenate([dq] + dk_parts + dv_parts + [jnp.zeros((512, 64), F32)], axis=1)
    g = g.astype(BF16)
    prod[...] = tn(a1[...], g)
    grad = nt(g, wqkv[...])
    n1, _ = normed(x[...].astype(F32))
    outer = rows_of([None, colsum(grad * n1), colsum(grad)], 8)
    g_sum = colsum(g.astype(F32))
    for i in range(8):
        to = w ^ i
        block = (keep if i % 2 == 0 else send).at[i // 2]
        turned = left(outer, to * 96, 768)[:, 0:640]
        extra = jnp.where(sublanes((8, 640)) == 0, g_sum, turned)
        mine = prod[pl.ds(pl.multiple_of(to * 96, 32), 96), :]
        block[...] = jnp.concatenate([mine, extra], axis=0).astype(BF16)
    core_halves(grad, d_keep, d_send, core, buf)


def tail_add_kernel(idx, ok, og, dk, dg, keep, send, buf):
    x_ = idx[1] // 2
    buf[:, 0:768] = ok[...].astype(F32) + og[...].astype(F32)
    buf[:, 768:1536] = dk[...].astype(F32) + dg[...].astype(F32)
    keep[...] = buf[pl.ds(pl.multiple_of(x_ * 128, 128), 128), :]
    send[...] = buf[pl.ds(pl.multiple_of((1 - x_) * 128, 128), 128), :].astype(BF16)


def token_kernel(idx, p, keep, got, tok, x2, dx2, out, grad):
    mine = pl.ds(pl.multiple_of(idx[1] * 128, 128), 128)
    both = keep[...] + got[...].astype(F32)
    out[...] = (x2[mine, :] + both[:, 0:768] + p[9:10]).astype(BF16)
    n1, rate = normed(tok[...].astype(F32))
    grad[...] = dx2[mine, :] + norm_back(both[:, 768:1536], n1, rate, p[0:1])


def sum_in_kernel(idx, s0, s1, s2, s3, own, t1, t2, t3, attn, extra, buf):
    n = idx[1]
    total = s0[...].astype(F32) + s1[...].astype(F32) + s2[...].astype(F32) + s3[...].astype(F32)
    buf[...] = total[0:96].reshape(4, 24, 768)
    own[...] = buf[n]
    for k, out in enumerate((t1, t2, t3)):
        out[...] = buf[n ^ (k + 1)].astype(BF16)
    attn[...] = total[96:120]
    extra[...] = total[120:128]


def sum_qkv_kernel(idx, s0, s1, s2, s3, own, t1, t2, t3, buf):
    n = idx[1]
    total = s0[...].astype(F32) + s1[...].astype(F32) + s2[...].astype(F32) + s3[...].astype(F32)
    buf[...] = total[0:96].reshape(4, 24, 640)
    own[0:24] = buf[n]
    own[24:32] = total[96:104]
    for k, out in enumerate((t1, t2, t3)):
        out[...] = jnp.concatenate([buf[n ^ (k + 1)], total[96:104]], axis=0).astype(BF16)


def final_in_kernel(idx, i0, i1, i2, i3, out, buf):
    n = idx[1]
    for k, i in enumerate((i0, i1, i2, i3)):
        buf[n ^ k] = i[...].astype(F32)
    for m in range(4):
        block = buf[m]
        for w in range(8):
            at = (w * 4 + m) * 96
            out[:, at : at + 96] = block[:, w * 96 : w * 96 + 96]


def final_kernel(idx, q0, q1, q2, q3, extra, gq, gains, biases, gffn, bffn, buf):
    w, n = idx[0], idx[1]
    for k, q in enumerate((q0, q1, q2, q3)):
        buf[n ^ k] = q[...].astype(F32)
    for m in range(4):
        block = buf[m]
        for part in range(3):
            at = part * 768 + m * 192
            gq[:, at : at + 192] = block[0:24, part * 192 : part * 192 + 192]
    tails = [buf[m][24:32] for m in range(4)]
    q_row = jnp.concatenate([t[:, 0:192] for t in tails], axis=1)
    v_row = jnp.concatenate([t[:, 384:576] for t in tails], axis=1)
    place = (w * 4 + n) * 24
    q_row = left(q_row, place, 768)[0:1, 0:24]
    v_row = left(v_row, place, 768)[0:1, 0:24]
    norm = left((tails[0] + tails[1] + tails[2] + tails[3])[:, 0:128], n * 24, 128)[:, 0:24]
    low, high, ffn = extra[:, 0:24], extra[:, 128:152], extra[:, 256:352]
    gains[0:1] = norm[1:2]
    gains[1:3] = low[1:3]
    biases[0:1] = norm[2:3]
    biases[1:2] = q_row
    biases[2:3] = v_row
    biases[3:5] = low[6:8]
    biases[5:7] = high[0:2]
    gffn[...] = ffn[0:1]
    bffn[...] = ffn[1:3]


def swap(values, axis, size, step):
    return lax.ppermute(values, axis, [(i, i ^ step) for i in range(size)])


def wide_gather(block):
    got = [block]
    z = {step: swap(block, "wide", 8, step) for step in (6, 4, 2)}
    y = swap(block, "wide", 8, 1)
    return (
        block, y, z[2], swap(z[2], "wide", 8, 1), z[4], swap(z[4], "wide", 8, 1),
        z[6], swap(z[6], "wide", 8, 1),
    )


def wide_scatter(keep, send):
    got = swap(send, "wide", 8, 1)
    shape = keep.shape[1:]
    parts = call(add_four_kernel, [(shape, BF16)] * 4, keep, got)
    return [parts[0]] + [swap(parts[i], "wide", 8, 2 * i) for i in (1, 2, 3)]


def fast_body(
    tokens, cotangent, w_qkv, w_attn, w_in, w_out, gains_model, biases_model, gain_ffn, biases_ffn,
    offsets,
):
    idx = jnp.stack([lax.axis_index("wide"), lax.axis_index("narrow")]).astype(jnp.int32)
    C = lambda v: swap(v, "narrow", 4, 1)
    X = lambda v: swap(v, "narrow", 4, 2)
    XC = lambda v: swap(v, "narrow", 4, 3)
    tx = X(tokens)
    prep = call(
        prep_kernel,
        [((24, 640), BF16)] * 4
        + [((48, 768), BF16), ((24, 768), BF16), ((48, 768), BF16), ((24, 768), BF16)],
        idx, w_qkv, w_in, w_attn, gains_model, biases_model, gain_ffn[None], biases_ffn,
        scratch=[((64, 128), F32), ((4, 24, 640), F32), ((4, 24, 768), F32)],
    )
    q_own = call(
        pack_q_kernel, [((96, 640), BF16)],
        idx, prep[0], C(prep[1]), X(prep[2]), XC(prep[3]), scratch=[((4, 24, 640), F32)],
    )[0]
    toks = (tokens, C(tokens), tx, C(tx))
    q_all = wide_gather(q_own)
    r_own = call(
        pack_i_kernel, [((144, 768), BF16)],
        idx, prep[4], C(prep[5]), X(prep[6]), XC(prep[7]),
        scratch=[((4, 24, 768), F32), ((2, 24, 768), F32)],
    )[0]
    gx = X(cotangent)
    cots = (cotangent, C(cotangent), gx, C(gx))
    x, wqkv, params, a1, qkv, o_t, lse, o_low = call(
        attend_kernel,
        [
            ((512, 768), BF16), ((768, 640), BF16), ((24, 768), F32), ((512, 768), BF16),
            ((512, 640), BF16), ((192, 512), F32), ((8, 512), F32), ((512, 192), BF16),
        ],
        idx, offsets, *toks, *q_all,
    )
    r_all = wide_gather(r_own)
    c_all = wide_gather(w_out)
    attn_own = call(pack_a_kernel, [((8, 48, 768), BF16)], idx, *r_all)[0]
    ox = X(o_low)
    o, u, x2, h2, f, dg, e, gy, win, wout, wattn, stats = call(
        middle_kernel,
        [
            ((512, 768), F32), ((512, 768), BF16), ((512, 768), F32), ((512, 768), BF16),
            ((512, 768), F32), ((512, 768), F32), ((512, 768), F32), ((512, 768), BF16),
            ((768, 768), BF16), ((768, 768), BF16), ((768, 768), BF16), ((8, 512), F32),
        ],
        idx, x, params, o_low, C(o_low), ox, C(ox), attn_own, C(attn_own), *cots, *r_all, *c_all,
        scratch=[((4, 512, 192), F32), ((8, 4, 24, 768), F32)],
    )
    stat_all = (stats, C(stats), X(stats), XC(stats))
    gc, d_keep, d_send = call(
        ffn_back_kernel, [((512, 768), BF16), ((256, 768), F32), ((256, 768), BF16)],
        idx, params, *stat_all, f, dg, e, win, scratch=[((512, 768), F32)],
    )
    d_half = call(add_kernel, [((256, 768), BF16)], d_keep, C(d_send))[0]
    d_x = X(d_half)
    out_keep, out_send, op_keep, op_send, gin, sums = call(
        ffn_grad_kernel,
        [
            ((4, 96, 768), BF16), ((4, 96, 768), BF16), ((256, 768), F32), ((256, 768), BF16),
            ((768, 768), BF16), ((8, 768), F32),
        ],
        idx, params, *stat_all, f, e, gc, gy, h2, wout,
        scratch=[((512, 768), F32), ((768, 768), F32)],
    )
    out_parts = wide_scatter(out_keep, out_send)
    dx2, do, in_keep, in_send = call(
        attn_back_kernel,
        [
            ((512, 768), F32), ((512, 192), BF16), ((4, 128, 768), BF16), ((4, 128, 768), BF16),
        ],
        idx, params, d_half, d_x, C(d_half), C(d_x), x2, gy, u, o, wattn, gin, sums,
        scratch=[((512, 768), F32), ((8, 128), F32), ((8, 4, 24, 768), F32)],
    )
    in_parts = wide_scatter(in_keep, in_send)
    qkv_keep, qkv_send, t_keep, t_send = call(
        head_back_kernel,
        [
            ((4, 104, 640), BF16), ((4, 104, 640), BF16), ((256, 768), F32), ((256, 768), BF16),
        ],
        idx, offsets, params, qkv, o_t, lse, do, a1, wqkv, x,
        scratch=[((512, 768), F32), ((768, 640), F32)],
    )
    qkv_parts = wide_scatter(qkv_keep, qkv_send)
    tail_keep, tail_send = call(
        tail_add_kernel, [((128, 1536), F32), ((128, 1536), BF16)],
        idx, op_keep, C(op_send), t_keep, C(t_send), scratch=[((256, 1536), F32)],
    )
    outputs, grad_inputs = call(
        token_kernel, [((128, 768), BF16), ((128, 768), F32)],
        idx, params, tail_keep, X(tail_send), tokens, x2, dx2,
    )
    grad_w_out = sum(part.astype(F32) for part in out_parts)
    i_own, i1, i2, i3, grad_w_attn, extra = call(
        sum_in_kernel,
        [((24, 768), F32)] + [((24, 768), BF16)] * 3 + [((24, 768), F32), ((8, 768), F32)],
        idx, *in_parts, scratch=[((4, 24, 768), F32)],
    )
    grad_w_in = call(
        final_in_kernel, [((24, 3072), F32)], idx, i_own, C(i1), X(i2), XC(i3),
        scratch=[((4, 24, 768), F32)],
    )[0]
    q_mine, q1, q2, q3 = call(
        sum_qkv_kernel, [((32, 640), F32)] + [((32, 640), BF16)] * 3, idx, *qkv_parts,
        scratch=[((4, 24, 640), F32)],
    )
    grad_w_qkv, grad_gains, grad_biases, grad_gain_ffn, grad_ffn_biases = call(
        final_kernel,
        [((24, 2304), F32), ((3, 24), F32), ((7, 24), F32), ((1, 96), F32), ((2, 96), F32)],
        idx, q_mine, C(q1), X(q2), XC(q3), extra, scratch=[((4, 32, 640), F32)],
    )
    return (
        outputs, grad_inputs, grad_w_qkv, grad_w_attn, grad_w_in, grad_w_out, grad_gains,
        grad_biases, grad_gain_ffn[0], grad_ffn_biases,
    )


def solution(mesh):
    fast = dict(mesh.shape) == {"wide": 8, "narrow": 4}
    return jax.shard_map(
        fast_body if fast else body,
        mesh=mesh,
        in_specs=(
            P(("wide", "narrow"), None),
            P(("wide", "narrow"), None),
            P(("wide", "narrow"), None),
            P(("wide", "narrow"), None),
            P(("wide", "narrow"), None),
            P(("wide", "narrow"), None),
            P(None, ("wide", "narrow")),
            P(None, ("wide", "narrow")),
            P(("wide", "narrow")),
            P(None, ("wide", "narrow")),
            P(),
        ),
        out_specs=(
            P(("wide", "narrow"), None),
            P(("wide", "narrow"), None),
            P(("wide", "narrow"), None),
            P(("wide", "narrow"), None),
            P(("wide", "narrow"), None),
            P(("wide", "narrow"), None),
            P(None, ("wide", "narrow")),
            P(None, ("wide", "narrow")),
            P(("wide", "narrow")),
            P(None, ("wide", "narrow")),
        ),
        check_vma=False,
    )
```

```python
import jax
import jax.numpy as jnp
from jax import lax
from jax.experimental import pallas as pl
from jax.experimental.pallas import tpu as pltpu
from jax.sharding import PartitionSpec as P

HEADS = 12
HEAD_DIM = 64
RATE0 = 1
RATE1 = 2
RATE2 = 4


EPSILON = 1e-05
SCORE_SCALE = 0.125
MASKED = -1e30


def layer_norm(values, norm_gain, norm_shift):
    average = jnp.mean(values, axis=-1, keepdims=True)
    centred = values - average
    spread = jnp.mean(centred * centred, axis=-1, keepdims=True)
    return centred * lax.rsqrt(spread + EPSILON) * norm_gain + norm_shift


def gelu_exact(values):
    return jax.nn.gelu(values, approximate=False)


def product(former, latter):
    return jnp.dot(former, latter, preferred_element_type=jnp.float32)


def product_tn(former, latter):
    return lax.dot_general(
        former, latter, (((0,), (0,)), ((), ())), preferred_element_type=jnp.float32
    )


def product_nt(former, latter):
    return lax.dot_general(
        former, latter, (((1,), (1,)), ((), ())), preferred_element_type=jnp.float32
    )


def one_hot(offset_row, dilation):
    return (jnp.arange(dilation)[:, None] == offset_row[None, :]).astype(jnp.float32)


def select_rows(dense_rows, selector, dilation):
    picked_rows = dense_rows.shape[0] // dilation
    shaped = dense_rows.reshape(picked_rows, dilation, HEADS, HEAD_DIM)
    picked = jnp.einsum(
        "trhd,rh->thd",
        shaped,
        selector.astype(dense_rows.dtype),
        preferred_element_type=jnp.float32,
    )
    return picked.reshape(picked_rows, HEADS * HEAD_DIM)


def spread_rows(sparse_rows, selector, dilation):
    shaped = sparse_rows.reshape(sparse_rows.shape[0], 1, HEADS, HEAD_DIM)
    placed = shaped * selector[None, :, :, None]
    return placed.reshape(sparse_rows.shape[0] * dilation, HEADS * HEAD_DIM)


def select_heads(dense_heads, selector, dilation):
    shaped = dense_heads.reshape(dense_heads.shape[0] // dilation, dilation, HEADS)
    return jnp.sum(shaped * selector[None], axis=1)


def spread_heads(sparse_heads, selector, dilation):
    placed = jnp.where(selector[None] > 0, sparse_heads[:, None, :], MASKED)
    return placed.reshape(sparse_heads.shape[0] * dilation, HEADS)


def head_major(values):
    return values.reshape(values.shape[0], HEADS, HEAD_DIM).transpose(1, 0, 2)


def row_major(values):
    return values.transpose(1, 0, 2).reshape(values.shape[1], HEADS * HEAD_DIM)


def key_mask(row_count, block_count, own_block):
    query_pos = jnp.arange(row_count)[:, None]
    position = jnp.arange(row_count * block_count)[None, :]
    key_block = position // row_count
    within = position % row_count
    return (key_block < own_block) | (key_block == own_block) & (within <= query_pos)


def masked_scores(head_query, head_keys, allowed):
    return jnp.where(allowed, product_nt(head_query, head_keys) * SCORE_SCALE, MASKED)


def pattern_lse(queries, keys, allowed):

    def one_head(operands):
        scores = masked_scores(operands[0], operands[1], allowed)
        peak_rows = jnp.max(scores, axis=1, keepdims=True)
        return peak_rows[:, 0] + jnp.log(jnp.sum(jnp.exp(scores - peak_rows), axis=1))

    return lax.map(one_head, (head_major(queries), head_major(keys))).T


def pattern_out(queries, keys, values, allowed, totals):

    def one_head(operands):
        head_query, head_keys, head_values, head_total = operands
        scores = masked_scores(head_query, head_keys, allowed)
        probability = jnp.where(allowed, jnp.exp(scores - head_total[:, None]), 0.0).astype(
            jnp.bfloat16
        )
        return product(probability, head_values)

    return row_major(
        lax.map(one_head, (head_major(queries), head_major(keys), head_major(values), totals.T))
    )


def pattern_back(queries, keys, values, allowed, totals, deltas, grad_out):

    def one_head(operands):
        head_query, head_keys, head_values, head_total, head_delta, head_grad = operands
        scores = masked_scores(head_query, head_keys, allowed)
        probability = jnp.where(allowed, jnp.exp(scores - head_total[:, None]), 0.0)
        grad_probs = product_nt(head_grad, head_values)
        grad_scores = (probability * (grad_probs - head_delta[:, None])).astype(jnp.bfloat16)
        grad_query = product(grad_scores, head_keys) * SCORE_SCALE
        grad_keys = product_tn(grad_scores, head_query) * SCORE_SCALE
        grad_values = product_tn(probability.astype(jnp.bfloat16), head_grad)
        return (grad_query, grad_keys, grad_values)

    results = lax.map(
        one_head,
        (
            head_major(queries),
            head_major(keys),
            head_major(values),
            totals.T,
            deltas.T,
            head_major(grad_out),
        ),
    )
    return (row_major(results[0]), row_major(results[1]), row_major(results[2]))


def body(
    tokens,
    cotangent,
    w_qkv,
    w_attn,
    w_in,
    w_out,
    gains_model,
    biases_model,
    gain_ffn,
    biases_ffn,
    offsets,
):
    gathered = (
        lax.all_gather(w_qkv, ("wide", "narrow"), axis=0, tiled=True),
        lax.all_gather(w_attn, ("wide", "narrow"), axis=0, tiled=True),
        lax.all_gather(w_in, ("wide", "narrow"), axis=0, tiled=True),
        lax.all_gather(w_out, ("wide", "narrow"), axis=0, tiled=True),
        lax.all_gather(gains_model, ("wide", "narrow"), axis=1, tiled=True),
        lax.all_gather(biases_model, ("wide", "narrow"), axis=1, tiled=True),
        lax.all_gather(gain_ffn, ("wide", "narrow"), axis=0, tiled=True),
        lax.all_gather(biases_ffn, ("wide", "narrow"), axis=1, tiled=True),
    )
    qkv_full, attn_full, in_full, out_full = (gathered[0], gathered[1], gathered[2], gathered[3])
    model_gains = gathered[4].astype(jnp.float32)
    model_biases = gathered[5].astype(jnp.float32)
    ffn_gain = gathered[6].astype(jnp.float32)
    ffn_biases = gathered[7].astype(jnp.float32)
    local_rows = tokens.shape[0]
    width = tokens.shape[1]
    inputs = tokens.astype(jnp.float32)
    normed_one, pull_one = jax.vjp(layer_norm, inputs, model_gains[0], model_biases[0])
    normed_low = normed_one.astype(jnp.bfloat16)
    projected = product(normed_low, qkv_full)
    queries = (projected[:, :width] + model_biases[1]).astype(jnp.bfloat16)
    keys = projected[:, width : 2 * width].astype(jnp.bfloat16)
    values = (projected[:, 2 * width :] + model_biases[2]).astype(jnp.bfloat16)
    size_narrow = lax.axis_size("narrow")
    narrow_place = lax.axis_index("narrow")
    dilations = (RATE0, RATE1, RATE2)
    selectors = (one_hot(offsets[0], RATE0), one_hot(offsets[1], RATE1), one_hot(offsets[2], RATE2))
    picked_q = [
        select_rows(queries, selectors[pattern], dilations[pattern]).astype(jnp.bfloat16)
        for pattern in range(3)
    ]
    picked_k = [
        select_rows(keys, selectors[pattern], dilations[pattern]).astype(jnp.bfloat16)
        for pattern in range(3)
    ]
    picked_v = [
        select_rows(values, selectors[pattern], dilations[pattern]).astype(jnp.bfloat16)
        for pattern in range(3)
    ]
    arrived = (
        lax.all_gather(picked_k[0], "narrow", axis=0, tiled=True),
        lax.all_gather(picked_v[0], "narrow", axis=0, tiled=True),
        lax.all_gather(picked_k[1], "narrow", axis=0, tiled=True),
        lax.all_gather(picked_v[1], "narrow", axis=0, tiled=True),
        lax.all_gather(picked_k[2], "narrow", axis=0, tiled=True),
        lax.all_gather(picked_v[2], "narrow", axis=0, tiled=True),
    )
    key_sets = (arrived[0], arrived[2], arrived[4])
    value_sets = (arrived[1], arrived[3], arrived[5])
    allowed_sets = tuple(
        (
            key_mask(local_rows // dilations[pattern], size_narrow, narrow_place)
            for pattern in range(3)
        )
    )
    partial_value = jnp.stack(
        [
            spread_heads(
                pattern_lse(picked_q[pattern], key_sets[pattern], allowed_sets[pattern]),
                selectors[pattern],
                dilations[pattern],
            )
            for pattern in range(3)
        ]
    )
    peak_rows = jnp.max(partial_value, axis=0)
    totals = peak_rows + jnp.log(jnp.sum(jnp.exp(partial_value - peak_rows), axis=0))
    attended = jnp.zeros((local_rows, width), jnp.float32)
    for pattern in range(3):
        pattern_totals = select_heads(totals, selectors[pattern], dilations[pattern])
        result_rows = pattern_out(
            picked_q[pattern],
            key_sets[pattern],
            value_sets[pattern],
            allowed_sets[pattern],
            pattern_totals,
        )
        attended = attended + spread_rows(result_rows, selectors[pattern], dilations[pattern])
    sub_normed, pull_sub = jax.vjp(layer_norm, attended, model_gains[1], model_biases[3])
    sub_low = sub_normed.astype(jnp.bfloat16)
    middle = inputs + product(sub_low, attn_full) + model_biases[4]
    normed_two, pull_two = jax.vjp(layer_norm, middle, model_gains[2], model_biases[5])
    normed_two_low = normed_two.astype(jnp.bfloat16)
    pre_act = product(normed_two_low, in_full) + ffn_biases[0]
    activated, pull_gelu = jax.vjp(gelu_exact, pre_act)
    ffn_normed, pull_ffn = jax.vjp(layer_norm, activated, ffn_gain, ffn_biases[1])
    ffn_low = ffn_normed.astype(jnp.bfloat16)
    outputs = (middle + product(ffn_low, out_full) + model_biases[6]).astype(jnp.bfloat16)
    regathered = (
        lax.all_gather(w_qkv, ("wide", "narrow"), axis=0, tiled=True),
        lax.all_gather(w_attn, ("wide", "narrow"), axis=0, tiled=True),
        lax.all_gather(w_in, ("wide", "narrow"), axis=0, tiled=True),
        lax.all_gather(w_out, ("wide", "narrow"), axis=0, tiled=True),
    )
    qkv_back, attn_back, in_back, out_back = (
        regathered[0],
        regathered[1],
        regathered[2],
        regathered[3],
    )
    grad_out_f = cotangent.astype(jnp.float32)
    grad_w_out = product_tn(ffn_low, cotangent)
    grad_bias_ffo = jnp.sum(cotangent.astype(jnp.float32), axis=0)
    grad_act, grad_gain_ffn, grad_bias_ffn_norm = pull_ffn(product_nt(cotangent, out_back))
    grad_pre = pull_gelu(grad_act)[0].astype(jnp.bfloat16)
    grad_w_in = product_tn(normed_two_low, grad_pre)
    grad_bias_pre = jnp.sum(grad_pre.astype(jnp.float32), axis=0)
    grad_mid_norm, grad_gain_two, grad_bias_two = pull_two(product_nt(grad_pre, in_back))
    grad_middle = grad_out_f + grad_mid_norm
    grad_branch = grad_middle.astype(jnp.bfloat16)
    grad_w_attn = product_tn(sub_low, grad_branch)
    grad_bias_branch = jnp.sum(grad_branch.astype(jnp.float32), axis=0)
    grad_att, grad_gain_sub, grad_bias_sub = pull_sub(product_nt(grad_branch, attn_back))
    grad_att_low = grad_att.astype(jnp.bfloat16)
    deltas = jnp.sum(
        (grad_att_low.astype(jnp.float32) * attended).reshape(local_rows, HEADS, HEAD_DIM), axis=2
    )
    backward_parts = []
    for pattern in range(3):
        backward_parts.append(
            pattern_back(
                picked_q[pattern],
                key_sets[pattern],
                value_sets[pattern],
                allowed_sets[pattern],
                select_heads(totals, selectors[pattern], dilations[pattern]),
                select_heads(deltas, selectors[pattern], dilations[pattern]),
                select_rows(grad_att_low, selectors[pattern], dilations[pattern]).astype(
                    jnp.bfloat16
                ),
            )
        )
    returned = (
        lax.psum_scatter(
            backward_parts[0][1].astype(jnp.bfloat16), "narrow", scatter_dimension=0, tiled=True
        ).astype(jnp.float32),
        lax.psum_scatter(
            backward_parts[0][2].astype(jnp.bfloat16), "narrow", scatter_dimension=0, tiled=True
        ).astype(jnp.float32),
        lax.psum_scatter(
            backward_parts[1][1].astype(jnp.bfloat16), "narrow", scatter_dimension=0, tiled=True
        ).astype(jnp.float32),
        lax.psum_scatter(
            backward_parts[1][2].astype(jnp.bfloat16), "narrow", scatter_dimension=0, tiled=True
        ).astype(jnp.float32),
        lax.psum_scatter(
            backward_parts[2][1].astype(jnp.bfloat16), "narrow", scatter_dimension=0, tiled=True
        ).astype(jnp.float32),
        lax.psum_scatter(
            backward_parts[2][2].astype(jnp.bfloat16), "narrow", scatter_dimension=0, tiled=True
        ).astype(jnp.float32),
    )
    key_grads = (returned[0], returned[2], returned[4])
    value_grads = (returned[1], returned[3], returned[5])
    grad_q = jnp.zeros((local_rows, width), jnp.float32)
    grad_k = jnp.zeros((local_rows, width), jnp.float32)
    grad_v = jnp.zeros((local_rows, width), jnp.float32)
    for pattern in range(3):
        grad_q = grad_q + spread_rows(
            backward_parts[pattern][0], selectors[pattern], dilations[pattern]
        )
        grad_k = grad_k + spread_rows(key_grads[pattern], selectors[pattern], dilations[pattern])
        grad_v = grad_v + spread_rows(value_grads[pattern], selectors[pattern], dilations[pattern])
    grad_q_low = grad_q.astype(jnp.bfloat16)
    grad_v_low = grad_v.astype(jnp.bfloat16)
    grad_qkv = jnp.concatenate([grad_q_low, grad_k.astype(jnp.bfloat16), grad_v_low], axis=1)
    grad_w_qkv = product_tn(normed_low, grad_qkv)
    grad_bias_q = jnp.sum(grad_q_low.astype(jnp.float32), axis=0)
    grad_bias_v = jnp.sum(grad_v_low.astype(jnp.float32), axis=0)
    grad_first, grad_gain_one, grad_bias_one = pull_one(product_nt(grad_qkv, qkv_back))
    grad_inputs = grad_middle + grad_first
    grad_gains = jnp.stack([grad_gain_one, grad_gain_sub, grad_gain_two])
    grad_biases = jnp.stack(
        [
            grad_bias_one,
            grad_bias_q,
            grad_bias_v,
            grad_bias_sub,
            grad_bias_branch,
            grad_bias_two,
            grad_bias_ffo,
        ]
    )
    grad_ffn_biases = jnp.stack([grad_bias_pre, grad_bias_ffn_norm])
    reduced = (
        lax.psum_scatter(grad_w_qkv, ("wide", "narrow"), scatter_dimension=0, tiled=True),
        lax.psum_scatter(grad_w_attn, ("wide", "narrow"), scatter_dimension=0, tiled=True),
        lax.psum_scatter(grad_w_in, ("wide", "narrow"), scatter_dimension=0, tiled=True),
        lax.psum_scatter(grad_w_out, ("wide", "narrow"), scatter_dimension=0, tiled=True),
        lax.psum_scatter(grad_gains, ("wide", "narrow"), scatter_dimension=1, tiled=True),
        lax.psum_scatter(grad_biases, ("wide", "narrow"), scatter_dimension=1, tiled=True),
        lax.psum_scatter(grad_gain_ffn, ("wide", "narrow"), scatter_dimension=0, tiled=True),
        lax.psum_scatter(grad_ffn_biases, ("wide", "narrow"), scatter_dimension=1, tiled=True),
    )
    return (
        outputs,
        grad_inputs,
        reduced[0],
        reduced[1],
        reduced[2],
        reduced[3],
        reduced[4],
        reduced[5],
        reduced[6],
        reduced[7],
    )


BF16 = jnp.bfloat16
F32 = jnp.float32
ALPHA = (
    -2.72614225801306e-10,
    2.77068142495902e-08,
    -2.10102402082508e-06,
    -5.69250639462346e-05,
    -7.34990630326855e-04,
    -2.95459980854025e-03,
    -1.60960333262415e-02,
)
BETA = (
    -1.45660718464996e-05,
    -2.13374055278905e-04,
    -1.68282697438203e-03,
    -7.37332916720468e-03,
    -1.42647390514189e-02,
)


def nn(a, b):
    return lax.dot_general(a, b, (((1,), (0,)), ((), ())), preferred_element_type=F32)


def nt(a, b):
    return lax.dot_general(a, b, (((1,), (1,)), ((), ())), preferred_element_type=F32)


def tn(a, b):
    return lax.dot_general(a, b, (((0,), (0,)), ((), ())), preferred_element_type=F32)


def erf(v):
    v = jnp.clip(v, -4.0, 4.0)
    s = v * v
    top = jnp.full_like(s, ALPHA[0])
    for term in ALPHA[1:]:
        top = top * s + term
    low = jnp.full_like(s, BETA[0])
    for term in BETA[1:]:
        low = low * s + term
    return v * top / low


def normed(v):
    centred = v - jnp.mean(v, axis=-1, keepdims=True)
    rate = lax.rsqrt(jnp.mean(centred * centred, axis=-1, keepdims=True) + EPSILON)
    return centred * rate, rate


def norm_back(e, n, rate, gain):
    t = e * gain
    return rate * (
        t - jnp.mean(t, axis=-1, keepdims=True) - n * jnp.mean(t * n, axis=-1, keepdims=True)
    )


def colsum(v):
    return jnp.sum(v, axis=0, keepdims=True)


def lanes(shape):
    return lax.broadcasted_iota(jnp.int32, shape, len(shape) - 1)


def sublanes(shape):
    return lax.broadcasted_iota(jnp.int32, shape, len(shape) - 2)


def rows_of(parts, count):
    shape = (count, next(part for part in parts if part is not None).shape[1])
    at = sublanes(shape)
    out = jnp.zeros(shape, F32)
    for i, part in enumerate(parts):
        if part is not None:
            out = jnp.where(at == i, part, out)
    return out


def to_rows(columns):
    shape = (columns[0].shape[0], 128)
    at = lanes(shape)
    out = jnp.zeros(shape, F32)
    for i, column in enumerate(columns):
        out = jnp.where(at == i, column, out)
    return out.T[0:8]


def to_columns(rows):
    wide = rows_of(rows, 128).T
    return [wide[:, i : i + 1] for i in range(len(rows))]


def left(v, amount, width):
    return pltpu.roll(v, lax.rem(width - amount, width), 1)


def call(kernel, outs, *operands, scratch=(), limit=24, final=False, held=True, us=0.0):
    whole = pl.BlockSpec(memory_space=pltpu.VMEM)
    placed = [
        a
        if a.dtype == jnp.int32
        else pltpu.with_memory_space_constraint(a, pltpu.VMEM if held else pltpu.HBM)
        for a in operands
    ]
    return pl.pallas_call(
        kernel,
        out_shape=[jax.ShapeDtypeStruct(s, d) if final else pltpu.VMEM(s, d) for s, d in outs],
        in_specs=[
            pl.BlockSpec(memory_space=pltpu.SMEM) if a.dtype == jnp.int32 else whole
            for a in operands
        ],
        out_specs=[whole for _ in outs],
        scratch_shapes=[pltpu.VMEM(s, d) for s, d in scratch],
        compiler_params=pltpu.CompilerParams(vmem_limit_bytes=limit << 20),
        cost_estimate=pl.CostEstimate(
            flops=int(us * 1e9), transcendentals=0, bytes_accessed=int(us * 3.6e6)
        ),
        name=kernel.__name__,
    )(*placed)


def after(value, *others):
    return lax.optimization_barrier((value, *others))[0]


def prep_kernel(
    idx, wqkv, win, wattn, gains, biases, gffn, bffn, tok, cot, wout, tok_out, cot_out, wout_out,
    b0, b1, b2, b3, small, qs, is_,
):
    n = idx[1]
    tok_out[...] = tok[...]
    cot_out[...] = cot[...]
    wout_out[...] = wout[...]
    small[...] = jnp.zeros_like(small)
    small[0:3, 0:24] = gains[...].astype(F32)
    small[3:10, 0:24] = biases[...].astype(F32)
    ffn_g = gffn[...].astype(F32)
    ffn_b = bffn[...].astype(F32)
    for k in range(4):
        small[16 + 8 * k : 17 + 8 * k, 0:24] = ffn_g[:, k * 24 : k * 24 + 24]
        small[17 + 8 * k : 19 + 8 * k, 0:24] = ffn_b[:, k * 24 : k * 24 + 24]
    eye = (sublanes((24, 128)) == lanes((24, 128))).astype(BF16)
    params = nt(eye, small[...].astype(BF16))
    weights = wqkv[...].astype(F32)
    for m in range(4):
        for part in range(3):
            at = part * 768 + m * 192
            qs[m, :, part * 192 : part * 192 + 192] = weights[:, at : at + 192]
        qs[m, :, 576:640] = params
    inner = win[...].astype(F32)
    for m in range(4):
        for w in range(8):
            at = (w * 4 + m) * 96
            is_[m, :, w * 96 : w * 96 + 96] = inner[:, at : at + 96]
    for k, out in enumerate((b0, b1, b2, b3)):
        out[:, 0:640] = qs[n ^ k].astype(BF16)
        out[:, 640:1408] = is_[n ^ k].astype(BF16)
        if k % 2 == 0:
            out[:, 1408:2176] = wattn[...]


def pack_kernel(idx, b0, b1, b2, b3, q_out, r_out, qs, is_, two):
    n = idx[1]
    for k, b in enumerate((b0, b1, b2, b3)):
        qs[n ^ k] = b[:, 0:640].astype(F32)
        is_[n ^ k] = b[:, 640:1408].astype(F32)
        if k % 2 == 0:
            two[(n ^ k) // 2] = b[:, 1408:2176].astype(F32)
    q_out[...] = qs[...].reshape(96, 640).astype(BF16)
    r_out[0:96] = is_[...].reshape(96, 768).astype(BF16)
    r_out[96:144] = two[...].reshape(48, 768).astype(BF16)


def place_i_kernel(idx, r0, r1, r2, r3, r4, r5, r6, r7, win, attn):
    w = idx[0]
    for j, r in enumerate((r0, r1, r2, r3, r4, r5, r6, r7)):
        win[pl.ds(pl.multiple_of((w ^ j) * 96, 32), 96), :] = r[0:96]
        attn[w ^ j] = r[96:144]


def place_c_kernel(idx, r0, r1, r2, r3, r4, r5, r6, r7, wout):
    w = idx[0]
    for j, r in enumerate((r0, r1, r2, r3, r4, r5, r6, r7)):
        wout[pl.ds(pl.multiple_of((w ^ j) * 96, 32), 96), :] = r[...]


def place_a_kernel(idx, a0, a1, wattn, buf):
    core = lax.rem(idx[1], 2)
    for side, a in ((core, a0), (1 - core, a1)):
        for w_ in range(8):
            for x_ in range(2):
                buf[w_, x_ * 2 + side] = a[w_, x_ * 24 : x_ * 24 + 24].astype(F32)
    wattn[...] = buf[...].reshape(768, 768).astype(BF16)


def place_t_kernel(idx, t0, t1, t2, t3, out):
    n = idx[1]
    for k, t in enumerate((t0, t1, t2, t3)):
        out[pl.ds(pl.multiple_of((n ^ k) * 128, 128), 128), :] = t[...]


def norm_kernel(x, n_out):
    n_out[...], _ = normed(x[...].astype(F32))


def attend_kernel(
    idx, off, n1, q0, q1, q2, q3, q4, q5, q6, q7,
    w_out, p_out, a_out, qkv_out, o_t_out, lse_out, o_out,
):
    w, n = idx[0], idx[1]
    for j, q in enumerate((q0, q1, q2, q3, q4, q5, q6, q7)):
        w_out[pl.ds(pl.multiple_of((w ^ j) * 96, 32), 96), :] = q[...]
    pick = (sublanes((64, 128)) + 64 == lanes((64, 128))).astype(BF16)
    table = nt(pick, w_out[:, 512:640])
    model = table[0:16]
    ffn = jnp.zeros((8, 768), F32)
    inside = lax.rem(lanes((8, 768)), 96) // 24
    for k in range(4):
        turned = pltpu.roll(table[16 + 8 * k : 24 + 8 * k], lax.rem(768 + (k - n) * 24, 768), 1)
        ffn = jnp.where(inside == k, turned, ffn)
    p_out[0:16] = model
    p_out[16:24] = ffn
    a1 = (n1[...] * model[0:1] + model[3:4]).astype(BF16)
    a_out[...] = a1
    qkv = nn(a1, w_out[...])
    lane = lanes((8, 768))
    bias_q = left(jnp.broadcast_to(model[4:5], (8, 768)), n * 192, 768)
    bias_v = pltpu.roll(
        jnp.broadcast_to(model[5:6], (8, 768)), lax.rem(768 + 384 - n * 192, 768), 1
    )
    bias = jnp.where(
        lane < 192, bias_q, jnp.where((lane >= 384) & (lane < 576), bias_v, 0.0)
    )[0:1, 0:640]
    qkv = jnp.where(lanes((1, 640)) < 576, qkv + bias, 0.0).astype(BF16)
    qkv_out[...] = qkv
    v_t = qkv[:, 384:576].astype(F32).T
    o_parts, lse_rows = [], []
    for h in range(3):
        head = n * 3 + h
        o1, o2 = off[1, head], off[2, head]
        at = lanes((1, 512))
        r1 = (lax.rem(at, 2) == o1).astype(F32)
        r2 = (lax.rem(at, 4) == o2).astype(F32)
        head_v = v_t[h * 64 : h * 64 + 64]
        ones = rows_of([jnp.ones((1, 512), F32), r1, r2], 8)
        left_side = jnp.concatenate([head_v, head_v * r1, head_v * r2, ones], axis=0).astype(BF16)
        head_q = qkv[:, h * 64 : h * 64 + 64] * jnp.asarray(SCORE_SCALE, BF16)
        head_k = qkv[:, 192 + h * 64 : 256 + h * 64]
        blocks, lses = [], []
        for i in range(2):
            keys = 256 * (i + 1)
            scores = nt(head_k[0:keys], head_q[i * 256 : i * 256 + 256])
            shape = (keys, 256)
            scores = jnp.where(sublanes(shape) <= lanes(shape) + i * 256, scores, MASKED)
            peak = jnp.max(scores, axis=0, keepdims=True)
            weight = jnp.exp(scores - peak).astype(BF16)
            both = nn(left_side[:, 0:keys], weight)
            s1, s2 = r1[:, i * 256 : i * 256 + 256], r2[:, i * 256 : i * 256 + 256]
            total = both[192:193] + s1 * both[193:194] + s2 * both[194:195]
            blocks.append((both[0:64] + s1 * both[64:128] + s2 * both[128:192]) / total)
            lses.append(peak + jnp.log(total))
        o_parts.append(jnp.concatenate(blocks, axis=1))
        lse_rows.append(jnp.concatenate(lses, axis=1))
    o_t = jnp.concatenate(o_parts, axis=0)
    o_t_out[...] = o_t
    lse_out[...] = rows_of(lse_rows, 8)
    o_out[...] = o_t.T.astype(BF16)


def middle_kernel(
    idx, x, p, o0, o1, o2, o3, wattn, win,
    n_o_out, rate_o_out, u_out, x2_out, h2_out, f_out, dg_out, stat_out, o_buf,
):
    n = idx[1]
    for k, o in enumerate((o0, o1, o2, o3)):
        o_buf[n ^ k] = o[...].astype(F32)
    o = jnp.concatenate([o_buf[m] for m in range(4)], axis=1)
    n_o, rate_o = normed(o)
    n_o_out[...] = n_o
    rate_o_out[...] = rate_o
    u = (n_o * p[1:2] + p[6:7]).astype(BF16)
    u_out[...] = u
    x2 = x[...].astype(F32) + nn(u, wattn[...]) + p[7:8]
    x2_out[...] = x2
    n2, _ = normed(x2)
    h2 = (n2 * p[2:3] + p[8:9]).astype(BF16)
    h2_out[...] = h2
    c = nn(h2, win[...]) + p[17:18]
    half = 0.5 + 0.5 * erf(c * 0.7071067811865476)
    f = c * half
    f_out[...] = f
    dg_out[...] = half + c * jnp.exp(c * c * -0.5) * 0.3989422804014327
    mean = jnp.mean(f, axis=1, keepdims=True)
    centred = f - mean
    stat_out[...] = to_rows([mean, jnp.sum(centred * centred, axis=1, keepdims=True)])


def cot_kernel(gy, wout, e_out):
    e_out[...] = nt(gy[...], wout[...])


def stat_kernel(p, e, f, stat_in, stat_out):
    t = e[...] * p[16:17]
    mean = jnp.mean(f[...], axis=1, keepdims=True)
    rows = to_rows(
        [jnp.sum(t, axis=1, keepdims=True), jnp.sum(t * (f[...] - mean), axis=1, keepdims=True)]
    )
    stat_out[...] = jnp.where(sublanes((8, 512)) < 2, stat_in[...], jnp.roll(rows, 2, axis=0))


def ffn_columns(s0, s1, s2, s3):
    parts = [s[...] for s in (s0, s1, s2, s3)]
    count = 768.0 * 4
    mean = sum(s[0:1] for s in parts) * 0.25
    spread = sum(s[1:2] + 768.0 * (s[0:1] - mean) * (s[0:1] - mean) for s in parts) / count
    rate = lax.rsqrt(spread + EPSILON)
    mean_t = sum(s[2:3] for s in parts) / count
    mean_tn = rate * sum(s[3:4] + (s[0:1] - mean) * s[2:3] for s in parts) / count
    return to_columns([mean, rate, mean_t, mean_tn])


def core_halves(value, keep, send, core, buf):
    buf[...] = value
    for x_ in range(2):
        mine = pl.ds(pl.multiple_of((x_ * 2 + core) * 128, 128), 128)
        other = pl.ds(pl.multiple_of((x_ * 2 + 1 - core) * 128, 128), 128)
        keep[x_ * 128 : x_ * 128 + 128, :] = buf[mine, :].astype(keep.dtype)
        send[x_ * 128 : x_ * 128 + 128, :] = buf[other, :].astype(send.dtype)


def ffn_back_kernel(idx, p, s0, s1, s2, s3, f, dg, e, win, gc_out, keep, send, buf):
    core = lax.rem(idx[1], 2)
    mean, rate, mean_t, mean_tn = ffn_columns(s0, s1, s2, s3)
    n_f = (f[...] - mean) * rate
    df = rate * (e[...] * p[16:17] - mean_t - n_f * mean_tn)
    gc = (df * dg[...]).astype(BF16)
    gc_out[...] = gc
    core_halves(nt(gc, win[...]), keep, send, core, buf)


def by_wide(value, w, steps, out):
    for i, step in enumerate(steps):
        out[i] = value[pl.ds(pl.multiple_of((w ^ step) * 96, 32), 96), :].astype(BF16)


def ffn_grad_kernel(
    idx, p, s0, s1, s2, s3, f, e, gy, z_out, keep_a, keep_b, send_a, send_b, sums, prod
):
    mean, rate, _, _ = ffn_columns(s0, s1, s2, s3)
    n_f = (f[...] - mean) * rate
    z = (n_f * p[16:17] + p[18:19]).astype(BF16)
    z_out[...] = z
    prod[...] = tn(z, gy[...])
    for steps, out in (((2, 6), keep_a), ((0, 4), keep_b), ((3, 7), send_a), ((1, 5), send_b)):
        by_wide(prod, idx[0], steps, out)
    sums[...] = rows_of([colsum(e[...] * n_f), None, colsum(e[...]), None], 8)


def in_grad_kernel(idx, h2, gc, keep_a, keep_b, send_a, send_b, prod):
    prod[...] = tn(h2[...], gc[...])
    for steps, out in (((4, 5), keep_a), ((0, 1), keep_b), ((6, 7), send_a), ((2, 3), send_b)):
        by_wide(prod, idx[0], steps, out)


def out_kernel(idx, z, wout, gc, gy, sums_in, keep, send, sums, buf):
    core_halves(nn(z[...], wout[...]), keep, send, lax.rem(idx[1], 2), buf)
    extra = rows_of([None, colsum(gc[...].astype(F32)), None, colsum(gy[...].astype(F32))], 8)
    sums[...] = sums_in[...] + extra


def prob_kernel(qkv, lse, *outs):
    for h in range(3):
        low_q = qkv[:, h * 64 : h * 64 + 64] * jnp.asarray(SCORE_SCALE, BF16)
        head_k = qkv[:, 192 + h * 64 : 256 + h * 64]
        for i in range(2):
            keys = 256 * (i + 1)
            here = slice(i * 256, i * 256 + 256)
            shape = (keys, 256)
            scores = nt(head_k[0:keys], low_q[here])
            outs[i][h] = jnp.where(
                sublanes(shape) <= lanes(shape) + i * 256,
                jnp.exp(scores - lse[h : h + 1, here]),
                0.0,
            )


def norm_two_kernel(x2, n2_out, rate_out):
    n2_out[...], rate_out[...] = normed(x2[...])


def add_kernel(keep, got, out):
    out[...] = (keep[...].astype(F32) + got[...].astype(F32)).astype(out.dtype)


def hop_kernel(keep, got, own, send):
    for i in range(2):
        own[i] = keep[2 * i].astype(F32) + got[2 * i].astype(F32)
        send[i] = (keep[2 * i + 1].astype(F32) + got[2 * i + 1].astype(F32)).astype(BF16)


def pair_kernel(keep, got, out):
    for i in range(2):
        out[i] = (keep[i].astype(F32) + got[i].astype(F32)).astype(out.dtype)


def last_hop_kernel(own, got, mine, send):
    mine[...] = own[0] + got[0].astype(F32)
    send[...] = (own[1] + got[1].astype(F32)).astype(BF16)


def sum_out_kernel(mine, got, out):
    out[...] = mine[...] + got[...].astype(F32)


def mid_back_kernel(
    idx, p, own, own_x, sib, sib_x, n2, rate2, gy, n_o, rate_o, wattn,
    dx2_out, ga_out, do_out, e2_out, eo_out,
):
    n = idx[1]
    core = lax.rem(n, 2)
    for x_ in range(2):
        at = slice(x_ * 128, x_ * 128 + 128)
        mine = pl.ds(pl.multiple_of((x_ * 2 + core) * 128, 128), 128)
        other = pl.ds(pl.multiple_of((x_ * 2 + 1 - core) * 128, 128), 128)
        e2_out[mine, :] = own[at].astype(F32) + own_x[at].astype(F32)
        e2_out[other, :] = sib[at].astype(F32) + sib_x[at].astype(F32)
    dx2 = gy[...].astype(F32) + norm_back(e2_out[...], n2[...], rate2[...], p[2:3])
    dx2_out[...] = dx2
    ga = dx2.astype(BF16)
    ga_out[...] = ga
    eo = nt(ga, wattn[...])
    eo_out[...] = eo
    d_o = norm_back(eo, n_o[...], rate_o[...], p[1:2])
    for m in range(4):
        @pl.when(n == m)
        def _():
            do_out[...] = d_o[:, m * 192 : m * 192 + 192].astype(BF16)


def attn_grad_kernel(idx, u, ga, eo, n_o, e2, n2, sums, keep, send, gat):
    w, n = idx[0], idx[1]
    e_o, e_2 = eo[...], e2[...]
    model = rows_of(
        [
            None,
            colsum(e_o * n_o[...]),
            colsum(e_2 * n2[...]),
            None,
            None,
            None,
            colsum(e_o),
            colsum(ga[...].astype(F32)),
            colsum(e_2),
            sums[3:4],
        ],
        16,
    )
    gat[...] = tn(u[...], ga[...]).reshape(8, 4, 24, 768)
    for i in range(8):
        to = w ^ i
        block = (keep if i % 2 == 0 else send).at[i // 2]
        mine = left(model, to * 96 + n * 24, 768)
        ffn = left(sums[...], to * 96, 768)
        extra = jnp.concatenate(
            [mine[0:8, 0:128], mine[8:16, 0:128], ffn[:, 0:128], jnp.zeros((8, 384), F32)], axis=1
        )
        block[...] = jnp.concatenate([gat[to, n], extra], axis=0).astype(BF16)


def head_back_kernel(
    idx, off, qkv, o_t, p0, p1, do, a1, wqkv, n1,
    keep_a, keep_b, send_a, send_b, d_keep, d_send, buf, prod,
):
    w, n = idx[0], idx[1]
    core = lax.rem(n, 2)
    do_t = do[...].astype(F32).T
    k_t = qkv[:, 192:384].astype(F32).T
    row = lanes((1, 512))
    column = sublanes((512, 1))
    dq_parts, dk_parts, dv_parts = [], [], []
    for h in range(3):
        head = n * 3 + h
        o1, o2 = off[1, head], off[2, head]
        r1 = (lax.rem(row, 2) == o1).astype(F32)
        r2 = (lax.rem(row, 4) == o2).astype(F32)
        c1 = (lax.rem(column, 2) == o1).astype(F32)
        c2 = (lax.rem(column, 4) == o2).astype(F32)
        span = slice(h * 64, h * 64 + 64)
        delta = colsum(do_t[span] * o_t[span, :])
        head_q = qkv[:, h * 64 : h * 64 + 64].astype(F32) * SCORE_SCALE
        head_v = qkv[:, 384 + h * 64 : 448 + h * 64]
        head_do = do[:, h * 64 : h * 64 + 64]
        do_f = head_do.astype(F32)
        q_all = jnp.concatenate([head_q, head_q * c1, head_q * c2], axis=1).astype(BF16)
        do_all = jnp.concatenate([do_f, do_f * c1, do_f * c2], axis=1).astype(BF16)
        kt = k_t[span]
        k_all = jnp.concatenate([kt, kt * r1, kt * r2], axis=0).astype(BF16)
        dk = jnp.zeros((512, 192), F32)
        dv = jnp.zeros((512, 192), F32)
        dq_blocks = []
        for i in range(2):
            keys = 256 * (i + 1)
            here = slice(i * 256, i * 256 + 256)
            prob = (p0, p1)[i][h]
            grad_p = nt(head_v[0:keys], head_do[here])
            grad_s = (prob * (grad_p - delta[:, here])).astype(BF16)
            dv_i = nn(prob.astype(BF16), do_all[here])
            dk_i = nn(grad_s, q_all[here])
            if keys < 512:
                zero = jnp.zeros((512 - keys, 192), F32)
                dv_i = jnp.concatenate([dv_i, zero], axis=0)
                dk_i = jnp.concatenate([dk_i, zero], axis=0)
            dv = dv + dv_i
            dk = dk + dk_i
            dq_i = nn(k_all[:, 0:keys], grad_s)
            dq_blocks.append(dq_i[0:64] + r1[:, here] * dq_i[64:128] + r2[:, here] * dq_i[128:192])
        dq_parts.append(jnp.concatenate(dq_blocks, axis=1) * SCORE_SCALE)
        dk_parts.append(dk[:, 0:64] + c1 * dk[:, 64:128] + c2 * dk[:, 128:192])
        dv_parts.append(dv[:, 0:64] + c1 * dv[:, 64:128] + c2 * dv[:, 128:192])
    dq = jnp.concatenate(dq_parts, axis=0).T
    g = jnp.concatenate([dq] + dk_parts + dv_parts + [jnp.zeros((512, 64), F32)], axis=1)
    g = g.astype(BF16)
    prod[...] = tn(a1[...], g)
    grad = nt(g, wqkv[...])
    outer = rows_of([None, colsum(grad * n1[...]), colsum(grad)], 8)
    g_sum = colsum(g.astype(F32))
    for i in range(8):
        to = w ^ i
        block = ((keep_b, keep_a), (send_b, send_a))[i % 2][i // 2 % 2].at[i // 4]
        turned = left(outer, to * 96, 768)[:, 0:640]
        extra = jnp.where(sublanes((8, 640)) == 0, g_sum, turned)
        mine = prod[pl.ds(pl.multiple_of(to * 96, 32), 96), :]
        block[...] = jnp.concatenate([mine, extra], axis=0).astype(BF16)
    core_halves(grad, d_keep, d_send, core, buf)


def tail_add_kernel(idx, ok, og, dk, dg, keep, send, buf):
    x_ = idx[1] // 2
    buf[:, 0:768] = ok[...].astype(F32) + og[...].astype(F32)
    buf[:, 768:1536] = dk[...].astype(F32) + dg[...].astype(F32)
    keep[...] = buf[pl.ds(pl.multiple_of(x_ * 128, 128), 128), :]
    send[...] = buf[pl.ds(pl.multiple_of((1 - x_) * 128, 128), 128), :].astype(BF16)


def token_kernel(idx, p, keep, got, tok, x2, dx2, out, grad):
    mine = pl.ds(pl.multiple_of(idx[1] * 128, 128), 128)
    both = keep[...] + got[...].astype(F32)
    out[...] = (x2[mine, :] + both[:, 0:768] + p[9:10]).astype(BF16)
    n1, rate = normed(tok[...].astype(F32))
    grad[...] = dx2[mine, :] + norm_back(both[:, 768:1536], n1, rate, p[0:1])


def sum_in_kernel(idx, mine, got, own, t1, t2, t3, buf):
    n = idx[1]
    buf[...] = (mine[...] + got[...].astype(F32)).reshape(4, 24, 768)
    own[...] = buf[n]
    for k, out in enumerate((t1, t2, t3)):
        out[...] = buf[n ^ (k + 1)].astype(BF16)


def sum_qkv_kernel(idx, mine, got, own, t1, t2, t3, buf):
    n = idx[1]
    total = mine[...] + got[...].astype(F32)
    buf[...] = total[0:96].reshape(4, 24, 640)
    own[0:24] = buf[n]
    own[24:32] = total[96:104]
    for k, out in enumerate((t1, t2, t3)):
        out[...] = jnp.concatenate([buf[n ^ (k + 1)], total[96:104]], axis=0).astype(BF16)


def final_in_kernel(idx, i0, i1, i2, i3, out, buf):
    n = idx[1]
    for k, i in enumerate((i0, i1, i2, i3)):
        buf[n ^ k] = i[...].astype(F32)
    for m in range(4):
        block = buf[m]
        for w in range(8):
            at = (w * 4 + m) * 96
            out[:, at : at + 96] = block[:, w * 96 : w * 96 + 96]


def final_kernel(idx, q0, q1, q2, q3, a_mine, a_got, gq, gattn, gains, biases, gffn, bffn, buf):
    w, n = idx[0], idx[1]
    total = a_mine[...] + a_got[...].astype(F32)
    gattn[...] = total[0:24]
    extra = total[24:32]
    for k, q in enumerate((q0, q1, q2, q3)):
        buf[n ^ k] = q[...].astype(F32)
    for m in range(4):
        block = buf[m]
        for part in range(3):
            at = part * 768 + m * 192
            gq[:, at : at + 192] = block[0:24, part * 192 : part * 192 + 192]
    tails = [buf[m][24:32] for m in range(4)]
    q_row = jnp.concatenate([t[:, 0:192] for t in tails], axis=1)
    v_row = jnp.concatenate([t[:, 384:576] for t in tails], axis=1)
    place = (w * 4 + n) * 24
    q_row = left(q_row, place, 768)[0:1, 0:24]
    v_row = left(v_row, place, 768)[0:1, 0:24]
    norm = left((tails[0] + tails[1] + tails[2] + tails[3])[:, 0:128], n * 24, 128)[:, 0:24]
    low, high, ffn = extra[:, 0:24], extra[:, 128:152], extra[:, 256:352]
    gains[0:1] = norm[1:2]
    gains[1:3] = low[1:3]
    biases[0:1] = norm[2:3]
    biases[1:2] = q_row
    biases[2:3] = v_row
    biases[3:5] = low[6:8]
    biases[5:7] = high[0:2]
    gffn[...] = ffn[0:1]
    bffn[...] = ffn[1:3]


def swap(values, axis, size, step):
    return lax.ppermute(values, axis, [(i, i ^ step) for i in range(size)])


def Y(v):
    return swap(v, "wide", 8, 1)


def Z1(v):
    return swap(v, "wide", 8, 2)


def Z2(v):
    return swap(v, "wide", 8, 4)


def C(v):
    return swap(v, "narrow", 4, 1)


def X(v):
    return swap(v, "narrow", 4, 2)


def XC(v):
    return swap(v, "narrow", 4, 3)


def fast_body(
    tokens, cotangent, w_qkv, w_attn, w_in, w_out, gains_model, biases_model, gain_ffn, biases_ffn,
    offsets,
):
    idx = jnp.stack([lax.axis_index("wide"), lax.axis_index("narrow")]).astype(jnp.int32)
    tokens, cotangent, w_out, b0, b1, b2, b3 = call(
        prep_kernel,
        [((128, 768), BF16), ((128, 768), BF16), ((96, 768), BF16)]
        + [((24, 2176 if k % 2 == 0 else 1408), BF16) for k in range(4)],
        idx, w_qkv, w_in, w_attn, gains_model, biases_model, gain_ffn[None], biases_ffn,
        tokens, cotangent, w_out,
        scratch=[((64, 128), F32), ((4, 24, 640), F32), ((4, 24, 768), F32)], held=False,
    )
    q_own, r_own = call(
        pack_kernel, [((96, 640), BF16), ((144, 768), BF16)], idx, b0, C(b1), X(b2), XC(b3),
        scratch=[((4, 24, 640), F32), ((4, 24, 768), F32), ((2, 24, 768), F32)],
    )
    cy = Y(after(w_out, q_own))
    qy = Y(q_own)
    q1 = Z1(q_own)
    q2 = Z2(q_own)
    r_own, tok, cy, qy, q1, q2 = lax.optimization_barrier((r_own, tokens, cy, qy, q1, q2))
    tx, tc = X(tok), C(tok)
    ry, q2y, q1y = Y(r_own), Y(q2), Y(q1)
    r1, q3 = Z1(r_own), Z1(q2)
    r2 = Z2(r_own)
    cot, c_own, tc, ry, q2y, q1y, r1, q3, tx, r2 = lax.optimization_barrier(
        (cotangent, w_out, tc, ry, q2y, q1y, r1, q3, tx, r2)
    )
    x = call(place_t_kernel, [((512, 768), BF16)], idx, tokens, tc, tx, C(tx))[0]
    n1 = call(norm_kernel, [((512, 768), F32)], x)[0]
    c2, c1 = Z2(c_own), Z1(c_own)
    r3 = Z1(r2)
    r2y, r1y = Y(r2), Y(r1)
    q3y = Y(q3)
    wqkv, params, a1, qkv, o_t, lse, o_low = call(
        attend_kernel,
        [
            ((768, 640), BF16), ((24, 768), F32), ((512, 768), BF16),
            ((512, 640), BF16), ((192, 512), F32), ((8, 512), F32), ((512, 192), BF16),
        ],
        idx, offsets, n1, q_own, qy, q1, q1y, q2, q2y, q3, q3y, us=4.0,
    )
    ox = X(o_low)
    r3, r1y, r2y, c2, c1, cot, _ = lax.optimization_barrier(
        (r3, r1y, r2y, c2, c1, cot, o_low)
    )
    gy_x = X(cot)
    c3 = Z1(c2)
    c2y, c1y = Y(c2), Y(c1)
    r3y = Z1(r2y)
    gy_x, c3, c2y, c1y, r3y, ox = lax.optimization_barrier((gy_x, c3, c2y, c1y, r3y, ox))
    c3y = Y(c3)
    gy = call(place_t_kernel, [((512, 768), BF16)], idx, cotangent, C(cot), gy_x, C(gy_x))[0]
    win, attn_own = call(
        place_i_kernel, [((768, 768), BF16), ((8, 48, 768), BF16)],
        idx, r_own, ry, r1, r1y, r2, r2y, r3, r3y,
    )
    wattn = call(
        place_a_kernel, [((768, 768), BF16)], idx, attn_own, C(attn_own),
        scratch=[((8, 4, 24, 768), F32)],
    )[0]
    n_o, rate_o, u, x2, h2, f, dg, stat_f = call(
        middle_kernel,
        [
            ((512, 768), F32), ((512, 1), F32), ((512, 768), BF16), ((512, 768), F32),
            ((512, 768), BF16), ((512, 768), F32), ((512, 768), F32), ((8, 512), F32),
        ],
        idx, x, params, o_low, C(o_low), ox, C(ox), wattn, win,
        scratch=[((4, 512, 192), F32)],
    )
    c3y = after(c3y, stat_f)
    wout = call(
        place_c_kernel, [((768, 768), BF16)], idx, c_own, cy, c1, c1y, c2, c2y, c3, c3y
    )[0]
    e = call(cot_kernel, [((512, 768), F32)], gy, wout)[0]
    stats = call(stat_kernel, [((8, 512), F32)], params, e, f, stat_f)[0]
    stat_all = (stats, C(stats), X(stats), XC(stats))
    gc, d_keep, d_send = call(
        ffn_back_kernel, [((512, 768), BF16), ((256, 768), F32), ((256, 768), BF16)],
        idx, params, *stat_all, f, dg, e, win, scratch=[((512, 768), F32)],
    )
    d_half = call(add_kernel, [((256, 768), BF16)], d_keep, C(d_send))[0]
    d_x = X(d_half)
    d_sib = C(d_half)
    two = ((2, 96, 768), BF16)
    z, out_ka, out_kb, out_sa, out_sb, sums = call(
        ffn_grad_kernel, [((512, 768), BF16), two, two, two, two, ((8, 768), F32)],
        idx, params, *stat_all, f, e, after(gy, d_half), scratch=[((768, 768), F32)],
    )
    in_ka, in_kb, in_sa, in_sb = call(
        in_grad_kernel, [two] * 4, idx, after(h2, d_half), gc, scratch=[((768, 768), F32)]
    )
    out_a, out_b = Y(out_sa), Y(out_sb)
    in_a, in_b = Z1(in_sa), Z1(in_sb)
    op_keep, op_send, sums = call(
        out_kernel, [((256, 768), F32), ((256, 768), BF16), ((8, 768), F32)],
        idx, z, wout, gc, gy, sums, scratch=[((512, 768), F32)],
    )
    p0, p1 = call(
        prob_kernel, [((3, 256, 256), F32), ((3, 512, 256), F32)], qkv, lse, us=1.5
    )
    n2, rate2 = call(norm_two_kernel, [((512, 768), F32), ((512, 1), F32)], x2)
    d_x, out_a, in_a, _ = lax.optimization_barrier((d_x, out_a, in_a, (op_send, p0, n2)))
    dx2, ga, do, e2, eo = call(
        mid_back_kernel,
        [
            ((512, 768), F32), ((512, 768), BF16), ((512, 192), BF16), ((512, 768), F32),
            ((512, 768), F32),
        ],
        idx, params, d_half, d_x, d_sib, C(d_x), n2, rate2, gy, n_o, rate_o, wattn,
    )
    keep_a, keep_b, qkv_a, qkv_b, t_keep, t_send = call(
        head_back_kernel,
        [
            ((2, 104, 640), BF16), ((2, 104, 640), BF16), ((2, 104, 640), BF16),
            ((2, 104, 640), BF16),
            ((256, 768), F32), ((256, 768), BF16),
        ],
        idx, offsets, qkv, o_t, p0, p1, do, a1, wqkv, n1,
        scratch=[((512, 768), F32), ((768, 640), F32)],
    )
    in_b, out_b, qkv_b, qkv_a = lax.optimization_barrier((in_b, out_b, qkv_b, qkv_a))
    out_on = call(pair_kernel, [two], out_ka, out_a)[0]
    in_on = call(pair_kernel, [two], in_ka, in_a)[0]
    a_got, b_got = Y(qkv_a), Y(qkv_b)
    out_z = Z1(out_on)
    in_z = Z2(in_on)
    out_own = call(pair_kernel, [((2, 96, 768), F32)], out_kb, out_b)[0]
    in_own = call(pair_kernel, [((2, 96, 768), F32)], in_kb, in_b)[0]
    at_keep, at_send = call(
        attn_grad_kernel, [((4, 32, 768), BF16), ((4, 32, 768), BF16)],
        idx, u, ga, eo, n_o, e2, n2, after(sums, qkv_a), scratch=[((8, 4, 24, 768), F32)],
    )
    at_y = Y(after(at_send, a_got))
    qkv_z = Z1(call(pair_kernel, [((2, 104, 640), BF16)], keep_a, a_got)[0])
    out_mine, out_on = call(
        last_hop_kernel, [((96, 768), F32), ((96, 768), BF16)], out_own, out_z
    )
    out_got = Z2(out_on)
    tail_keep, tail_send = call(
        tail_add_kernel, [((128, 1536), F32), ((128, 1536), BF16)],
        idx, op_keep, C(op_send), t_keep, C(t_send), scratch=[((256, 1536), F32)],
    )
    tail_got = X(tail_send)
    tail_got, at_y, qkv_z, in_z, in_own, b_got, out_mine = lax.optimization_barrier(
        (tail_got, at_y, qkv_z, in_z, in_own, b_got, out_mine)
    )
    own = call(pair_kernel, [((2, 104, 640), F32)], keep_b, b_got)[0]
    qkv_mine, on = call(last_hop_kernel, [((104, 640), F32), ((104, 640), BF16)], own, qkv_z)
    qkv_got = Z2(on)
    in_mine, on = call(last_hop_kernel, [((96, 768), F32), ((96, 768), BF16)], in_own, in_z)
    in_got = Y(on)
    at_own, on = call(
        hop_kernel, [((2, 32, 768), F32), ((2, 32, 768), BF16)], at_keep, at_y
    )
    at_mine, on = call(
        last_hop_kernel, [((32, 768), F32), ((32, 768), BF16)], at_own, Z1(on)
    )
    at_got = Z2(on)
    outputs, grad_inputs = call(
        token_kernel, [((128, 768), BF16), ((128, 768), F32)],
        idx, params, tail_keep, tail_got, tokens, x2, dx2, final=True,
    )
    grad_w_out = call(sum_out_kernel, [((96, 768), F32)], out_mine, out_got, final=True)[0]
    i_own, i1, i2, i3 = call(
        sum_in_kernel, [((24, 768), F32)] + [((24, 768), BF16)] * 3,
        idx, in_mine, in_got, scratch=[((4, 24, 768), F32)],
    )
    grad_w_in = call(
        final_in_kernel, [((24, 3072), F32)], idx, i_own, C(i1), X(i2), XC(i3),
        scratch=[((4, 24, 768), F32)], final=True,
    )[0]
    qkv_got, outputs, grad_w_in, grad_w_out = lax.optimization_barrier(
        (qkv_got, outputs, grad_w_in, grad_w_out)
    )
    q_mine, q1, q2, q3 = call(
        sum_qkv_kernel, [((32, 640), F32)] + [((32, 640), BF16)] * 3, idx, qkv_mine, qkv_got,
        scratch=[((4, 24, 640), F32)],
    )
    grad_w_qkv, grad_w_attn, grad_gains, grad_biases, grad_gain_ffn, grad_ffn_biases = call(
        final_kernel,
        [
            ((24, 2304), F32), ((24, 768), F32), ((3, 24), F32), ((7, 24), F32), ((1, 96), F32),
            ((2, 96), F32),
        ],
        idx, q_mine, C(q1), X(q2), XC(q3), at_mine, at_got, scratch=[((4, 32, 640), F32)],
        final=True,
    )
    return (
        outputs, grad_inputs, grad_w_qkv, grad_w_attn, grad_w_in, grad_w_out, grad_gains,
        grad_biases, grad_gain_ffn[0], grad_ffn_biases,
    )


def solution(mesh):
    fast = dict(mesh.shape) == {"wide": 8, "narrow": 4}
    return jax.shard_map(
        fast_body if fast else body,
        mesh=mesh,
        in_specs=(
            P(("wide", "narrow"), None),
            P(("wide", "narrow"), None),
            P(("wide", "narrow"), None),
            P(("wide", "narrow"), None),
            P(("wide", "narrow"), None),
            P(("wide", "narrow"), None),
            P(None, ("wide", "narrow")),
            P(None, ("wide", "narrow")),
            P(("wide", "narrow")),
            P(None, ("wide", "narrow")),
            P(),
        ),
        out_specs=(
            P(("wide", "narrow"), None),
            P(("wide", "narrow"), None),
            P(("wide", "narrow"), None),
            P(("wide", "narrow"), None),
            P(("wide", "narrow"), None),
            P(("wide", "narrow"), None),
            P(None, ("wide", "narrow")),
            P(None, ("wide", "narrow")),
            P(("wide", "narrow")),
            P(None, ("wide", "narrow")),
        ),
        check_vma=False,
    )
```

```python
import jax
import jax.numpy as jnp
from jax import lax
from jax.experimental import pallas as pl
from jax.experimental.pallas import tpu as pltpu
from jax.sharding import PartitionSpec as P

HEADS = 12
HEAD_DIM = 64
RATE0 = 1
RATE1 = 2
RATE2 = 4


EPSILON = 1e-05
SCORE_SCALE = 0.125
MASKED = -1e30


def layer_norm(values, norm_gain, norm_shift):
    average = jnp.mean(values, axis=-1, keepdims=True)
    centred = values - average
    spread = jnp.mean(centred * centred, axis=-1, keepdims=True)
    return centred * lax.rsqrt(spread + EPSILON) * norm_gain + norm_shift


def gelu_exact(values):
    return jax.nn.gelu(values, approximate=False)


def product(former, latter):
    return jnp.dot(former, latter, preferred_element_type=jnp.float32)


def product_tn(former, latter):
    return lax.dot_general(
        former, latter, (((0,), (0,)), ((), ())), preferred_element_type=jnp.float32
    )


def product_nt(former, latter):
    return lax.dot_general(
        former, latter, (((1,), (1,)), ((), ())), preferred_element_type=jnp.float32
    )


def one_hot(offset_row, dilation):
    return (jnp.arange(dilation)[:, None] == offset_row[None, :]).astype(jnp.float32)


def select_rows(dense_rows, selector, dilation):
    picked_rows = dense_rows.shape[0] // dilation
    shaped = dense_rows.reshape(picked_rows, dilation, HEADS, HEAD_DIM)
    picked = jnp.einsum(
        "trhd,rh->thd",
        shaped,
        selector.astype(dense_rows.dtype),
        preferred_element_type=jnp.float32,
    )
    return picked.reshape(picked_rows, HEADS * HEAD_DIM)


def spread_rows(sparse_rows, selector, dilation):
    shaped = sparse_rows.reshape(sparse_rows.shape[0], 1, HEADS, HEAD_DIM)
    placed = shaped * selector[None, :, :, None]
    return placed.reshape(sparse_rows.shape[0] * dilation, HEADS * HEAD_DIM)


def select_heads(dense_heads, selector, dilation):
    shaped = dense_heads.reshape(dense_heads.shape[0] // dilation, dilation, HEADS)
    return jnp.sum(shaped * selector[None], axis=1)


def spread_heads(sparse_heads, selector, dilation):
    placed = jnp.where(selector[None] > 0, sparse_heads[:, None, :], MASKED)
    return placed.reshape(sparse_heads.shape[0] * dilation, HEADS)


def head_major(values):
    return values.reshape(values.shape[0], HEADS, HEAD_DIM).transpose(1, 0, 2)


def row_major(values):
    return values.transpose(1, 0, 2).reshape(values.shape[1], HEADS * HEAD_DIM)


def key_mask(row_count, block_count, own_block):
    query_pos = jnp.arange(row_count)[:, None]
    position = jnp.arange(row_count * block_count)[None, :]
    key_block = position // row_count
    within = position % row_count
    return (key_block < own_block) | (key_block == own_block) & (within <= query_pos)


def masked_scores(head_query, head_keys, allowed):
    return jnp.where(allowed, product_nt(head_query, head_keys) * SCORE_SCALE, MASKED)


def pattern_lse(queries, keys, allowed):

    def one_head(operands):
        scores = masked_scores(operands[0], operands[1], allowed)
        peak_rows = jnp.max(scores, axis=1, keepdims=True)
        return peak_rows[:, 0] + jnp.log(jnp.sum(jnp.exp(scores - peak_rows), axis=1))

    return lax.map(one_head, (head_major(queries), head_major(keys))).T


def pattern_out(queries, keys, values, allowed, totals):

    def one_head(operands):
        head_query, head_keys, head_values, head_total = operands
        scores = masked_scores(head_query, head_keys, allowed)
        probability = jnp.where(allowed, jnp.exp(scores - head_total[:, None]), 0.0).astype(
            jnp.bfloat16
        )
        return product(probability, head_values)

    return row_major(
        lax.map(one_head, (head_major(queries), head_major(keys), head_major(values), totals.T))
    )


def pattern_back(queries, keys, values, allowed, totals, deltas, grad_out):

    def one_head(operands):
        head_query, head_keys, head_values, head_total, head_delta, head_grad = operands
        scores = masked_scores(head_query, head_keys, allowed)
        probability = jnp.where(allowed, jnp.exp(scores - head_total[:, None]), 0.0)
        grad_probs = product_nt(head_grad, head_values)
        grad_scores = (probability * (grad_probs - head_delta[:, None])).astype(jnp.bfloat16)
        grad_query = product(grad_scores, head_keys) * SCORE_SCALE
        grad_keys = product_tn(grad_scores, head_query) * SCORE_SCALE
        grad_values = product_tn(probability.astype(jnp.bfloat16), head_grad)
        return (grad_query, grad_keys, grad_values)

    results = lax.map(
        one_head,
        (
            head_major(queries),
            head_major(keys),
            head_major(values),
            totals.T,
            deltas.T,
            head_major(grad_out),
        ),
    )
    return (row_major(results[0]), row_major(results[1]), row_major(results[2]))


def body(
    tokens,
    cotangent,
    w_qkv,
    w_attn,
    w_in,
    w_out,
    gains_model,
    biases_model,
    gain_ffn,
    biases_ffn,
    offsets,
):
    gathered = (
        lax.all_gather(w_qkv, ("wide", "narrow"), axis=0, tiled=True),
        lax.all_gather(w_attn, ("wide", "narrow"), axis=0, tiled=True),
        lax.all_gather(w_in, ("wide", "narrow"), axis=0, tiled=True),
        lax.all_gather(w_out, ("wide", "narrow"), axis=0, tiled=True),
        lax.all_gather(gains_model, ("wide", "narrow"), axis=1, tiled=True),
        lax.all_gather(biases_model, ("wide", "narrow"), axis=1, tiled=True),
        lax.all_gather(gain_ffn, ("wide", "narrow"), axis=0, tiled=True),
        lax.all_gather(biases_ffn, ("wide", "narrow"), axis=1, tiled=True),
    )
    qkv_full, attn_full, in_full, out_full = (gathered[0], gathered[1], gathered[2], gathered[3])
    model_gains = gathered[4].astype(jnp.float32)
    model_biases = gathered[5].astype(jnp.float32)
    ffn_gain = gathered[6].astype(jnp.float32)
    ffn_biases = gathered[7].astype(jnp.float32)
    local_rows = tokens.shape[0]
    width = tokens.shape[1]
    inputs = tokens.astype(jnp.float32)
    normed_one, pull_one = jax.vjp(layer_norm, inputs, model_gains[0], model_biases[0])
    normed_low = normed_one.astype(jnp.bfloat16)
    projected = product(normed_low, qkv_full)
    queries = (projected[:, :width] + model_biases[1]).astype(jnp.bfloat16)
    keys = projected[:, width : 2 * width].astype(jnp.bfloat16)
    values = (projected[:, 2 * width :] + model_biases[2]).astype(jnp.bfloat16)
    size_narrow = lax.axis_size("narrow")
    narrow_place = lax.axis_index("narrow")
    dilations = (RATE0, RATE1, RATE2)
    selectors = (one_hot(offsets[0], RATE0), one_hot(offsets[1], RATE1), one_hot(offsets[2], RATE2))
    picked_q = [
        select_rows(queries, selectors[pattern], dilations[pattern]).astype(jnp.bfloat16)
        for pattern in range(3)
    ]
    picked_k = [
        select_rows(keys, selectors[pattern], dilations[pattern]).astype(jnp.bfloat16)
        for pattern in range(3)
    ]
    picked_v = [
        select_rows(values, selectors[pattern], dilations[pattern]).astype(jnp.bfloat16)
        for pattern in range(3)
    ]
    arrived = (
        lax.all_gather(picked_k[0], "narrow", axis=0, tiled=True),
        lax.all_gather(picked_v[0], "narrow", axis=0, tiled=True),
        lax.all_gather(picked_k[1], "narrow", axis=0, tiled=True),
        lax.all_gather(picked_v[1], "narrow", axis=0, tiled=True),
        lax.all_gather(picked_k[2], "narrow", axis=0, tiled=True),
        lax.all_gather(picked_v[2], "narrow", axis=0, tiled=True),
    )
    key_sets = (arrived[0], arrived[2], arrived[4])
    value_sets = (arrived[1], arrived[3], arrived[5])
    allowed_sets = tuple(
        (
            key_mask(local_rows // dilations[pattern], size_narrow, narrow_place)
            for pattern in range(3)
        )
    )
    partial_value = jnp.stack(
        [
            spread_heads(
                pattern_lse(picked_q[pattern], key_sets[pattern], allowed_sets[pattern]),
                selectors[pattern],
                dilations[pattern],
            )
            for pattern in range(3)
        ]
    )
    peak_rows = jnp.max(partial_value, axis=0)
    totals = peak_rows + jnp.log(jnp.sum(jnp.exp(partial_value - peak_rows), axis=0))
    attended = jnp.zeros((local_rows, width), jnp.float32)
    for pattern in range(3):
        pattern_totals = select_heads(totals, selectors[pattern], dilations[pattern])
        result_rows = pattern_out(
            picked_q[pattern],
            key_sets[pattern],
            value_sets[pattern],
            allowed_sets[pattern],
            pattern_totals,
        )
        attended = attended + spread_rows(result_rows, selectors[pattern], dilations[pattern])
    sub_normed, pull_sub = jax.vjp(layer_norm, attended, model_gains[1], model_biases[3])
    sub_low = sub_normed.astype(jnp.bfloat16)
    middle = inputs + product(sub_low, attn_full) + model_biases[4]
    normed_two, pull_two = jax.vjp(layer_norm, middle, model_gains[2], model_biases[5])
    normed_two_low = normed_two.astype(jnp.bfloat16)
    pre_act = product(normed_two_low, in_full) + ffn_biases[0]
    activated, pull_gelu = jax.vjp(gelu_exact, pre_act)
    ffn_normed, pull_ffn = jax.vjp(layer_norm, activated, ffn_gain, ffn_biases[1])
    ffn_low = ffn_normed.astype(jnp.bfloat16)
    outputs = (middle + product(ffn_low, out_full) + model_biases[6]).astype(jnp.bfloat16)
    regathered = (
        lax.all_gather(w_qkv, ("wide", "narrow"), axis=0, tiled=True),
        lax.all_gather(w_attn, ("wide", "narrow"), axis=0, tiled=True),
        lax.all_gather(w_in, ("wide", "narrow"), axis=0, tiled=True),
        lax.all_gather(w_out, ("wide", "narrow"), axis=0, tiled=True),
    )
    qkv_back, attn_back, in_back, out_back = (
        regathered[0],
        regathered[1],
        regathered[2],
        regathered[3],
    )
    grad_out_f = cotangent.astype(jnp.float32)
    grad_w_out = product_tn(ffn_low, cotangent)
    grad_bias_ffo = jnp.sum(cotangent.astype(jnp.float32), axis=0)
    grad_act, grad_gain_ffn, grad_bias_ffn_norm = pull_ffn(product_nt(cotangent, out_back))
    grad_pre = pull_gelu(grad_act)[0].astype(jnp.bfloat16)
    grad_w_in = product_tn(normed_two_low, grad_pre)
    grad_bias_pre = jnp.sum(grad_pre.astype(jnp.float32), axis=0)
    grad_mid_norm, grad_gain_two, grad_bias_two = pull_two(product_nt(grad_pre, in_back))
    grad_middle = grad_out_f + grad_mid_norm
    grad_branch = grad_middle.astype(jnp.bfloat16)
    grad_w_attn = product_tn(sub_low, grad_branch)
    grad_bias_branch = jnp.sum(grad_branch.astype(jnp.float32), axis=0)
    grad_att, grad_gain_sub, grad_bias_sub = pull_sub(product_nt(grad_branch, attn_back))
    grad_att_low = grad_att.astype(jnp.bfloat16)
    deltas = jnp.sum(
        (grad_att_low.astype(jnp.float32) * attended).reshape(local_rows, HEADS, HEAD_DIM), axis=2
    )
    backward_parts = []
    for pattern in range(3):
        backward_parts.append(
            pattern_back(
                picked_q[pattern],
                key_sets[pattern],
                value_sets[pattern],
                allowed_sets[pattern],
                select_heads(totals, selectors[pattern], dilations[pattern]),
                select_heads(deltas, selectors[pattern], dilations[pattern]),
                select_rows(grad_att_low, selectors[pattern], dilations[pattern]).astype(
                    jnp.bfloat16
                ),
            )
        )
    returned = (
        lax.psum_scatter(
            backward_parts[0][1].astype(jnp.bfloat16), "narrow", scatter_dimension=0, tiled=True
        ).astype(jnp.float32),
        lax.psum_scatter(
            backward_parts[0][2].astype(jnp.bfloat16), "narrow", scatter_dimension=0, tiled=True
        ).astype(jnp.float32),
        lax.psum_scatter(
            backward_parts[1][1].astype(jnp.bfloat16), "narrow", scatter_dimension=0, tiled=True
        ).astype(jnp.float32),
        lax.psum_scatter(
            backward_parts[1][2].astype(jnp.bfloat16), "narrow", scatter_dimension=0, tiled=True
        ).astype(jnp.float32),
        lax.psum_scatter(
            backward_parts[2][1].astype(jnp.bfloat16), "narrow", scatter_dimension=0, tiled=True
        ).astype(jnp.float32),
        lax.psum_scatter(
            backward_parts[2][2].astype(jnp.bfloat16), "narrow", scatter_dimension=0, tiled=True
        ).astype(jnp.float32),
    )
    key_grads = (returned[0], returned[2], returned[4])
    value_grads = (returned[1], returned[3], returned[5])
    grad_q = jnp.zeros((local_rows, width), jnp.float32)
    grad_k = jnp.zeros((local_rows, width), jnp.float32)
    grad_v = jnp.zeros((local_rows, width), jnp.float32)
    for pattern in range(3):
        grad_q = grad_q + spread_rows(
            backward_parts[pattern][0], selectors[pattern], dilations[pattern]
        )
        grad_k = grad_k + spread_rows(key_grads[pattern], selectors[pattern], dilations[pattern])
        grad_v = grad_v + spread_rows(value_grads[pattern], selectors[pattern], dilations[pattern])
    grad_q_low = grad_q.astype(jnp.bfloat16)
    grad_v_low = grad_v.astype(jnp.bfloat16)
    grad_qkv = jnp.concatenate([grad_q_low, grad_k.astype(jnp.bfloat16), grad_v_low], axis=1)
    grad_w_qkv = product_tn(normed_low, grad_qkv)
    grad_bias_q = jnp.sum(grad_q_low.astype(jnp.float32), axis=0)
    grad_bias_v = jnp.sum(grad_v_low.astype(jnp.float32), axis=0)
    grad_first, grad_gain_one, grad_bias_one = pull_one(product_nt(grad_qkv, qkv_back))
    grad_inputs = grad_middle + grad_first
    grad_gains = jnp.stack([grad_gain_one, grad_gain_sub, grad_gain_two])
    grad_biases = jnp.stack(
        [
            grad_bias_one,
            grad_bias_q,
            grad_bias_v,
            grad_bias_sub,
            grad_bias_branch,
            grad_bias_two,
            grad_bias_ffo,
        ]
    )
    grad_ffn_biases = jnp.stack([grad_bias_pre, grad_bias_ffn_norm])
    reduced = (
        lax.psum_scatter(grad_w_qkv, ("wide", "narrow"), scatter_dimension=0, tiled=True),
        lax.psum_scatter(grad_w_attn, ("wide", "narrow"), scatter_dimension=0, tiled=True),
        lax.psum_scatter(grad_w_in, ("wide", "narrow"), scatter_dimension=0, tiled=True),
        lax.psum_scatter(grad_w_out, ("wide", "narrow"), scatter_dimension=0, tiled=True),
        lax.psum_scatter(grad_gains, ("wide", "narrow"), scatter_dimension=1, tiled=True),
        lax.psum_scatter(grad_biases, ("wide", "narrow"), scatter_dimension=1, tiled=True),
        lax.psum_scatter(grad_gain_ffn, ("wide", "narrow"), scatter_dimension=0, tiled=True),
        lax.psum_scatter(grad_ffn_biases, ("wide", "narrow"), scatter_dimension=1, tiled=True),
    )
    return (
        outputs,
        grad_inputs,
        reduced[0],
        reduced[1],
        reduced[2],
        reduced[3],
        reduced[4],
        reduced[5],
        reduced[6],
        reduced[7],
    )


BF16 = jnp.bfloat16
F32 = jnp.float32
ALPHA = (
    -2.72614225801306e-10,
    2.77068142495902e-08,
    -2.10102402082508e-06,
    -5.69250639462346e-05,
    -7.34990630326855e-04,
    -2.95459980854025e-03,
    -1.60960333262415e-02,
)
BETA = (
    -1.45660718464996e-05,
    -2.13374055278905e-04,
    -1.68282697438203e-03,
    -7.37332916720468e-03,
    -1.42647390514189e-02,
)


def nn(a, b):
    return lax.dot_general(a, b, (((1,), (0,)), ((), ())), preferred_element_type=F32)


def nt(a, b):
    return lax.dot_general(a, b, (((1,), (1,)), ((), ())), preferred_element_type=F32)


def tn(a, b):
    return lax.dot_general(a, b, (((0,), (0,)), ((), ())), preferred_element_type=F32)


def erf(v):
    v = jnp.clip(v, -4.0, 4.0)
    s = v * v
    top = jnp.full_like(s, ALPHA[0])
    for term in ALPHA[1:]:
        top = top * s + term
    low = jnp.full_like(s, BETA[0])
    for term in BETA[1:]:
        low = low * s + term
    return v * top / low


def normed(v):
    centred = v - jnp.mean(v, axis=-1, keepdims=True)
    rate = lax.rsqrt(jnp.mean(centred * centred, axis=-1, keepdims=True) + EPSILON)
    return centred * rate, rate


def norm_back(e, n, rate, gain):
    t = e * gain
    return rate * (
        t - jnp.mean(t, axis=-1, keepdims=True) - n * jnp.mean(t * n, axis=-1, keepdims=True)
    )


def colsum(v):
    return jnp.sum(v, axis=0, keepdims=True)


def lanes(shape):
    return lax.broadcasted_iota(jnp.int32, shape, len(shape) - 1)


def sublanes(shape):
    return lax.broadcasted_iota(jnp.int32, shape, len(shape) - 2)


def rows_of(parts, count):
    shape = (count, next(part for part in parts if part is not None).shape[1])
    at = sublanes(shape)
    out = jnp.zeros(shape, F32)
    for i, part in enumerate(parts):
        if part is not None:
            out = jnp.where(at == i, part, out)
    return out


def to_rows(columns):
    shape = (columns[0].shape[0], 128)
    at = lanes(shape)
    out = jnp.zeros(shape, F32)
    for i, column in enumerate(columns):
        out = jnp.where(at == i, column, out)
    return out.T[0:8]


def to_columns(rows):
    wide = rows_of(rows, 128).T
    return [wide[:, i : i + 1] for i in range(len(rows))]


def left(v, amount, width):
    return pltpu.roll(v, lax.rem(width - amount, width), 1)


class Place:
    def __getitem__(self, axis):
        return lax.axis_index(("wide", "narrow")[axis])


def call(kernel, outs, *operands, scratch=(), limit=24, final=False, held=True, us=0.0, alias=None):
    whole = pl.BlockSpec(memory_space=pltpu.VMEM)
    space = pltpu.VMEM if held else pltpu.HBM
    placed = [pltpu.with_memory_space_constraint(a, space) for a in operands]
    return pl.pallas_call(
        kernel,
        out_shape=[jax.ShapeDtypeStruct(s, d) if final else pltpu.VMEM(s, d) for s, d in outs],
        in_specs=[whole for _ in operands],
        out_specs=[whole for _ in outs],
        scratch_shapes=[pltpu.VMEM(s, d) for s, d in scratch],
        compiler_params=pltpu.CompilerParams(vmem_limit_bytes=limit << 20),
        cost_estimate=pl.CostEstimate(
            flops=int(us * 1e9), transcendentals=0, bytes_accessed=int(us * 3.6e6)
        ),
        input_output_aliases=alias or {},
        name=kernel.__name__,
    )(*placed)


def offset_of(off, pattern, head):
    row = off[pattern : pattern + 1, :].astype(F32)
    return jnp.sum(jnp.where(lanes(row.shape) == head, row, 0.0), axis=1, keepdims=True)


def after(value, *others):
    return lax.optimization_barrier((value, *others))[0]


def prep_kernel(
    wqkv, win, wattn, gains, biases, gffn, bffn, tok, cot, wout, tok_out, cot_out, wout_out,
    b0, b1, b2, b3, small, qs, is_,
):
    idx = Place()
    n = idx[1]
    tok_out[...] = tok[...]
    cot_out[...] = cot[...]
    wout_out[...] = wout[...]
    small[...] = jnp.zeros_like(small)
    small[0:3, 0:24] = gains[...].astype(F32)
    small[3:10, 0:24] = biases[...].astype(F32)
    ffn_g = gffn[...].astype(F32)
    ffn_b = bffn[...].astype(F32)
    for k in range(4):
        small[16 + 8 * k : 17 + 8 * k, 0:24] = ffn_g[:, k * 24 : k * 24 + 24]
        small[17 + 8 * k : 19 + 8 * k, 0:24] = ffn_b[:, k * 24 : k * 24 + 24]
    eye = (sublanes((24, 128)) == lanes((24, 128))).astype(BF16)
    params = nt(eye, small[...].astype(BF16))
    weights = wqkv[...].astype(F32)
    for m in range(4):
        for part in range(3):
            at = part * 768 + m * 192
            qs[m, :, part * 192 : part * 192 + 192] = weights[:, at : at + 192]
        qs[m, :, 576:640] = params
    inner = win[...].astype(F32)
    for m in range(4):
        for w in range(8):
            at = (w * 4 + m) * 96
            is_[m, :, w * 96 : w * 96 + 96] = inner[:, at : at + 96]
    for k, out in enumerate((b0, b1, b2, b3)):
        out[:, 0:640] = qs[n ^ k].astype(BF16)
        out[:, 640:1408] = is_[n ^ k].astype(BF16)
        if k % 2 == 0:
            out[:, 1408:2176] = wattn[...]


def pack_kernel(b0, b1, b2, b3, q_out, r_out, qs, is_, two):
    idx = Place()
    n = idx[1]
    for k, b in enumerate((b0, b1, b2, b3)):
        qs[n ^ k] = b[:, 0:640].astype(F32)
        is_[n ^ k] = b[:, 640:1408].astype(F32)
        if k % 2 == 0:
            two[(n ^ k) // 2] = b[:, 1408:2176].astype(F32)
    q_out[...] = qs[...].reshape(96, 640).astype(BF16)
    r_out[0:96] = is_[...].reshape(96, 768).astype(BF16)
    r_out[96:144] = two[...].reshape(48, 768).astype(BF16)


def place_i_kernel(r0, r1, r2, r3, r4, r5, r6, win, attn):
    idx = Place()
    w = idx[0]
    for j, r in enumerate((r0, r1, r2, r3, r4, r5, r6)):
        win[pl.ds(pl.multiple_of((w ^ j) * 96, 32), 96), :] = r[0:96]
        attn[j] = r[96:144]


def merge_cores(mine, other, core, buf):
    for x_ in range(2):
        buf[x_ * 2 + core] = mine[x_ * 24 : x_ * 24 + 24].astype(F32)
        buf[x_ * 2 + 1 - core] = other[x_ * 24 : x_ * 24 + 24].astype(F32)
    return buf[...].reshape(96, 768).astype(BF16)


def place_a_kernel(mine, other, wattn, buf):
    idx = Place()
    w, core = idx[0], lax.rem(idx[1], 2)
    for j in range(7):
        block = merge_cores(mine[j], other[j], core, buf)
        wattn[pl.ds(pl.multiple_of((w ^ j) * 96, 32), 96), :] = block


def place_last_kernel(win_in, wattn_in, mine, other, win, wattn, buf):
    idx = Place()
    here = pl.ds(pl.multiple_of((idx[0] ^ 7) * 96, 32), 96)
    win[here, :] = mine[0:96]
    block = merge_cores(mine[96:144], other[96:144], lax.rem(idx[1], 2), buf)
    wattn[here, :] = block


def place_c_kernel(r0, r1, r2, r3, r4, r5, r6, wout):
    idx = Place()
    w = idx[0]
    for j, r in enumerate((r0, r1, r2, r3, r4, r5, r6)):
        wout[pl.ds(pl.multiple_of((w ^ j) * 96, 32), 96), :] = r[...]


def place_c_last_kernel(wout_in, block, wout):
    idx = Place()
    wout[pl.ds(pl.multiple_of((idx[0] ^ 7) * 96, 32), 96), :] = block[...]


def place_t_kernel(t0, t1, t2, t3, out):
    idx = Place()
    n = idx[1]
    for k, t in enumerate((t0, t1, t2, t3)):
        out[pl.ds(pl.multiple_of((n ^ k) * 128, 128), 128), :] = t[...]


def norm_kernel(x, n_out):
    n_out[...], _ = normed(x[...].astype(F32))


def attend_kernel(
    off, n1, q0, q1, q2, q3, q4, q5, q6, q7,
    w_out, p_out, a_out, qkv_out, o_t_out, lse_out, o_out,
):
    idx = Place()
    w, n = idx[0], idx[1]
    for j, q in enumerate((q0, q1, q2, q3, q4, q5, q6, q7)):
        w_out[pl.ds(pl.multiple_of((w ^ j) * 96, 32), 96), :] = q[...]
    pick = (sublanes((64, 128)) + 64 == lanes((64, 128))).astype(BF16)
    table = nt(pick, w_out[:, 512:640])
    model = table[0:16]
    ffn = jnp.zeros((8, 768), F32)
    inside = lax.rem(lanes((8, 768)), 96) // 24
    for k in range(4):
        turned = pltpu.roll(table[16 + 8 * k : 24 + 8 * k], lax.rem(768 + (k - n) * 24, 768), 1)
        ffn = jnp.where(inside == k, turned, ffn)
    p_out[0:16] = model
    p_out[16:24] = ffn
    a1 = (n1[...] * model[0:1] + model[3:4]).astype(BF16)
    a_out[...] = a1
    qkv = nn(a1, w_out[...])
    lane = lanes((8, 768))
    bias_q = left(jnp.broadcast_to(model[4:5], (8, 768)), n * 192, 768)
    bias_v = pltpu.roll(
        jnp.broadcast_to(model[5:6], (8, 768)), lax.rem(768 + 384 - n * 192, 768), 1
    )
    bias = jnp.where(
        lane < 192, bias_q, jnp.where((lane >= 384) & (lane < 576), bias_v, 0.0)
    )[0:1, 0:640]
    qkv = jnp.where(lanes((1, 640)) < 576, qkv + bias, 0.0).astype(BF16)
    qkv_out[...] = qkv
    v_t = qkv[:, 384:576].astype(F32).T
    o_parts, lse_rows = [], []
    for h in range(3):
        head = n * 3 + h
        o1, o2 = offset_of(off, 1, head), offset_of(off, 2, head)
        at = lanes((1, 512))
        r1 = (lax.rem(at, 2).astype(F32) == o1).astype(F32)
        r2 = (lax.rem(at, 4).astype(F32) == o2).astype(F32)
        head_v = v_t[h * 64 : h * 64 + 64]
        ones = rows_of([jnp.ones((1, 512), F32), r1, r2], 8)
        left_side = jnp.concatenate([head_v, head_v * r1, head_v * r2, ones], axis=0).astype(BF16)
        head_q = qkv[:, h * 64 : h * 64 + 64] * jnp.asarray(SCORE_SCALE, BF16)
        head_k = qkv[:, 192 + h * 64 : 256 + h * 64]
        blocks, lses = [], []
        for i in range(2):
            keys = 256 * (i + 1)
            scores = nt(head_k[0:keys], head_q[i * 256 : i * 256 + 256])
            shape = (keys, 256)
            scores = jnp.where(sublanes(shape) <= lanes(shape) + i * 256, scores, MASKED)
            peak = jnp.max(scores, axis=0, keepdims=True)
            weight = jnp.exp(scores - peak).astype(BF16)
            both = nn(left_side[:, 0:keys], weight)
            s1, s2 = r1[:, i * 256 : i * 256 + 256], r2[:, i * 256 : i * 256 + 256]
            total = both[192:193] + s1 * both[193:194] + s2 * both[194:195]
            blocks.append((both[0:64] + s1 * both[64:128] + s2 * both[128:192]) / total)
            lses.append(peak + jnp.log(total))
        o_parts.append(jnp.concatenate(blocks, axis=1))
        lse_rows.append(jnp.concatenate(lses, axis=1))
    o_t = jnp.concatenate(o_parts, axis=0)
    o_t_out[...] = o_t
    lse_out[...] = rows_of(lse_rows, 8)
    o_out[...] = o_t.T.astype(BF16)


def sub_norm_kernel(p, o0, o1, o2, o3, n_o_out, rate_o_out, u_out, o_buf):
    idx = Place()
    n = idx[1]
    for k, o in enumerate((o0, o1, o2, o3)):
        o_buf[n ^ k] = o[...].astype(F32)
    o = jnp.concatenate([o_buf[m] for m in range(4)], axis=1)
    n_o, rate_o = normed(o)
    n_o_out[...] = n_o
    rate_o_out[...] = rate_o
    u_out[...] = (n_o * p[1:2] + p[6:7]).astype(BF16)


def middle_kernel(x, p, u, wattn, win, x2_out, h2_out, f_out, dg_out, stat_out):
    x2 = x[...].astype(F32) + nn(u[...], wattn[...]) + p[7:8]
    x2_out[...] = x2
    n2, _ = normed(x2)
    h2 = (n2 * p[2:3] + p[8:9]).astype(BF16)
    h2_out[...] = h2
    c = nn(h2, win[...]) + p[17:18]
    half = 0.5 + 0.5 * erf(c * 0.7071067811865476)
    f = c * half
    f_out[...] = f
    dg_out[...] = half + c * jnp.exp(c * c * -0.5) * 0.3989422804014327
    mean = jnp.mean(f, axis=1, keepdims=True)
    centred = f - mean
    stat_out[...] = to_rows([mean, jnp.sum(centred * centred, axis=1, keepdims=True)])


def cot_kernel(gy, wout, p, f, stat_in, e_out, stat_out):
    e = nt(gy[...], wout[...])
    e_out[...] = e
    t = e * p[16:17]
    mean = to_columns([stat_in[0:1]])[0]
    rows = to_rows(
        [jnp.sum(t, axis=1, keepdims=True), jnp.sum(t * (f[...] - mean), axis=1, keepdims=True)]
    )
    stat_out[...] = jnp.where(sublanes((8, 512)) < 2, stat_in[...], jnp.roll(rows, 2, axis=0))


def ffn_columns(s0, s1, s2, s3):
    parts = [s[...] for s in (s0, s1, s2, s3)]
    count = 768.0 * 4
    mean = sum(s[0:1] for s in parts) * 0.25
    spread = sum(s[1:2] + 768.0 * (s[0:1] - mean) * (s[0:1] - mean) for s in parts) / count
    rate = lax.rsqrt(spread + EPSILON)
    mean_t = sum(s[2:3] for s in parts) / count
    mean_tn = rate * sum(s[3:4] + (s[0:1] - mean) * s[2:3] for s in parts) / count
    return to_columns([mean, rate, mean_t, mean_tn])


def core_halves(value, keep, send, core, buf):
    buf[...] = value
    for x_ in range(2):
        mine = pl.ds(pl.multiple_of((x_ * 2 + core) * 128, 128), 128)
        other = pl.ds(pl.multiple_of((x_ * 2 + 1 - core) * 128, 128), 128)
        keep[x_ * 128 : x_ * 128 + 128, :] = buf[mine, :].astype(keep.dtype)
        send[x_ * 128 : x_ * 128 + 128, :] = buf[other, :].astype(send.dtype)


def ffn_back_kernel(p, s0, s1, s2, s3, f, dg, e, win, gc_out, keep, send, buf):
    idx = Place()
    core = lax.rem(idx[1], 2)
    mean, rate, mean_t, mean_tn = ffn_columns(s0, s1, s2, s3)
    n_f = (f[...] - mean) * rate
    df = rate * (e[...] * p[16:17] - mean_t - n_f * mean_tn)
    gc = (df * dg[...]).astype(BF16)
    gc_out[...] = gc
    core_halves(nt(gc, win[...]), keep, send, core, buf)


def by_wide(value, w, steps, out):
    for i, step in enumerate(steps):
        out[i] = value[pl.ds(pl.multiple_of((w ^ step) * 96, 32), 96), :].astype(BF16)


def ffn_grad_kernel(
    p, s0, s1, s2, s3, f, e, gy, z_out, keep_a, keep_b, send_a, send_b, sums, prod
):
    idx = Place()
    mean, rate, _, _ = ffn_columns(s0, s1, s2, s3)
    n_f = (f[...] - mean) * rate
    z = (n_f * p[16:17] + p[18:19]).astype(BF16)
    z_out[...] = z
    prod[...] = tn(z, gy[...])
    for steps, out in (((2, 6), keep_a), ((0, 4), keep_b), ((3, 7), send_a), ((1, 5), send_b)):
        by_wide(prod, idx[0], steps, out)
    sums[...] = rows_of([colsum(e[...] * n_f), None, colsum(e[...]), None], 8)


def in_grad_kernel(h2, gc, keep_a, keep_b, send_a, send_b, prod):
    idx = Place()
    prod[...] = tn(h2[...], gc[...])
    for steps, out in (((4, 5), keep_a), ((0, 1), keep_b), ((6, 7), send_a), ((2, 3), send_b)):
        by_wide(prod, idx[0], steps, out)


def out_kernel(z, wout, gc, gy, sums_in, keep, send, sums, buf):
    idx = Place()
    core_halves(nn(z[...], wout[...]), keep, send, lax.rem(idx[1], 2), buf)
    extra = rows_of([None, colsum(gc[...].astype(F32)), None, colsum(gy[...].astype(F32))], 8)
    sums[...] = sums_in[...] + extra


def prob_kernel(qkv, lse, *outs):
    for h in range(3):
        low_q = qkv[:, h * 64 : h * 64 + 64] * jnp.asarray(SCORE_SCALE, BF16)
        head_k = qkv[:, 192 + h * 64 : 256 + h * 64]
        for i in range(2):
            keys = 256 * (i + 1)
            here = slice(i * 256, i * 256 + 256)
            shape = (keys, 256)
            scores = nt(head_k[0:keys], low_q[here])
            outs[i][h] = jnp.where(
                sublanes(shape) <= lanes(shape) + i * 256,
                jnp.exp(scores - lse[h : h + 1, here]),
                0.0,
            )


def norm_two_kernel(x2, n2_out, rate_out):
    n2_out[...], rate_out[...] = normed(x2[...])


def add_kernel(keep, got, out):
    out[...] = (keep[...].astype(F32) + got[...].astype(F32)).astype(out.dtype)


def hop_kernel(keep, got, own, send):
    for i in range(2):
        own[i] = keep[2 * i].astype(F32) + got[2 * i].astype(F32)
        send[i] = (keep[2 * i + 1].astype(F32) + got[2 * i + 1].astype(F32)).astype(BF16)


def pair_kernel(keep, got, out):
    for i in range(2):
        out[i] = (keep[i].astype(F32) + got[i].astype(F32)).astype(out.dtype)


def split_kernel(keep, got, first, second):
    first[...] = (keep[0].astype(F32) + got[0].astype(F32)).astype(first.dtype)
    second[...] = (keep[1].astype(F32) + got[1].astype(F32)).astype(second.dtype)


def last_hop_kernel(own, got, mine, send):
    mine[...] = own[0] + got[0].astype(F32)
    send[...] = (own[1] + got[1].astype(F32)).astype(BF16)


def sum_out_kernel(mine, got, out):
    out[...] = mine[...] + got[...].astype(F32)


def mid_back_kernel(
    p, own, own_x, sib, sib_x, n2, rate2, gy, n_o, rate_o, wattn,
    dx2_out, ga_out, do_out, e2_out, eo_out,
):
    idx = Place()
    n = idx[1]
    core = lax.rem(n, 2)
    for x_ in range(2):
        at = slice(x_ * 128, x_ * 128 + 128)
        mine = pl.ds(pl.multiple_of((x_ * 2 + core) * 128, 128), 128)
        other = pl.ds(pl.multiple_of((x_ * 2 + 1 - core) * 128, 128), 128)
        e2_out[mine, :] = own[at].astype(F32) + own_x[at].astype(F32)
        e2_out[other, :] = sib[at].astype(F32) + sib_x[at].astype(F32)
    dx2 = gy[...].astype(F32) + norm_back(e2_out[...], n2[...], rate2[...], p[2:3])
    dx2_out[...] = dx2
    ga = dx2.astype(BF16)
    ga_out[...] = ga
    eo = nt(ga, wattn[...])
    eo_out[...] = eo
    d_o = norm_back(eo, n_o[...], rate_o[...], p[1:2])
    for m in range(4):
        @pl.when(n == m)
        def _():
            do_out[...] = d_o[:, m * 192 : m * 192 + 192].astype(BF16)


def attn_grad_kernel(u, ga, eo, n_o, e2, n2, sums, keep, send, gat):
    idx = Place()
    w, n = idx[0], idx[1]
    e_o, e_2 = eo[...], e2[...]
    model = rows_of(
        [
            None,
            colsum(e_o * n_o[...]),
            colsum(e_2 * n2[...]),
            None,
            None,
            None,
            colsum(e_o),
            colsum(ga[...].astype(F32)),
            colsum(e_2),
            sums[3:4],
        ],
        16,
    )
    gat[...] = tn(u[...], ga[...]).reshape(8, 4, 24, 768)
    for i in range(8):
        to = w ^ i
        block = (keep if i % 2 == 0 else send).at[i // 2]
        mine = left(model, to * 96 + n * 24, 768)
        ffn = left(sums[...], to * 96, 768)
        extra = jnp.concatenate(
            [mine[0:8, 0:128], mine[8:16, 0:128], ffn[:, 0:128], jnp.zeros((8, 384), F32)], axis=1
        )
        block[...] = jnp.concatenate([gat[to, n], extra], axis=0).astype(BF16)


def head_back_kernel(
    off, qkv, o_t, p0, p1, do, a1, wqkv, n1,
    keep_a, keep_b, send_a, send_b, d_keep, d_send, buf, prod,
):
    idx = Place()
    w, n = idx[0], idx[1]
    core = lax.rem(n, 2)
    do_t = do[...].astype(F32).T
    k_t = qkv[:, 192:384].astype(F32).T
    row = lanes((1, 512))
    column = sublanes((512, 1))
    dq_parts, dk_parts, dv_parts = [], [], []
    for h in range(3):
        head = n * 3 + h
        o1, o2 = offset_of(off, 1, head), offset_of(off, 2, head)
        r1 = (lax.rem(row, 2).astype(F32) == o1).astype(F32)
        r2 = (lax.rem(row, 4).astype(F32) == o2).astype(F32)
        c1 = (lax.rem(column, 2).astype(F32) == o1).astype(F32)
        c2 = (lax.rem(column, 4).astype(F32) == o2).astype(F32)
        span = slice(h * 64, h * 64 + 64)
        delta = colsum(do_t[span] * o_t[span, :])
        head_q = qkv[:, h * 64 : h * 64 + 64].astype(F32) * SCORE_SCALE
        head_v = qkv[:, 384 + h * 64 : 448 + h * 64]
        head_do = do[:, h * 64 : h * 64 + 64]
        do_f = head_do.astype(F32)
        q_all = jnp.concatenate([head_q, head_q * c1, head_q * c2], axis=1).astype(BF16)
        do_all = jnp.concatenate([do_f, do_f * c1, do_f * c2], axis=1).astype(BF16)
        kt = k_t[span]
        k_all = jnp.concatenate([kt, kt * r1, kt * r2], axis=0).astype(BF16)
        dk = jnp.zeros((512, 192), F32)
        dv = jnp.zeros((512, 192), F32)
        dq_blocks = []
        for i in range(2):
            keys = 256 * (i + 1)
            here = slice(i * 256, i * 256 + 256)
            prob = (p0, p1)[i][h]
            grad_p = nt(head_v[0:keys], head_do[here])
            grad_s = (prob * (grad_p - delta[:, here])).astype(BF16)
            dv_i = nn(prob.astype(BF16), do_all[here])
            dk_i = nn(grad_s, q_all[here])
            if keys < 512:
                zero = jnp.zeros((512 - keys, 192), F32)
                dv_i = jnp.concatenate([dv_i, zero], axis=0)
                dk_i = jnp.concatenate([dk_i, zero], axis=0)
            dv = dv + dv_i
            dk = dk + dk_i
            dq_i = nn(k_all[:, 0:keys], grad_s)
            dq_blocks.append(dq_i[0:64] + r1[:, here] * dq_i[64:128] + r2[:, here] * dq_i[128:192])
        dq_parts.append(jnp.concatenate(dq_blocks, axis=1) * SCORE_SCALE)
        dk_parts.append(dk[:, 0:64] + c1 * dk[:, 64:128] + c2 * dk[:, 128:192])
        dv_parts.append(dv[:, 0:64] + c1 * dv[:, 64:128] + c2 * dv[:, 128:192])
    dq = jnp.concatenate(dq_parts, axis=0).T
    g = jnp.concatenate([dq] + dk_parts + dv_parts + [jnp.zeros((512, 64), F32)], axis=1)
    g = g.astype(BF16)
    prod[...] = tn(a1[...], g)
    grad = nt(g, wqkv[...])
    outer = rows_of([None, colsum(grad * n1[...]), colsum(grad)], 8)
    g_sum = colsum(g.astype(F32))
    for i in range(8):
        to = w ^ i
        block = ((keep_b, keep_a), (send_b, send_a))[i % 2][i // 2 % 2].at[i // 4]
        turned = left(outer, to * 96, 768)[:, 0:640]
        extra = jnp.where(sublanes((8, 640)) == 0, g_sum, turned)
        mine = prod[pl.ds(pl.multiple_of(to * 96, 32), 96), :]
        block[...] = jnp.concatenate([mine, extra], axis=0).astype(BF16)
    core_halves(grad, d_keep, d_send, core, buf)


def tail_add_kernel(ok, og, dk, dg, keep, send, buf):
    idx = Place()
    x_ = idx[1] // 2
    buf[:, 0:768] = ok[...].astype(F32) + og[...].astype(F32)
    buf[:, 768:1536] = dk[...].astype(F32) + dg[...].astype(F32)
    keep[...] = buf[pl.ds(pl.multiple_of(x_ * 128, 128), 128), :]
    send[...] = buf[pl.ds(pl.multiple_of((1 - x_) * 128, 128), 128), :].astype(BF16)


def token_kernel(p, keep, got, tok, x2, dx2, out, grad):
    idx = Place()
    mine = pl.ds(pl.multiple_of(idx[1] * 128, 128), 128)
    both = keep[...] + got[...].astype(F32)
    out[...] = (x2[mine, :] + both[:, 0:768] + p[9:10]).astype(BF16)
    n1, rate = normed(tok[...].astype(F32))
    grad[...] = dx2[mine, :] + norm_back(both[:, 768:1536], n1, rate, p[0:1])


def sum_in_kernel(mine, got, own, t1, t2, t3, buf):
    idx = Place()
    n = idx[1]
    buf[...] = (mine[...] + got[...].astype(F32)).reshape(4, 24, 768)
    own[...] = buf[n]
    for k, out in enumerate((t1, t2, t3)):
        out[...] = buf[n ^ (k + 1)].astype(BF16)


def sum_qkv_kernel(mine, z1, z2, z3, own, t1, t2, t3, buf):
    idx = Place()
    n = idx[1]
    total = mine[...] + z1[...].astype(F32) + z2[...].astype(F32) + z3[...].astype(F32)
    buf[...] = total[0:96].reshape(4, 24, 640)
    own[0:24] = buf[n]
    own[24:32] = total[96:104]
    for k, out in enumerate((t1, t2, t3)):
        out[...] = jnp.concatenate([buf[n ^ (k + 1)], total[96:104]], axis=0).astype(BF16)


def final_in_kernel(i0, i1, i2, i3, out, buf):
    idx = Place()
    n = idx[1]
    for k, i in enumerate((i0, i1, i2, i3)):
        buf[n ^ k] = i[...].astype(F32)
    for m in range(4):
        block = buf[m]
        for w in range(8):
            at = (w * 4 + m) * 96
            out[:, at : at + 96] = block[:, w * 96 : w * 96 + 96]


def final_kernel(q0, q1, q2, q3, a_mine, a_got, gq, gattn, gains, biases, gffn, bffn, buf):
    idx = Place()
    w, n = idx[0], idx[1]
    total = a_mine[...] + a_got[...].astype(F32)
    gattn[...] = total[0:24]
    extra = total[24:32]
    for k, q in enumerate((q0, q1, q2, q3)):
        buf[n ^ k] = q[...].astype(F32)
    for m in range(4):
        block = buf[m]
        for part in range(3):
            at = part * 768 + m * 192
            gq[:, at : at + 192] = block[0:24, part * 192 : part * 192 + 192]
    tails = [buf[m][24:32] for m in range(4)]
    q_row = jnp.concatenate([t[:, 0:192] for t in tails], axis=1)
    v_row = jnp.concatenate([t[:, 384:576] for t in tails], axis=1)
    place = (w * 4 + n) * 24
    q_row = left(q_row, place, 768)[0:1, 0:24]
    v_row = left(v_row, place, 768)[0:1, 0:24]
    norm = left((tails[0] + tails[1] + tails[2] + tails[3])[:, 0:128], n * 24, 128)[:, 0:24]
    low, high, ffn = extra[:, 0:24], extra[:, 128:152], extra[:, 256:352]
    gains[0:1] = norm[1:2]
    gains[1:3] = low[1:3]
    biases[0:1] = norm[2:3]
    biases[1:2] = q_row
    biases[2:3] = v_row
    biases[3:5] = low[6:8]
    biases[5:7] = high[0:2]
    gffn[...] = ffn[0:1]
    bffn[...] = ffn[1:3]


def swap(values, axis, size, step):
    return lax.ppermute(values, axis, [(i, i ^ step) for i in range(size)])


def Y(v):
    return swap(v, "wide", 8, 1)


def Z1(v):
    return swap(v, "wide", 8, 2)


def Z2(v):
    return swap(v, "wide", 8, 4)


def Z3(v):
    return swap(v, "wide", 8, 6)


def C(v):
    return swap(v, "narrow", 4, 1)


def X(v):
    return swap(v, "narrow", 4, 2)


def XC(v):
    return swap(v, "narrow", 4, 3)


TABLE = (
    ("cy", 0, 4), ("ry", 4, 6), ("b1", 0, 0), ("b3", 0, 0), ("qy", 2, 4), ("b2", 0, 0), ("pack", 2, 5),
    ("q1", 2, 4), ("txc", 6, 0), ("q2", 2, 6), ("q2y", 4, 6), ("tc", 0, 6), ("q1y", 4, 5), ("x", 6, 10),
    ("r1", 4, 6), ("q3", 4, 6), ("gx", 6, 8), ("tx", 4, 6), ("r1y", 6, 7), ("n1", 6, 15), ("c1", 4, 9),
    ("c2y", 8, 9), ("c2", 6, 8), ("r2", 4, 6), ("r3", 6, 7), ("q3y", 4, 0), ("c3", 6, 10), ("c1y", 6, 10),
    ("ox", 8, 10), ("r3y", 6, 0), ("oc", 10, 0), ("gy", 8, 17), ("c3y", 11, 14), ("attend", 6, 8),
    ("r2y", 6, 8), ("gxc", 8, 0), ("ac", 10, 0), ("gc", 8, 0), ("place_i", 7, 9), ("sub", 10, 0),
    ("place_l", 10, 0), ("oxc", 10, 0), ("place_a", 10, 0), ("place_c", 10, 11), ("r3yc", 10, 0),
    ("middle", 10, 15), ("s3", 14, 0), ("s2", 14, 15), ("dc", 14, 0), ("place_cl", 14, 15),
    ("ffn_back", 14, 0), ("s1", 14, 0), ("add", 15, 0), ("dx", 16, 17), ("ds", 18, 0), ("e", 14, 0),
    ("in_grad", 14, 0), ("n2", 15, 19), ("ffn_grad", 16, 0), ("out_b", 18, 20), ("dxc", 18, 0),
    ("out", 16, 18), ("prob", 19, 20), ("out_a", 16, 0), ("in_a", 16, 18), ("opc", 18, 19), ("mid", 18, 19),
    ("out_z", 20, 22), ("in_on", 18, 0), ("qa", 20, 0), ("in_b", 17, 20), ("qb", 20, 0), ("out_on", 18, 0),
    ("qz1", 20, 0), ("split_b", 20, 21), ("out_own", 18, 22), ("in_own", 20, 0), ("at_y", 19, 22),
    ("qz3", 20, 0), ("split_a", 20, 0), ("attn_grad", 19, 0), ("head", 19, 0), ("in_z", 20, 22),
    ("out_last", 22, 0), ("in_y", 22, 0), ("tail", 20, 0), ("qz2", 20, 24), ("tail_add", 20, 0),
    ("out_z2", 22, 0), ("token", 22, 25), ("at_hop", 22, 0), ("tc_g", 20, 0), ("at_z2", 23, 0),
    ("at_z1", 22, 0), ("n2q", 23, 25), ("sum_out", 25, 26), ("at_last", 22, 0), ("in_last", 20, 0),
    ("n1q", 21, 25), ("n3q", 24, 27), ("i2", 22, 0), ("sum_in", 22, 0), ("i3", 22, 0), ("i1", 22, 0),
    ("sum_qkv", 21, 32), ("final_in", 22, 26), ("final", 32, 0),
)


def steps(env):
    offsets = env["offsets"]
    two, two_f = ((2, 96, 768), BF16), ((2, 96, 768), F32)
    full, full_f, half, half_f = (
        ((512, 768), BF16), ((512, 768), F32), ((256, 768), BF16), ((256, 768), F32),
    )
    sq = ((768, 768), BF16)
    blk, blk2 = ((104, 640), BF16), ((2, 104, 640), BF16)

    def kernel(name, body, outs, ins, lead=(), results=None, **keys):
        results = results or (name,)
        table[name] = (
            tuple(ins), results, lambda *a: call(body, outs, *lead, *a, us=COST.get(name, 0.0), **keys)
        )

    def move(name, how, source):
        table[name] = ((source,), (name,), lambda a: (how(a),))

    table = {}
    for name, how, source in (
        ("b1", C, "b1_s"), ("b2", X, "b2_s"), ("b3", XC, "b3_s"), ("cy", Y, "w_out"),
        ("qy", Y, "q"), ("q1", Z1, "q"), ("q2", Z2, "q"), ("q3", Z1, "q2"), ("q1y", Y, "q1"),
        ("q2y", Y, "q2"), ("q3y", Y, "q3"), ("ry", Y, "r"), ("r1", Z1, "r"), ("r2", Z2, "r"),
        ("r3", Z1, "r2"), ("r1y", Y, "r1"), ("r2y", Y, "r2"), ("r3y", Z1, "r2y"),
        ("c1", Z1, "w_out"), ("c2", Z2, "w_out"), ("c3", Z1, "c2"), ("c1y", Y, "c1"),
        ("c2y", Y, "c2"), ("c3y", Y, "c3"), ("tc", C, "tokens"), ("tx", X, "tokens"), ("txc", C, "tx"),
        ("gc", C, "cotangent"), ("gx", X, "cotangent"), ("gxc", C, "gx"),
        ("oc", C, "o_low"), ("ox", X, "o_low"), ("oxc", C, "ox"), ("ac", C, "attn"), ("r3yc", C, "r3y"),
        ("s1", C, "stats"), ("s2", X, "stats"), ("s3", XC, "stats"), ("dc", C, "d_send"),
        ("dx", X, "d_half"), ("ds", C, "d_half"), ("dxc", C, "dx"), ("out_a", Y, "out_sa"),
        ("out_b", Y, "out_sb"), ("in_a", Z1, "in_sa"), ("in_b", Z1, "in_sb"), ("opc", C, "op_send"),
        ("qa", Y, "qkv_a"), ("qb", Y, "qkv_b"), ("out_z", Z1, "out_on"), ("in_z", Z2, "in_on"),
        ("tc_g", C, "t_send"), ("at_y", Y, "at_send"), ("qz1", Z1, "send_1"), ("qz2", Z2, "send_2"),
        ("qz3", Z3, "send_3"), ("out_z2", Z2, "out_to"), ("tail", X, "tail_send"), ("in_y", Y, "in_to"),
        ("at_z1", Z1, "at_on"), ("at_z2", Z2, "at_to"), ("i1", C, "i1_s"), ("i2", X, "i2_s"),
        ("i3", XC, "i3_s"), ("n1q", C, "n1_s"), ("n2q", X, "n2_s"), ("n3q", XC, "n3_s"),
    ):
        move(name, how, source)
    kernel(
        "pack", pack_kernel, [((96, 640), BF16), ((144, 768), BF16)], ("b0", "b1", "b2", "b3"), (), ("q", "r"),
        scratch=[((4, 24, 640), F32), ((4, 24, 768), F32), ((2, 24, 768), F32)],
    )
    kernel("x", place_t_kernel, [full], ("tokens", "tc", "tx", "txc"))
    kernel("n1", norm_kernel, [full_f], ("x",))
    kernel(
        "attend", attend_kernel,
        [
            ((768, 640), BF16), ((24, 768), F32), full, ((512, 640), BF16), ((192, 512), F32),
            ((8, 512), F32), ((512, 192), BF16),
        ],
        ("n1", "q", "qy", "q1", "q1y", "q2", "q2y", "q3", "q3y"), (offsets,),
        ("wqkv", "params", "a1", "qkv", "o_t", "lse", "o_low"),
    )
    kernel("gy", place_t_kernel, [full], ("cotangent", "gc", "gx", "gxc"))
    kernel(
        "place_i", place_i_kernel, [sq, ((7, 48, 768), BF16)], ("r", "ry", "r1", "r1y", "r2", "r2y", "r3"), (),
        ("win_7", "attn"),
    )
    kernel("place_a", place_a_kernel, [sq], ("attn", "ac"), (), ("wattn_7",), scratch=[((4, 24, 768), F32)])
    kernel(
        "place_l", place_last_kernel, [sq, sq], ("win_7", "wattn_7", "r3y", "r3yc"), (), ("win", "wattn"),
        scratch=[((4, 24, 768), F32)], alias={0: 0, 1: 1},
    )
    kernel(
        "sub", sub_norm_kernel, [full_f, ((512, 1), F32), full], ("params", "o_low", "oc", "ox", "oxc"), (),
        ("n_o", "rate_o", "u"), scratch=[((4, 512, 192), F32)],
    )
    kernel(
        "middle", middle_kernel, [full_f, full, full_f, full_f, ((8, 512), F32)],
        ("x", "params", "u", "wattn", "win"), (), ("x2", "h2", "f", "dg", "stat_f"),
    )
    kernel(
        "place_c", place_c_kernel, [sq], ("w_out", "cy", "c1", "c1y", "c2", "c2y", "c3"), (), ("wout_7",)
    )
    kernel("place_cl", place_c_last_kernel, [sq], ("wout_7", "c3y"), (), ("wout",), alias={0: 0})
    kernel(
        "e", cot_kernel, [full_f, ((8, 512), F32)], ("gy", "wout", "params", "f", "stat_f"), (), ("e", "stats")
    )
    stats = ("params", "stats", "s1", "s2", "s3")
    kernel(
        "ffn_back", ffn_back_kernel, [full, half_f, half], (*stats, "f", "dg", "e", "win"), (),
        ("gc_f", "d_keep", "d_send"), scratch=[full_f],
    )
    kernel("add", add_kernel, [half], ("d_keep", "dc"), (), ("d_half",))
    kernel(
        "ffn_grad", ffn_grad_kernel, [full, two, two, two, two, ((8, 768), F32)],
        (*stats, "f", "e", "gy"), (), ("z", "out_ka", "out_kb", "out_sa", "out_sb", "sums_f"),
        scratch=[((768, 768), F32)],
    )
    kernel(
        "in_grad", in_grad_kernel, [two] * 4, ("h2", "gc_f"), (), ("in_ka", "in_kb", "in_sa", "in_sb"),
        scratch=[((768, 768), F32)],
    )
    kernel(
        "out", out_kernel, [half_f, half, ((8, 768), F32)], ("z", "wout", "gc_f", "gy", "sums_f"), (),
        ("op_keep", "op_send", "sums"), scratch=[full_f],
    )
    kernel(
        "prob", prob_kernel, [((3, 256, 256), F32), ((3, 512, 256), F32)], ("qkv", "lse"), (), ("p0", "p1")
    )
    kernel("n2", norm_two_kernel, [full_f, ((512, 1), F32)], ("x2",), (), ("n2", "rate2"))
    kernel(
        "mid", mid_back_kernel, [full_f, full, ((512, 192), BF16), full_f, full_f],
        ("params", "d_half", "dx", "ds", "dxc", "n2", "rate2", "gy", "n_o", "rate_o", "wattn"), (),
        ("dx2", "ga", "do", "e2", "eo"),
    )
    kernel(
        "head", head_back_kernel, [blk2, blk2, blk2, blk2, half_f, half],
        ("qkv", "o_t", "p0", "p1", "do", "a1", "wqkv", "n1"), (offsets,),
        ("keep_a", "keep_b", "qkv_a", "qkv_b", "t_keep", "t_send"), scratch=[full_f, ((768, 640), F32)],
    )
    kernel("out_on", pair_kernel, [two], ("out_ka", "out_a"))
    kernel("in_on", pair_kernel, [two], ("in_ka", "in_a"))
    kernel("out_own", pair_kernel, [two_f], ("out_kb", "out_b"))
    kernel("in_own", pair_kernel, [two_f], ("in_kb", "in_b"))
    kernel(
        "attn_grad", attn_grad_kernel, [((4, 32, 768), BF16)] * 2, ("u", "ga", "eo", "n_o", "e2", "n2", "sums"), (),
        ("at_keep", "at_send"), scratch=[((8, 4, 24, 768), F32)],
    )
    kernel("split_a", split_kernel, [blk, blk], ("keep_a", "qa"), (), ("send_1", "send_3"))
    kernel("split_b", split_kernel, [((104, 640), F32), blk], ("keep_b", "qb"), (), ("q_sum", "send_2"))
    block = [((96, 768), F32), ((96, 768), BF16)]
    kernel("out_last", last_hop_kernel, block, ("out_own", "out_z"), (), ("out_mine", "out_to"))
    kernel("in_last", last_hop_kernel, block, ("in_own", "in_z"), (), ("in_mine", "in_to"))
    kernel(
        "at_hop", hop_kernel, [((2, 32, 768), F32), ((2, 32, 768), BF16)], ("at_keep", "at_y"), (), ("at_own", "at_on")
    )
    kernel(
        "at_last", last_hop_kernel, [((32, 768), F32), ((32, 768), BF16)], ("at_own", "at_z1"), (),
        ("at_mine", "at_to"),
    )
    kernel(
        "tail_add", tail_add_kernel, [((128, 1536), F32), ((128, 1536), BF16)],
        ("op_keep", "opc", "t_keep", "tc_g"), (), ("tail_keep", "tail_send"), scratch=[((256, 1536), F32)],
    )
    kernel(
        "token", token_kernel, [((128, 768), BF16), ((128, 768), F32)],
        ("params", "tail_keep", "tail", "tokens", "x2", "dx2"), (), ("outputs", "grad_inputs"), final=True,
    )
    kernel(
        "sum_out", sum_out_kernel, [((96, 768), F32)], ("out_mine", "out_z2"), (), ("grad_w_out",), final=True
    )
    small = ((24, 768), BF16)
    kernel(
        "sum_in", sum_in_kernel, [((24, 768), F32), small, small, small], ("in_mine", "in_y"), (),
        ("i_own", "i1_s", "i2_s", "i3_s"), scratch=[((4, 24, 768), F32)],
    )
    kernel(
        "final_in", final_in_kernel, [((24, 3072), F32)], ("i_own", "i1", "i2", "i3"), (), ("grad_w_in",),
        scratch=[((4, 24, 768), F32)], final=True,
    )
    row = ((32, 640), BF16)
    kernel(
        "sum_qkv", sum_qkv_kernel, [((32, 640), F32), row, row, row], ("q_sum", "qz1", "qz2", "qz3"), (),
        ("q_mine", "n1_s", "n2_s", "n3_s"), scratch=[((4, 24, 640), F32)],
    )
    kernel(
        "final", final_kernel,
        [
            ((24, 2304), F32), ((24, 768), F32), ((3, 24), F32), ((7, 24), F32), ((1, 96), F32), ((2, 96), F32),
        ],
        ("q_mine", "n1q", "n2q", "n3q", "at_mine", "at_z2"), (),
        ("grad_w_qkv", "grad_w_attn", "grad_gains", "grad_biases", "grad_gain_ffn", "grad_ffn_biases"),
        scratch=[((4, 32, 640), F32)], final=True,
    )
    return table


COST = {
    "attend": 4.0,
    "middle": 2.0,
    "ffn_back": 4.0,
    "ffn_grad": 4.0,
    "in_grad": 8.0,
    "out": 1.0,
    "mid": 1.0,
    "attn_grad": 8.0,
}


def fast_body(
    tokens, cotangent, w_qkv, w_attn, w_in, w_out, gains_model, biases_model, gain_ffn, biases_ffn, offsets
):
    env = {"offsets": offsets}
    first = ("tokens", "cotangent", "w_out", "b0", "b1_s", "b2_s", "b3_s")
    outs = call(
        prep_kernel,
        [((128, 768), BF16), ((128, 768), BF16), ((96, 768), BF16)]
        + [((24, 2176 if k % 2 == 0 else 1408), BF16) for k in range(4)],
        w_qkv, w_in, w_attn, gains_model, biases_model, gain_ffn[None], biases_ffn,
        tokens, cotangent, w_out,
        scratch=[((64, 128), F32), ((4, 24, 640), F32), ((4, 24, 768), F32)], held=False,
    )
    env.update(zip(first, outs))
    table = steps(env)
    for slot in range(max(at for _, at, _ in TABLE) + 1):
        now = [name for name, at, _ in TABLE if at == slot]
        tied = [r for name, _, done in TABLE if done == slot and done > 0 for r in table[name][1]]
        tied += [v for name in now for v in table[name][0] if v in env]
        tied = list(dict.fromkeys(tied))
        if slot and tied:
            env.update(zip(tied, lax.optimization_barrier(tuple(env[v] for v in tied))))
        while now:
            name = next(n for n in now if all(v in env for v in table[n][0]))
            now.remove(name)
            ins, results, run = table[name]
            env.update(zip(results, run(*(env[v] for v in ins))))
    return (
        env["outputs"], env["grad_inputs"], env["grad_w_qkv"], env["grad_w_attn"], env["grad_w_in"],
        env["grad_w_out"], env["grad_gains"], env["grad_biases"], env["grad_gain_ffn"][0],
        env["grad_ffn_biases"],
    )


def solution(mesh):
    fast = dict(mesh.shape) == {"wide": 8, "narrow": 4}
    return jax.shard_map(
        fast_body if fast else body,
        mesh=mesh,
        in_specs=(
            P(("wide", "narrow"), None),
            P(("wide", "narrow"), None),
            P(("wide", "narrow"), None),
            P(("wide", "narrow"), None),
            P(("wide", "narrow"), None),
            P(("wide", "narrow"), None),
            P(None, ("wide", "narrow")),
            P(None, ("wide", "narrow")),
            P(("wide", "narrow")),
            P(None, ("wide", "narrow")),
            P(),
        ),
        out_specs=(
            P(("wide", "narrow"), None),
            P(("wide", "narrow"), None),
            P(("wide", "narrow"), None),
            P(("wide", "narrow"), None),
            P(("wide", "narrow"), None),
            P(("wide", "narrow"), None),
            P(None, ("wide", "narrow")),
            P(None, ("wide", "narrow")),
            P(("wide", "narrow")),
            P(None, ("wide", "narrow")),
        ),
        check_vma=False,
    )
```

```python
import jax
import jax.numpy as jnp
from jax import lax
from jax.experimental import pallas as pl
from jax.experimental.pallas import tpu as pltpu
from jax.sharding import PartitionSpec as P

HEADS = 12
HEAD_DIM = 64
RATE0 = 1
RATE1 = 2
RATE2 = 4


EPSILON = 1e-05
SCORE_SCALE = 0.125
MASKED = -1e30


def layer_norm(values, norm_gain, norm_shift):
    average = jnp.mean(values, axis=-1, keepdims=True)
    centred = values - average
    spread = jnp.mean(centred * centred, axis=-1, keepdims=True)
    return centred * lax.rsqrt(spread + EPSILON) * norm_gain + norm_shift


def gelu_exact(values):
    return jax.nn.gelu(values, approximate=False)


def product(former, latter):
    return jnp.dot(former, latter, preferred_element_type=jnp.float32)


def product_tn(former, latter):
    return lax.dot_general(
        former, latter, (((0,), (0,)), ((), ())), preferred_element_type=jnp.float32
    )


def product_nt(former, latter):
    return lax.dot_general(
        former, latter, (((1,), (1,)), ((), ())), preferred_element_type=jnp.float32
    )


def one_hot(offset_row, dilation):
    return (jnp.arange(dilation)[:, None] == offset_row[None, :]).astype(jnp.float32)


def select_rows(dense_rows, selector, dilation):
    picked_rows = dense_rows.shape[0] // dilation
    shaped = dense_rows.reshape(picked_rows, dilation, HEADS, HEAD_DIM)
    picked = jnp.einsum(
        "trhd,rh->thd",
        shaped,
        selector.astype(dense_rows.dtype),
        preferred_element_type=jnp.float32,
    )
    return picked.reshape(picked_rows, HEADS * HEAD_DIM)


def spread_rows(sparse_rows, selector, dilation):
    shaped = sparse_rows.reshape(sparse_rows.shape[0], 1, HEADS, HEAD_DIM)
    placed = shaped * selector[None, :, :, None]
    return placed.reshape(sparse_rows.shape[0] * dilation, HEADS * HEAD_DIM)


def select_heads(dense_heads, selector, dilation):
    shaped = dense_heads.reshape(dense_heads.shape[0] // dilation, dilation, HEADS)
    return jnp.sum(shaped * selector[None], axis=1)


def spread_heads(sparse_heads, selector, dilation):
    placed = jnp.where(selector[None] > 0, sparse_heads[:, None, :], MASKED)
    return placed.reshape(sparse_heads.shape[0] * dilation, HEADS)


def head_major(values):
    return values.reshape(values.shape[0], HEADS, HEAD_DIM).transpose(1, 0, 2)


def row_major(values):
    return values.transpose(1, 0, 2).reshape(values.shape[1], HEADS * HEAD_DIM)


def key_mask(row_count, block_count, own_block):
    query_pos = jnp.arange(row_count)[:, None]
    position = jnp.arange(row_count * block_count)[None, :]
    key_block = position // row_count
    within = position % row_count
    return (key_block < own_block) | (key_block == own_block) & (within <= query_pos)


def masked_scores(head_query, head_keys, allowed):
    return jnp.where(allowed, product_nt(head_query, head_keys) * SCORE_SCALE, MASKED)


def pattern_lse(queries, keys, allowed):

    def one_head(operands):
        scores = masked_scores(operands[0], operands[1], allowed)
        peak_rows = jnp.max(scores, axis=1, keepdims=True)
        return peak_rows[:, 0] + jnp.log(jnp.sum(jnp.exp(scores - peak_rows), axis=1))

    return lax.map(one_head, (head_major(queries), head_major(keys))).T


def pattern_out(queries, keys, values, allowed, totals):

    def one_head(operands):
        head_query, head_keys, head_values, head_total = operands
        scores = masked_scores(head_query, head_keys, allowed)
        probability = jnp.where(allowed, jnp.exp(scores - head_total[:, None]), 0.0).astype(
            jnp.bfloat16
        )
        return product(probability, head_values)

    return row_major(
        lax.map(one_head, (head_major(queries), head_major(keys), head_major(values), totals.T))
    )


def pattern_back(queries, keys, values, allowed, totals, deltas, grad_out):

    def one_head(operands):
        head_query, head_keys, head_values, head_total, head_delta, head_grad = operands
        scores = masked_scores(head_query, head_keys, allowed)
        probability = jnp.where(allowed, jnp.exp(scores - head_total[:, None]), 0.0)
        grad_probs = product_nt(head_grad, head_values)
        grad_scores = (probability * (grad_probs - head_delta[:, None])).astype(jnp.bfloat16)
        grad_query = product(grad_scores, head_keys) * SCORE_SCALE
        grad_keys = product_tn(grad_scores, head_query) * SCORE_SCALE
        grad_values = product_tn(probability.astype(jnp.bfloat16), head_grad)
        return (grad_query, grad_keys, grad_values)

    results = lax.map(
        one_head,
        (
            head_major(queries),
            head_major(keys),
            head_major(values),
            totals.T,
            deltas.T,
            head_major(grad_out),
        ),
    )
    return (row_major(results[0]), row_major(results[1]), row_major(results[2]))


def body(
    tokens,
    cotangent,
    w_qkv,
    w_attn,
    w_in,
    w_out,
    gains_model,
    biases_model,
    gain_ffn,
    biases_ffn,
    offsets,
):
    gathered = (
        lax.all_gather(w_qkv, ("wide", "narrow"), axis=0, tiled=True),
        lax.all_gather(w_attn, ("wide", "narrow"), axis=0, tiled=True),
        lax.all_gather(w_in, ("wide", "narrow"), axis=0, tiled=True),
        lax.all_gather(w_out, ("wide", "narrow"), axis=0, tiled=True),
        lax.all_gather(gains_model, ("wide", "narrow"), axis=1, tiled=True),
        lax.all_gather(biases_model, ("wide", "narrow"), axis=1, tiled=True),
        lax.all_gather(gain_ffn, ("wide", "narrow"), axis=0, tiled=True),
        lax.all_gather(biases_ffn, ("wide", "narrow"), axis=1, tiled=True),
    )
    qkv_full, attn_full, in_full, out_full = (gathered[0], gathered[1], gathered[2], gathered[3])
    model_gains = gathered[4].astype(jnp.float32)
    model_biases = gathered[5].astype(jnp.float32)
    ffn_gain = gathered[6].astype(jnp.float32)
    ffn_biases = gathered[7].astype(jnp.float32)
    local_rows = tokens.shape[0]
    width = tokens.shape[1]
    inputs = tokens.astype(jnp.float32)
    normed_one, pull_one = jax.vjp(layer_norm, inputs, model_gains[0], model_biases[0])
    normed_low = normed_one.astype(jnp.bfloat16)
    projected = product(normed_low, qkv_full)
    queries = (projected[:, :width] + model_biases[1]).astype(jnp.bfloat16)
    keys = projected[:, width : 2 * width].astype(jnp.bfloat16)
    values = (projected[:, 2 * width :] + model_biases[2]).astype(jnp.bfloat16)
    size_narrow = lax.axis_size("narrow")
    narrow_place = lax.axis_index("narrow")
    dilations = (RATE0, RATE1, RATE2)
    selectors = (one_hot(offsets[0], RATE0), one_hot(offsets[1], RATE1), one_hot(offsets[2], RATE2))
    picked_q = [
        select_rows(queries, selectors[pattern], dilations[pattern]).astype(jnp.bfloat16)
        for pattern in range(3)
    ]
    picked_k = [
        select_rows(keys, selectors[pattern], dilations[pattern]).astype(jnp.bfloat16)
        for pattern in range(3)
    ]
    picked_v = [
        select_rows(values, selectors[pattern], dilations[pattern]).astype(jnp.bfloat16)
        for pattern in range(3)
    ]
    arrived = (
        lax.all_gather(picked_k[0], "narrow", axis=0, tiled=True),
        lax.all_gather(picked_v[0], "narrow", axis=0, tiled=True),
        lax.all_gather(picked_k[1], "narrow", axis=0, tiled=True),
        lax.all_gather(picked_v[1], "narrow", axis=0, tiled=True),
        lax.all_gather(picked_k[2], "narrow", axis=0, tiled=True),
        lax.all_gather(picked_v[2], "narrow", axis=0, tiled=True),
    )
    key_sets = (arrived[0], arrived[2], arrived[4])
    value_sets = (arrived[1], arrived[3], arrived[5])
    allowed_sets = tuple(
        (
            key_mask(local_rows // dilations[pattern], size_narrow, narrow_place)
            for pattern in range(3)
        )
    )
    partial_value = jnp.stack(
        [
            spread_heads(
                pattern_lse(picked_q[pattern], key_sets[pattern], allowed_sets[pattern]),
                selectors[pattern],
                dilations[pattern],
            )
            for pattern in range(3)
        ]
    )
    peak_rows = jnp.max(partial_value, axis=0)
    totals = peak_rows + jnp.log(jnp.sum(jnp.exp(partial_value - peak_rows), axis=0))
    attended = jnp.zeros((local_rows, width), jnp.float32)
    for pattern in range(3):
        pattern_totals = select_heads(totals, selectors[pattern], dilations[pattern])
        result_rows = pattern_out(
            picked_q[pattern],
            key_sets[pattern],
            value_sets[pattern],
            allowed_sets[pattern],
            pattern_totals,
        )
        attended = attended + spread_rows(result_rows, selectors[pattern], dilations[pattern])
    sub_normed, pull_sub = jax.vjp(layer_norm, attended, model_gains[1], model_biases[3])
    sub_low = sub_normed.astype(jnp.bfloat16)
    middle = inputs + product(sub_low, attn_full) + model_biases[4]
    normed_two, pull_two = jax.vjp(layer_norm, middle, model_gains[2], model_biases[5])
    normed_two_low = normed_two.astype(jnp.bfloat16)
    pre_act = product(normed_two_low, in_full) + ffn_biases[0]
    activated, pull_gelu = jax.vjp(gelu_exact, pre_act)
    ffn_normed, pull_ffn = jax.vjp(layer_norm, activated, ffn_gain, ffn_biases[1])
    ffn_low = ffn_normed.astype(jnp.bfloat16)
    outputs = (middle + product(ffn_low, out_full) + model_biases[6]).astype(jnp.bfloat16)
    regathered = (
        lax.all_gather(w_qkv, ("wide", "narrow"), axis=0, tiled=True),
        lax.all_gather(w_attn, ("wide", "narrow"), axis=0, tiled=True),
        lax.all_gather(w_in, ("wide", "narrow"), axis=0, tiled=True),
        lax.all_gather(w_out, ("wide", "narrow"), axis=0, tiled=True),
    )
    qkv_back, attn_back, in_back, out_back = (
        regathered[0],
        regathered[1],
        regathered[2],
        regathered[3],
    )
    grad_out_f = cotangent.astype(jnp.float32)
    grad_w_out = product_tn(ffn_low, cotangent)
    grad_bias_ffo = jnp.sum(cotangent.astype(jnp.float32), axis=0)
    grad_act, grad_gain_ffn, grad_bias_ffn_norm = pull_ffn(product_nt(cotangent, out_back))
    grad_pre = pull_gelu(grad_act)[0].astype(jnp.bfloat16)
    grad_w_in = product_tn(normed_two_low, grad_pre)
    grad_bias_pre = jnp.sum(grad_pre.astype(jnp.float32), axis=0)
    grad_mid_norm, grad_gain_two, grad_bias_two = pull_two(product_nt(grad_pre, in_back))
    grad_middle = grad_out_f + grad_mid_norm
    grad_branch = grad_middle.astype(jnp.bfloat16)
    grad_w_attn = product_tn(sub_low, grad_branch)
    grad_bias_branch = jnp.sum(grad_branch.astype(jnp.float32), axis=0)
    grad_att, grad_gain_sub, grad_bias_sub = pull_sub(product_nt(grad_branch, attn_back))
    grad_att_low = grad_att.astype(jnp.bfloat16)
    deltas = jnp.sum(
        (grad_att_low.astype(jnp.float32) * attended).reshape(local_rows, HEADS, HEAD_DIM), axis=2
    )
    backward_parts = []
    for pattern in range(3):
        backward_parts.append(
            pattern_back(
                picked_q[pattern],
                key_sets[pattern],
                value_sets[pattern],
                allowed_sets[pattern],
                select_heads(totals, selectors[pattern], dilations[pattern]),
                select_heads(deltas, selectors[pattern], dilations[pattern]),
                select_rows(grad_att_low, selectors[pattern], dilations[pattern]).astype(
                    jnp.bfloat16
                ),
            )
        )
    returned = (
        lax.psum_scatter(
            backward_parts[0][1].astype(jnp.bfloat16), "narrow", scatter_dimension=0, tiled=True
        ).astype(jnp.float32),
        lax.psum_scatter(
            backward_parts[0][2].astype(jnp.bfloat16), "narrow", scatter_dimension=0, tiled=True
        ).astype(jnp.float32),
        lax.psum_scatter(
            backward_parts[1][1].astype(jnp.bfloat16), "narrow", scatter_dimension=0, tiled=True
        ).astype(jnp.float32),
        lax.psum_scatter(
            backward_parts[1][2].astype(jnp.bfloat16), "narrow", scatter_dimension=0, tiled=True
        ).astype(jnp.float32),
        lax.psum_scatter(
            backward_parts[2][1].astype(jnp.bfloat16), "narrow", scatter_dimension=0, tiled=True
        ).astype(jnp.float32),
        lax.psum_scatter(
            backward_parts[2][2].astype(jnp.bfloat16), "narrow", scatter_dimension=0, tiled=True
        ).astype(jnp.float32),
    )
    key_grads = (returned[0], returned[2], returned[4])
    value_grads = (returned[1], returned[3], returned[5])
    grad_q = jnp.zeros((local_rows, width), jnp.float32)
    grad_k = jnp.zeros((local_rows, width), jnp.float32)
    grad_v = jnp.zeros((local_rows, width), jnp.float32)
    for pattern in range(3):
        grad_q = grad_q + spread_rows(
            backward_parts[pattern][0], selectors[pattern], dilations[pattern]
        )
        grad_k = grad_k + spread_rows(key_grads[pattern], selectors[pattern], dilations[pattern])
        grad_v = grad_v + spread_rows(value_grads[pattern], selectors[pattern], dilations[pattern])
    grad_q_low = grad_q.astype(jnp.bfloat16)
    grad_v_low = grad_v.astype(jnp.bfloat16)
    grad_qkv = jnp.concatenate([grad_q_low, grad_k.astype(jnp.bfloat16), grad_v_low], axis=1)
    grad_w_qkv = product_tn(normed_low, grad_qkv)
    grad_bias_q = jnp.sum(grad_q_low.astype(jnp.float32), axis=0)
    grad_bias_v = jnp.sum(grad_v_low.astype(jnp.float32), axis=0)
    grad_first, grad_gain_one, grad_bias_one = pull_one(product_nt(grad_qkv, qkv_back))
    grad_inputs = grad_middle + grad_first
    grad_gains = jnp.stack([grad_gain_one, grad_gain_sub, grad_gain_two])
    grad_biases = jnp.stack(
        [
            grad_bias_one,
            grad_bias_q,
            grad_bias_v,
            grad_bias_sub,
            grad_bias_branch,
            grad_bias_two,
            grad_bias_ffo,
        ]
    )
    grad_ffn_biases = jnp.stack([grad_bias_pre, grad_bias_ffn_norm])
    reduced = (
        lax.psum_scatter(grad_w_qkv, ("wide", "narrow"), scatter_dimension=0, tiled=True),
        lax.psum_scatter(grad_w_attn, ("wide", "narrow"), scatter_dimension=0, tiled=True),
        lax.psum_scatter(grad_w_in, ("wide", "narrow"), scatter_dimension=0, tiled=True),
        lax.psum_scatter(grad_w_out, ("wide", "narrow"), scatter_dimension=0, tiled=True),
        lax.psum_scatter(grad_gains, ("wide", "narrow"), scatter_dimension=1, tiled=True),
        lax.psum_scatter(grad_biases, ("wide", "narrow"), scatter_dimension=1, tiled=True),
        lax.psum_scatter(grad_gain_ffn, ("wide", "narrow"), scatter_dimension=0, tiled=True),
        lax.psum_scatter(grad_ffn_biases, ("wide", "narrow"), scatter_dimension=1, tiled=True),
    )
    return (
        outputs,
        grad_inputs,
        reduced[0],
        reduced[1],
        reduced[2],
        reduced[3],
        reduced[4],
        reduced[5],
        reduced[6],
        reduced[7],
    )


BF16 = jnp.bfloat16
F32 = jnp.float32
ALPHA = (
    -2.72614225801306e-10,
    2.77068142495902e-08,
    -2.10102402082508e-06,
    -5.69250639462346e-05,
    -7.34990630326855e-04,
    -2.95459980854025e-03,
    -1.60960333262415e-02,
)
BETA = (
    -1.45660718464996e-05,
    -2.13374055278905e-04,
    -1.68282697438203e-03,
    -7.37332916720468e-03,
    -1.42647390514189e-02,
)


def nn(a, b):
    return lax.dot_general(a, b, (((1,), (0,)), ((), ())), preferred_element_type=F32)


def nt(a, b):
    return lax.dot_general(a, b, (((1,), (1,)), ((), ())), preferred_element_type=F32)


def tn(a, b):
    return lax.dot_general(a, b, (((0,), (0,)), ((), ())), preferred_element_type=F32)


def erf(v):
    v = jnp.clip(v, -4.0, 4.0)
    s = v * v
    top = jnp.full_like(s, ALPHA[0])
    for term in ALPHA[1:]:
        top = top * s + term
    low = jnp.full_like(s, BETA[0])
    for term in BETA[1:]:
        low = low * s + term
    return v * top / low


def normed(v):
    centred = v - jnp.mean(v, axis=-1, keepdims=True)
    rate = lax.rsqrt(jnp.mean(centred * centred, axis=-1, keepdims=True) + EPSILON)
    return centred * rate, rate


def norm_back(e, n, rate, gain):
    t = e * gain
    return rate * (
        t - jnp.mean(t, axis=-1, keepdims=True) - n * jnp.mean(t * n, axis=-1, keepdims=True)
    )


def colsum(v):
    return jnp.sum(v, axis=0, keepdims=True)


def lanes(shape):
    return lax.broadcasted_iota(jnp.int32, shape, len(shape) - 1)


def sublanes(shape):
    return lax.broadcasted_iota(jnp.int32, shape, len(shape) - 2)


def rows_of(parts, count):
    shape = (count, next(part for part in parts if part is not None).shape[1])
    at = sublanes(shape)
    out = jnp.zeros(shape, F32)
    for i, part in enumerate(parts):
        if part is not None:
            out = jnp.where(at == i, part, out)
    return out


def to_rows(columns):
    shape = (columns[0].shape[0], 128)
    at = lanes(shape)
    out = jnp.zeros(shape, F32)
    for i, column in enumerate(columns):
        out = jnp.where(at == i, column, out)
    return out.T[0:8]


def to_columns(rows):
    wide = rows_of(rows, 128).T
    return [wide[:, i : i + 1] for i in range(len(rows))]


def left(v, amount, width):
    return pltpu.roll(v, lax.rem(width - amount, width), 1)


class Place:
    def __getitem__(self, axis):
        return lax.axis_index(("wide", "narrow")[axis])


def call(kernel, outs, *operands, scratch=(), limit=24, final=False, held=True, us=0.0, alias=None):
    whole = pl.BlockSpec(memory_space=pltpu.VMEM)
    space = pltpu.VMEM if held else pltpu.HBM
    placed = [pltpu.with_memory_space_constraint(a, space) for a in operands]
    return pl.pallas_call(
        kernel,
        out_shape=[jax.ShapeDtypeStruct(s, d) if final else pltpu.VMEM(s, d) for s, d in outs],
        in_specs=[whole for _ in operands],
        out_specs=[whole for _ in outs],
        scratch_shapes=[pltpu.VMEM(s, d) for s, d in scratch],
        compiler_params=pltpu.CompilerParams(vmem_limit_bytes=limit << 20),
        cost_estimate=pl.CostEstimate(
            flops=int(us * 1e9), transcendentals=0, bytes_accessed=int(us * 3.6e6)
        ),
        input_output_aliases=alias or {},
        name=kernel.__name__,
    )(*placed)


def offset_of(off, pattern, head):
    row = off[pattern : pattern + 1, :].astype(F32)
    return jnp.sum(jnp.where(lanes(row.shape) == head, row, 0.0), axis=1, keepdims=True)


def after(value, *others):
    return lax.optimization_barrier((value, *others))[0]


def prep_kernel(
    wqkv, win, wattn, gains, biases, gffn, bffn, tok, cot, wout, tok_out, cot_out, wout_out,
    b0, b1, b2, b3, small, qs, is_,
):
    idx = Place()
    n = idx[1]
    tok_out[...] = tok[...]
    cot_out[...] = cot[...]
    wout_out[...] = wout[...]
    small[...] = jnp.zeros_like(small)
    small[0:3, 0:24] = gains[...].astype(F32)
    small[3:10, 0:24] = biases[...].astype(F32)
    ffn_g = gffn[...].astype(F32)
    ffn_b = bffn[...].astype(F32)
    for k in range(4):
        small[16 + 8 * k : 17 + 8 * k, 0:24] = ffn_g[:, k * 24 : k * 24 + 24]
        small[17 + 8 * k : 19 + 8 * k, 0:24] = ffn_b[:, k * 24 : k * 24 + 24]
    eye = (sublanes((24, 128)) == lanes((24, 128))).astype(BF16)
    params = nt(eye, small[...].astype(BF16))
    weights = wqkv[...].astype(F32)
    for m in range(4):
        for part in range(3):
            at = part * 768 + m * 192
            qs[m, :, part * 192 : part * 192 + 192] = weights[:, at : at + 192]
        qs[m, :, 576:640] = params
    inner = win[...].astype(F32)
    for m in range(4):
        for w in range(8):
            at = (w * 4 + m) * 96
            is_[m, :, w * 96 : w * 96 + 96] = inner[:, at : at + 96]
    for k, out in enumerate((b0, b1, b2, b3)):
        out[:, 0:640] = qs[n ^ k].astype(BF16)
        out[:, 640:1408] = is_[n ^ k].astype(BF16)
        if k % 2 == 0:
            out[:, 1408:2176] = wattn[...]


def pack_kernel(b0, b1, b2, b3, q_out, r_out, qs, is_, two):
    idx = Place()
    n = idx[1]
    for k, b in enumerate((b0, b1, b2, b3)):
        qs[n ^ k] = b[:, 0:640].astype(F32)
        is_[n ^ k] = b[:, 640:1408].astype(F32)
        if k % 2 == 0:
            two[(n ^ k) // 2] = b[:, 1408:2176].astype(F32)
    q_out[...] = qs[...].reshape(96, 640).astype(BF16)
    r_out[0:96] = is_[...].reshape(96, 768).astype(BF16)
    r_out[96:144] = two[...].reshape(48, 768).astype(BF16)


def place_i_kernel(r0, r1, r2, r3, r4, r5, r6, win, attn):
    idx = Place()
    w = idx[0]
    for j, r in enumerate((r0, r1, r2, r3, r4, r5, r6)):
        win[pl.ds(pl.multiple_of((w ^ j) * 96, 32), 96), :] = r[0:96]
        attn[j] = r[96:144]


def merge_cores(mine, other, core, buf):
    for x_ in range(2):
        buf[x_ * 2 + core] = mine[x_ * 24 : x_ * 24 + 24].astype(F32)
        buf[x_ * 2 + 1 - core] = other[x_ * 24 : x_ * 24 + 24].astype(F32)
    return buf[...].reshape(96, 768).astype(BF16)


def place_a_kernel(mine, other, wattn, buf):
    idx = Place()
    w, core = idx[0], lax.rem(idx[1], 2)
    for j in range(7):
        block = merge_cores(mine[j], other[j], core, buf)
        wattn[pl.ds(pl.multiple_of((w ^ j) * 96, 32), 96), :] = block


def place_last_kernel(win_in, wattn_in, mine, other, win, wattn, buf):
    idx = Place()
    here = pl.ds(pl.multiple_of((idx[0] ^ 7) * 96, 32), 96)
    win[here, :] = mine[0:96]
    block = merge_cores(mine[96:144], other[96:144], lax.rem(idx[1], 2), buf)
    wattn[here, :] = block


def place_c_kernel(r0, r1, r2, r3, r4, r5, r6, wout):
    idx = Place()
    w = idx[0]
    for j, r in enumerate((r0, r1, r2, r3, r4, r5, r6)):
        wout[pl.ds(pl.multiple_of((w ^ j) * 96, 32), 96), :] = r[...]


def place_c_last_kernel(wout_in, block, wout):
    idx = Place()
    wout[pl.ds(pl.multiple_of((idx[0] ^ 7) * 96, 32), 96), :] = block[...]


def place_t_kernel(t0, t1, t2, t3, out):
    idx = Place()
    n = idx[1]
    for k, t in enumerate((t0, t1, t2, t3)):
        out[pl.ds(pl.multiple_of((n ^ k) * 128, 128), 128), :] = t[...]


def norm_kernel(x, n_out):
    n_out[...], _ = normed(x[...].astype(F32))


def attend_kernel(
    off, n1, q0, q1, q2, q3, q4, q5, q6, q7,
    w_out, p_out, a_out, qkv_out, o_t_out, lse_out, o_out,
):
    idx = Place()
    w, n = idx[0], idx[1]
    for j, q in enumerate((q0, q1, q2, q3, q4, q5, q6, q7)):
        w_out[pl.ds(pl.multiple_of((w ^ j) * 96, 32), 96), :] = q[...]
    pick = (sublanes((64, 128)) + 64 == lanes((64, 128))).astype(BF16)
    table = nt(pick, w_out[:, 512:640])
    model = table[0:16]
    ffn = jnp.zeros((8, 768), F32)
    inside = lax.rem(lanes((8, 768)), 96) // 24
    for k in range(4):
        turned = pltpu.roll(table[16 + 8 * k : 24 + 8 * k], lax.rem(768 + (k - n) * 24, 768), 1)
        ffn = jnp.where(inside == k, turned, ffn)
    p_out[0:16] = model
    p_out[16:24] = ffn
    a1 = (n1[...] * model[0:1] + model[3:4]).astype(BF16)
    a_out[...] = a1
    qkv = nn(a1, w_out[...])
    lane = lanes((8, 768))
    bias_q = left(jnp.broadcast_to(model[4:5], (8, 768)), n * 192, 768)
    bias_v = pltpu.roll(
        jnp.broadcast_to(model[5:6], (8, 768)), lax.rem(768 + 384 - n * 192, 768), 1
    )
    bias = jnp.where(
        lane < 192, bias_q, jnp.where((lane >= 384) & (lane < 576), bias_v, 0.0)
    )[0:1, 0:640]
    qkv = jnp.where(lanes((1, 640)) < 576, qkv + bias, 0.0).astype(BF16)
    qkv_out[...] = qkv
    v_t = qkv[:, 384:576].astype(F32).T
    o_parts, lse_rows = [], []
    for h in range(3):
        head = n * 3 + h
        o1, o2 = offset_of(off, 1, head), offset_of(off, 2, head)
        at = lanes((1, 512))
        r1 = (lax.rem(at, 2).astype(F32) == o1).astype(F32)
        r2 = (lax.rem(at, 4).astype(F32) == o2).astype(F32)
        head_v = v_t[h * 64 : h * 64 + 64]
        ones = rows_of([jnp.ones((1, 512), F32), r1, r2], 8)
        left_side = jnp.concatenate([head_v, head_v * r1, head_v * r2, ones], axis=0).astype(BF16)
        head_q = qkv[:, h * 64 : h * 64 + 64] * jnp.asarray(SCORE_SCALE, BF16)
        head_k = qkv[:, 192 + h * 64 : 256 + h * 64]
        blocks, lses = [], []
        for i in range(2):
            keys = 256 * (i + 1)
            scores = nt(head_k[0:keys], head_q[i * 256 : i * 256 + 256])
            shape = (keys, 256)
            scores = jnp.where(sublanes(shape) <= lanes(shape) + i * 256, scores, MASKED)
            peak = jnp.max(scores, axis=0, keepdims=True)
            weight = jnp.exp(scores - peak).astype(BF16)
            both = nn(left_side[:, 0:keys], weight)
            s1, s2 = r1[:, i * 256 : i * 256 + 256], r2[:, i * 256 : i * 256 + 256]
            total = both[192:193] + s1 * both[193:194] + s2 * both[194:195]
            blocks.append((both[0:64] + s1 * both[64:128] + s2 * both[128:192]) / total)
            lses.append(peak + jnp.log(total))
        o_parts.append(jnp.concatenate(blocks, axis=1))
        lse_rows.append(jnp.concatenate(lses, axis=1))
    o_t = jnp.concatenate(o_parts, axis=0)
    o_t_out[...] = o_t
    lse_out[...] = rows_of(lse_rows, 8)
    o_out[...] = o_t.T.astype(BF16)


def sub_norm_kernel(p, o0, o1, o2, o3, n_o_out, rate_o_out, u_out, o_buf):
    idx = Place()
    n = idx[1]
    for k, o in enumerate((o0, o1, o2, o3)):
        o_buf[n ^ k] = o[...].astype(F32)
    o = jnp.concatenate([o_buf[m] for m in range(4)], axis=1)
    n_o, rate_o = normed(o)
    n_o_out[...] = n_o
    rate_o_out[...] = rate_o
    u_out[...] = (n_o * p[1:2] + p[6:7]).astype(BF16)


def middle_kernel(x, p, u, wattn, win, x2_out, h2_out, f_out, dg_out, stat_out):
    x2 = x[...].astype(F32) + nn(u[...], wattn[...]) + p[7:8]
    x2_out[...] = x2
    n2, _ = normed(x2)
    h2 = (n2 * p[2:3] + p[8:9]).astype(BF16)
    h2_out[...] = h2
    c = nn(h2, win[...]) + p[17:18]
    half = 0.5 + 0.5 * erf(c * 0.7071067811865476)
    f = c * half
    f_out[...] = f
    dg_out[...] = half + c * jnp.exp(c * c * -0.5) * 0.3989422804014327
    mean = jnp.mean(f, axis=1, keepdims=True)
    centred = f - mean
    stat_out[...] = to_rows([mean, jnp.sum(centred * centred, axis=1, keepdims=True)])


def cot_kernel(gy, wout, p, f, stat_in, e_out, stat_out):
    e = nt(gy[...], wout[...])
    e_out[...] = e
    t = e * p[16:17]
    mean = to_columns([stat_in[0:1]])[0]
    rows = to_rows(
        [jnp.sum(t, axis=1, keepdims=True), jnp.sum(t * (f[...] - mean), axis=1, keepdims=True)]
    )
    stat_out[...] = jnp.where(sublanes((8, 512)) < 2, stat_in[...], jnp.roll(rows, 2, axis=0))


def ffn_columns(s0, s1, s2, s3):
    parts = [s[...] for s in (s0, s1, s2, s3)]
    count = 768.0 * 4
    mean = sum(s[0:1] for s in parts) * 0.25
    spread = sum(s[1:2] + 768.0 * (s[0:1] - mean) * (s[0:1] - mean) for s in parts) / count
    rate = lax.rsqrt(spread + EPSILON)
    mean_t = sum(s[2:3] for s in parts) / count
    mean_tn = rate * sum(s[3:4] + (s[0:1] - mean) * s[2:3] for s in parts) / count
    return to_columns([mean, rate, mean_t, mean_tn])


def core_halves(value, keep, send, core, buf):
    buf[...] = value
    for x_ in range(2):
        mine = pl.ds(pl.multiple_of((x_ * 2 + core) * 128, 128), 128)
        other = pl.ds(pl.multiple_of((x_ * 2 + 1 - core) * 128, 128), 128)
        keep[x_ * 128 : x_ * 128 + 128, :] = buf[mine, :].astype(keep.dtype)
        send[x_ * 128 : x_ * 128 + 128, :] = buf[other, :].astype(send.dtype)


def ffn_back_kernel(p, s0, s1, s2, s3, f, dg, e, win, gc_out, keep, send, buf):
    idx = Place()
    core = lax.rem(idx[1], 2)
    mean, rate, mean_t, mean_tn = ffn_columns(s0, s1, s2, s3)
    n_f = (f[...] - mean) * rate
    df = rate * (e[...] * p[16:17] - mean_t - n_f * mean_tn)
    gc = (df * dg[...]).astype(BF16)
    gc_out[...] = gc
    core_halves(nt(gc, win[...]), keep, send, core, buf)


def by_wide(value, w, steps, out):
    for i, step in enumerate(steps):
        out[i] = value[pl.ds(pl.multiple_of((w ^ step) * 96, 32), 96), :].astype(BF16)


def ffn_grad_kernel(
    p, s0, s1, s2, s3, f, e, gy, z_out, keep_a, keep_b, send_a, send_b, sums, prod
):
    idx = Place()
    mean, rate, _, _ = ffn_columns(s0, s1, s2, s3)
    n_f = (f[...] - mean) * rate
    z = (n_f * p[16:17] + p[18:19]).astype(BF16)
    z_out[...] = z
    prod[...] = tn(z, gy[...])
    for steps, out in (((2, 6), keep_a), ((0, 4), keep_b), ((3, 7), send_a), ((1, 5), send_b)):
        by_wide(prod, idx[0], steps, out)
    sums[...] = rows_of([colsum(e[...] * n_f), None, colsum(e[...]), None], 8)


def in_grad_kernel(h2, gc, keep_a, keep_b, send_a, send_b, prod):
    idx = Place()
    prod[...] = tn(h2[...], gc[...])
    for steps, out in (((4, 5), keep_a), ((0, 1), keep_b), ((6, 7), send_a), ((2, 3), send_b)):
        by_wide(prod, idx[0], steps, out)


def out_kernel(z, wout, gc, gy, sums_in, keep, send, sums, buf):
    idx = Place()
    core_halves(nn(z[...], wout[...]), keep, send, lax.rem(idx[1], 2), buf)
    extra = rows_of([None, colsum(gc[...].astype(F32)), None, colsum(gy[...].astype(F32))], 8)
    sums[...] = sums_in[...] + extra


def prob_kernel(qkv, lse, *outs):
    for h in range(3):
        low_q = qkv[:, h * 64 : h * 64 + 64] * jnp.asarray(SCORE_SCALE, BF16)
        head_k = qkv[:, 192 + h * 64 : 256 + h * 64]
        for i in range(2):
            keys = 256 * (i + 1)
            here = slice(i * 256, i * 256 + 256)
            shape = (keys, 256)
            scores = nt(head_k[0:keys], low_q[here])
            outs[i][h] = jnp.where(
                sublanes(shape) <= lanes(shape) + i * 256,
                jnp.exp(scores - lse[h : h + 1, here]),
                0.0,
            )


def norm_two_kernel(x2, n2_out, rate_out):
    n2_out[...], rate_out[...] = normed(x2[...])


def add_kernel(keep, got, out):
    out[...] = (keep[...].astype(F32) + got[...].astype(F32)).astype(out.dtype)


def hop_kernel(keep, got, own, send):
    for i in range(2):
        own[i] = keep[2 * i].astype(F32) + got[2 * i].astype(F32)
        send[i] = (keep[2 * i + 1].astype(F32) + got[2 * i + 1].astype(F32)).astype(BF16)


def pair_kernel(keep, got, out):
    for i in range(2):
        out[i] = (keep[i].astype(F32) + got[i].astype(F32)).astype(out.dtype)


def split_kernel(keep, got, first, second):
    first[...] = (keep[0].astype(F32) + got[0].astype(F32)).astype(first.dtype)
    second[...] = (keep[1].astype(F32) + got[1].astype(F32)).astype(second.dtype)


def last_hop_kernel(own, got, mine, send):
    mine[...] = own[0] + got[0].astype(F32)
    send[...] = (own[1] + got[1].astype(F32)).astype(BF16)


def sum_out_kernel(mine, got, out):
    out[...] = mine[...] + got[...].astype(F32)


def mid_back_kernel(
    p, own, own_x, sib, sib_x, n2, rate2, gy, n_o, rate_o, wattn,
    dx2_out, ga_out, do_out, e2_out, eo_out,
):
    idx = Place()
    n = idx[1]
    core = lax.rem(n, 2)
    for x_ in range(2):
        at = slice(x_ * 128, x_ * 128 + 128)
        mine = pl.ds(pl.multiple_of((x_ * 2 + core) * 128, 128), 128)
        other = pl.ds(pl.multiple_of((x_ * 2 + 1 - core) * 128, 128), 128)
        e2_out[mine, :] = own[at].astype(F32) + own_x[at].astype(F32)
        e2_out[other, :] = sib[at].astype(F32) + sib_x[at].astype(F32)
    dx2 = gy[...].astype(F32) + norm_back(e2_out[...], n2[...], rate2[...], p[2:3])
    dx2_out[...] = dx2
    ga = dx2.astype(BF16)
    ga_out[...] = ga
    eo = nt(ga, wattn[...])
    eo_out[...] = eo
    d_o = norm_back(eo, n_o[...], rate_o[...], p[1:2])
    for m in range(4):
        @pl.when(n == m)
        def _():
            do_out[...] = d_o[:, m * 192 : m * 192 + 192].astype(BF16)


def attn_grad_kernel(u, ga, eo, n_o, e2, n2, sums, keep, send, gat):
    idx = Place()
    w, n = idx[0], idx[1]
    e_o, e_2 = eo[...], e2[...]
    model = rows_of(
        [
            None,
            colsum(e_o * n_o[...]),
            colsum(e_2 * n2[...]),
            None,
            None,
            None,
            colsum(e_o),
            colsum(ga[...].astype(F32)),
            colsum(e_2),
            sums[3:4],
        ],
        16,
    )
    gat[...] = tn(u[...], ga[...]).reshape(8, 4, 24, 768)
    for i in range(8):
        to = w ^ i
        block = (keep if i % 2 == 0 else send).at[i // 2]
        mine = left(model, to * 96 + n * 24, 768)
        ffn = left(sums[...], to * 96, 768)
        extra = jnp.concatenate(
            [mine[0:8, 0:128], mine[8:16, 0:128], ffn[:, 0:128], jnp.zeros((8, 384), F32)], axis=1
        )
        block[...] = jnp.concatenate([gat[to, n], extra], axis=0).astype(BF16)


def head_back_kernel(
    off, qkv, o_t, p0, p1, do, a1, wqkv, n1,
    keep_a, keep_b, send_a, send_b, d_keep, d_send, buf, prod,
):
    idx = Place()
    w, n = idx[0], idx[1]
    core = lax.rem(n, 2)
    do_t = do[...].astype(F32).T
    k_t = qkv[:, 192:384].astype(F32).T
    row = lanes((1, 512))
    column = sublanes((512, 1))
    dq_parts, dk_parts, dv_parts = [], [], []
    for h in range(3):
        head = n * 3 + h
        o1, o2 = offset_of(off, 1, head), offset_of(off, 2, head)
        r1 = (lax.rem(row, 2).astype(F32) == o1).astype(F32)
        r2 = (lax.rem(row, 4).astype(F32) == o2).astype(F32)
        c1 = (lax.rem(column, 2).astype(F32) == o1).astype(F32)
        c2 = (lax.rem(column, 4).astype(F32) == o2).astype(F32)
        span = slice(h * 64, h * 64 + 64)
        delta = colsum(do_t[span] * o_t[span, :])
        head_q = qkv[:, h * 64 : h * 64 + 64].astype(F32) * SCORE_SCALE
        head_v = qkv[:, 384 + h * 64 : 448 + h * 64]
        head_do = do[:, h * 64 : h * 64 + 64]
        do_f = head_do.astype(F32)
        q_all = jnp.concatenate([head_q, head_q * c1, head_q * c2], axis=1).astype(BF16)
        do_all = jnp.concatenate([do_f, do_f * c1, do_f * c2], axis=1).astype(BF16)
        kt = k_t[span]
        k_all = jnp.concatenate([kt, kt * r1, kt * r2], axis=0).astype(BF16)
        dk = jnp.zeros((512, 192), F32)
        dv = jnp.zeros((512, 192), F32)
        dq_blocks = []
        for i in range(2):
            keys = 256 * (i + 1)
            here = slice(i * 256, i * 256 + 256)
            prob = (p0, p1)[i][h]
            grad_p = nt(head_v[0:keys], head_do[here])
            grad_s = (prob * (grad_p - delta[:, here])).astype(BF16)
            dv_i = nn(prob.astype(BF16), do_all[here])
            dk_i = nn(grad_s, q_all[here])
            if keys < 512:
                zero = jnp.zeros((512 - keys, 192), F32)
                dv_i = jnp.concatenate([dv_i, zero], axis=0)
                dk_i = jnp.concatenate([dk_i, zero], axis=0)
            dv = dv + dv_i
            dk = dk + dk_i
            dq_i = nn(k_all[:, 0:keys], grad_s)
            dq_blocks.append(dq_i[0:64] + r1[:, here] * dq_i[64:128] + r2[:, here] * dq_i[128:192])
        dq_parts.append(jnp.concatenate(dq_blocks, axis=1) * SCORE_SCALE)
        dk_parts.append(dk[:, 0:64] + c1 * dk[:, 64:128] + c2 * dk[:, 128:192])
        dv_parts.append(dv[:, 0:64] + c1 * dv[:, 64:128] + c2 * dv[:, 128:192])
    dq = jnp.concatenate(dq_parts, axis=0).T
    g = jnp.concatenate([dq] + dk_parts + dv_parts + [jnp.zeros((512, 64), F32)], axis=1)
    g = g.astype(BF16)
    prod[...] = tn(a1[...], g)
    grad = nt(g, wqkv[...])
    outer = rows_of([None, colsum(grad * n1[...]), colsum(grad)], 8)
    g_sum = colsum(g.astype(F32))
    for i in range(8):
        to = w ^ i
        block = ((keep_b, keep_a), (send_b, send_a))[i % 2][i // 2 % 2].at[i // 4]
        turned = left(outer, to * 96, 768)[:, 0:640]
        extra = jnp.where(sublanes((8, 640)) == 0, g_sum, turned)
        mine = prod[pl.ds(pl.multiple_of(to * 96, 32), 96), :]
        block[...] = jnp.concatenate([mine, extra], axis=0).astype(BF16)
    core_halves(grad, d_keep, d_send, core, buf)


def tail_add_kernel(ok, og, dk, dg, keep, send, buf):
    idx = Place()
    x_ = idx[1] // 2
    buf[:, 0:768] = ok[...].astype(F32) + og[...].astype(F32)
    buf[:, 768:1536] = dk[...].astype(F32) + dg[...].astype(F32)
    keep[...] = buf[pl.ds(pl.multiple_of(x_ * 128, 128), 128), :]
    send[...] = buf[pl.ds(pl.multiple_of((1 - x_) * 128, 128), 128), :].astype(BF16)


def token_kernel(p, keep, got, tok, x2, dx2, out, grad):
    idx = Place()
    mine = pl.ds(pl.multiple_of(idx[1] * 128, 128), 128)
    both = keep[...] + got[...].astype(F32)
    out[...] = (x2[mine, :] + both[:, 0:768] + p[9:10]).astype(BF16)
    n1, rate = normed(tok[...].astype(F32))
    grad[...] = dx2[mine, :] + norm_back(both[:, 768:1536], n1, rate, p[0:1])


def sum_in_kernel(mine, got, own, t1, t2, t3, buf):
    idx = Place()
    n = idx[1]
    buf[...] = (mine[...] + got[...].astype(F32)).reshape(4, 24, 768)
    own[...] = buf[n]
    for k, out in enumerate((t1, t2, t3)):
        out[...] = buf[n ^ (k + 1)].astype(BF16)


def sum_qkv_kernel(mine, z1, z2, z3, own, t1, t2, t3, buf):
    idx = Place()
    n = idx[1]
    total = mine[...] + z1[...].astype(F32) + z2[...].astype(F32) + z3[...].astype(F32)
    buf[...] = total[0:96].reshape(4, 24, 640)
    own[0:24] = buf[n]
    own[24:32] = total[96:104]
    for k, out in enumerate((t1, t2, t3)):
        out[...] = jnp.concatenate([buf[n ^ (k + 1)], total[96:104]], axis=0).astype(BF16)


def final_in_kernel(i0, i1, i2, i3, out, buf):
    idx = Place()
    n = idx[1]
    for k, i in enumerate((i0, i1, i2, i3)):
        buf[n ^ k] = i[...].astype(F32)
    for m in range(4):
        block = buf[m]
        for w in range(8):
            at = (w * 4 + m) * 96
            out[:, at : at + 96] = block[:, w * 96 : w * 96 + 96]


def final_kernel(q0, q1, q2, q3, a_mine, a_got, gq, gattn, gains, biases, gffn, bffn, buf):
    idx = Place()
    w, n = idx[0], idx[1]
    total = a_mine[...] + a_got[...].astype(F32)
    gattn[...] = total[0:24]
    extra = total[24:32]
    for k, q in enumerate((q0, q1, q2, q3)):
        buf[n ^ k] = q[...].astype(F32)
    for m in range(4):
        block = buf[m]
        for part in range(3):
            at = part * 768 + m * 192
            gq[:, at : at + 192] = block[0:24, part * 192 : part * 192 + 192]
    tails = [buf[m][24:32] for m in range(4)]
    q_row = jnp.concatenate([t[:, 0:192] for t in tails], axis=1)
    v_row = jnp.concatenate([t[:, 384:576] for t in tails], axis=1)
    place = (w * 4 + n) * 24
    q_row = left(q_row, place, 768)[0:1, 0:24]
    v_row = left(v_row, place, 768)[0:1, 0:24]
    norm = left((tails[0] + tails[1] + tails[2] + tails[3])[:, 0:128], n * 24, 128)[:, 0:24]
    low, high, ffn = extra[:, 0:24], extra[:, 128:152], extra[:, 256:352]
    gains[0:1] = norm[1:2]
    gains[1:3] = low[1:3]
    biases[0:1] = norm[2:3]
    biases[1:2] = q_row
    biases[2:3] = v_row
    biases[3:5] = low[6:8]
    biases[5:7] = high[0:2]
    gffn[...] = ffn[0:1]
    bffn[...] = ffn[1:3]


def swap(values, axis, size, step):
    return lax.ppermute(values, axis, [(i, i ^ step) for i in range(size)])


def Y(v):
    return swap(v, "wide", 8, 1)


def Z1(v):
    return swap(v, "wide", 8, 2)


def Z2(v):
    return swap(v, "wide", 8, 4)


def Z3(v):
    return swap(v, "wide", 8, 6)


def C(v):
    return swap(v, "narrow", 4, 1)


def X(v):
    return swap(v, "narrow", 4, 2)


def XC(v):
    return swap(v, "narrow", 4, 3)


class Names:
    def __getattr__(self, name):
        return name


N = Names()
TABLE = (
    (N.cy, 1, 4), (N.ry, 4, 6), (N.b1, 0, 2), (N.b3, 0, 2), (N.qy, 2, 4), (N.b2, 0, 0), (N.q2y, 4, 6),
    (N.pack, 2, 5), (N.q1, 2, 4), (N.txc, 6, 0), (N.q2, 2, 6), (N.tc, 2, 6), (N.q1y, 4, 5), (N.x, 6, 10),
    (N.r1, 4, 6), (N.gx, 6, 8), (N.tx, 4, 6), (N.r1y, 6, 7), (N.c2y, 6, 9), (N.n1, 6, 14), (N.c1, 3, 7),
    (N.q3, 4, 6), (N.c2, 6, 0), (N.r2, 4, 6), (N.r3, 6, 7), (N.q3y, 4, 0), (N.c3, 6, 10), (N.c1y, 6, 10),
    (N.ox, 8, 10), (N.r3y, 6, 10), (N.oc, 10, 0), (N.c3y, 11, 14), (N.gy, 8, 17), (N.attend, 6, 8),
    (N.place_i, 7, 9), (N.gxc, 8, 0), (N.ac, 10, 0), (N.r2y, 6, 7), (N.gc, 8, 0), (N.sub, 10, 13),
    (N.place_l, 10, 0), (N.oxc, 10, 0), (N.place_a, 10, 0), (N.middle, 10, 18), (N.s3, 14, 0),
    (N.s2, 14, 15), (N.dx, 17, 18), (N.dc, 14, 0), (N.r3yc, 10, 0), (N.place_c, 12, 14),
    (N.place_cl, 14, 0), (N.ffn_back, 14, 0), (N.s1, 14, 0), (N.e, 14, 0), (N.in_grad, 14, 0),
    (N.add, 16, 0), (N.ds, 18, 0), (N.n2, 18, 19), (N.ffn_grad, 15, 0), (N.out, 16, 20), (N.out_b, 18, 20),
    (N.dxc, 18, 0), (N.prob, 19, 0), (N.in_a, 16, 18), (N.mid, 18, 20), (N.opc, 18, 19), (N.out_z, 20, 22),
    (N.in_b, 17, 20), (N.in_on, 18, 19), (N.qa, 20, 0), (N.out_on, 18, 20), (N.qb, 20, 0), (N.out_a, 16, 0),
    (N.qz1, 20, 0), (N.split_b, 20, 21), (N.out_own, 18, 22), (N.in_own, 20, 0), (N.at_y, 19, 22),
    (N.qz3, 20, 0), (N.split_a, 20, 0), (N.attn_grad, 19, 0), (N.head, 19, 0), (N.in_z, 20, 0),
    (N.out_last, 22, 0), (N.tail, 20, 0), (N.qz2, 20, 24), (N.tail_add, 20, 0), (N.in_y, 22, 0),
    (N.out_z2, 22, 0), (N.token, 22, 27), (N.at_hop, 22, 0), (N.tc_g, 20, 0), (N.at_z2, 23, 0),
    (N.n2q, 23, 25), (N.sum_out, 25, 26), (N.at_last, 22, 25), (N.i3, 22, 0), (N.at_z1, 22, 0),
    (N.in_last, 20, 0), (N.n1q, 21, 25), (N.sum_qkv, 21, 0), (N.n3q, 24, 27), (N.sum_in, 22, 0),
    (N.i1, 22, 0), (N.i2, 22, 0), (N.final_in, 22, 28), (N.final, 32, 0),
)


def steps(env):
    offsets = env[N.offsets]
    two, two_f = ((2, 96, 768), BF16), ((2, 96, 768), F32)
    full, full_f, half, half_f = (
        ((512, 768), BF16), ((512, 768), F32), ((256, 768), BF16), ((256, 768), F32),
    )
    sq = ((768, 768), BF16)
    blk, blk2 = ((104, 640), BF16), ((2, 104, 640), BF16)

    def kernel(name, body, outs, ins, lead=(), results=None, **keys):
        results = results or (name,)
        table[name] = (
            tuple(ins), results, lambda *a: call(body, outs, *lead, *a, us=COST.get(name, 0.0), **keys)
        )

    def move(name, how, source):
        table[name] = ((source,), (name,), lambda a: (how(a),))

    table = {}
    for name, how, source in (
        (N.b1, C, N.b1_s), (N.b2, X, N.b2_s), (N.b3, XC, N.b3_s), (N.cy, Y, N.w_out),
        (N.qy, Y, N.q), (N.q1, Z1, N.q), (N.q2, Z2, N.q), (N.q3, Z1, N.q2), (N.q1y, Y, N.q1),
        (N.q2y, Y, N.q2), (N.q3y, Y, N.q3), (N.ry, Y, N.r), (N.r1, Z1, N.r), (N.r2, Z2, N.r),
        (N.r3, Z1, N.r2), (N.r1y, Y, N.r1), (N.r2y, Y, N.r2), (N.r3y, Z1, N.r2y),
        (N.c1, Z1, N.w_out), (N.c2, Z2, N.w_out), (N.c3, Z1, N.c2), (N.c1y, Y, N.c1),
        (N.c2y, Y, N.c2), (N.c3y, Y, N.c3), (N.tc, C, N.tokens), (N.tx, X, N.tokens), (N.txc, C, N.tx),
        (N.gc, C, N.cotangent), (N.gx, X, N.cotangent), (N.gxc, C, N.gx),
        (N.oc, C, N.o_low), (N.ox, X, N.o_low), (N.oxc, C, N.ox), (N.ac, C, N.attn), (N.r3yc, C, N.r3y),
        (N.s1, C, N.stats), (N.s2, X, N.stats), (N.s3, XC, N.stats), (N.dc, C, N.d_send),
        (N.dx, X, N.d_half), (N.ds, C, N.d_half), (N.dxc, C, N.dx), (N.out_a, Y, N.out_sa),
        (N.out_b, Y, N.out_sb), (N.in_a, Z1, N.in_sa), (N.in_b, Z1, N.in_sb), (N.opc, C, N.op_send),
        (N.qa, Y, N.qkv_a), (N.qb, Y, N.qkv_b), (N.out_z, Z1, N.out_on), (N.in_z, Z2, N.in_on),
        (N.tc_g, C, N.t_send), (N.at_y, Y, N.at_send), (N.qz1, Z1, N.send_1), (N.qz2, Z2, N.send_2),
        (N.qz3, Z3, N.send_3), (N.out_z2, Z2, N.out_to), (N.tail, X, N.tail_send), (N.in_y, Y, N.in_to),
        (N.at_z1, Z1, N.at_on), (N.at_z2, Z2, N.at_to), (N.i1, C, N.i1_s), (N.i2, X, N.i2_s),
        (N.i3, XC, N.i3_s), (N.n1q, C, N.n1_s), (N.n2q, X, N.n2_s), (N.n3q, XC, N.n3_s),
    ):
        move(name, how, source)
    kernel(
        N.pack, pack_kernel, [((96, 640), BF16), ((144, 768), BF16)], (N.b0, N.b1, N.b2, N.b3), (), (N.q, N.r),
        scratch=[((4, 24, 640), F32), ((4, 24, 768), F32), ((2, 24, 768), F32)],
    )
    kernel(N.x, place_t_kernel, [full], (N.tokens, N.tc, N.tx, N.txc))
    kernel(N.n1, norm_kernel, [full_f], (N.x,))
    kernel(
        N.attend, attend_kernel,
        [
            ((768, 640), BF16), ((24, 768), F32), full, ((512, 640), BF16), ((192, 512), F32),
            ((8, 512), F32), ((512, 192), BF16),
        ],
        (N.n1, N.q, N.qy, N.q1, N.q1y, N.q2, N.q2y, N.q3, N.q3y), (offsets,),
        (N.wqkv, N.params, N.a1, N.qkv, N.o_t, N.lse, N.o_low),
    )
    kernel(N.gy, place_t_kernel, [full], (N.cotangent, N.gc, N.gx, N.gxc))
    kernel(
        N.place_i, place_i_kernel, [sq, ((7, 48, 768), BF16)], (N.r, N.ry, N.r1, N.r1y, N.r2, N.r2y, N.r3), (),
        (N.win_7, N.attn),
    )
    kernel(N.place_a, place_a_kernel, [sq], (N.attn, N.ac), (), (N.wattn_7,), scratch=[((4, 24, 768), F32)])
    kernel(
        N.place_l, place_last_kernel, [sq, sq], (N.win_7, N.wattn_7, N.r3y, N.r3yc), (), (N.win, N.wattn),
        scratch=[((4, 24, 768), F32)], alias={0: 0, 1: 1},
    )
    kernel(
        N.sub, sub_norm_kernel, [full_f, ((512, 1), F32), full], (N.params, N.o_low, N.oc, N.ox, N.oxc), (),
        (N.n_o, N.rate_o, N.u), scratch=[((4, 512, 192), F32)],
    )
    kernel(
        N.middle, middle_kernel, [full_f, full, full_f, full_f, ((8, 512), F32)],
        (N.x, N.params, N.u, N.wattn, N.win), (), (N.x2, N.h2, N.f, N.dg, N.stat_f),
    )
    kernel(
        N.place_c, place_c_kernel, [sq], (N.w_out, N.cy, N.c1, N.c1y, N.c2, N.c2y, N.c3), (), (N.wout_7,)
    )
    kernel(N.place_cl, place_c_last_kernel, [sq], (N.wout_7, N.c3y), (), (N.wout,), alias={0: 0})
    kernel(
        N.e, cot_kernel, [full_f, ((8, 512), F32)], (N.gy, N.wout, N.params, N.f, N.stat_f), (), (N.e, N.stats)
    )
    stats = (N.params, N.stats, N.s1, N.s2, N.s3)
    kernel(
        N.ffn_back, ffn_back_kernel, [full, half_f, half], (*stats, N.f, N.dg, N.e, N.win), (),
        (N.gc_f, N.d_keep, N.d_send), scratch=[full_f],
    )
    kernel(N.add, add_kernel, [half], (N.d_keep, N.dc), (), (N.d_half,))
    kernel(
        N.ffn_grad, ffn_grad_kernel, [full, two, two, two, two, ((8, 768), F32)],
        (*stats, N.f, N.e, N.gy), (), (N.z, N.out_ka, N.out_kb, N.out_sa, N.out_sb, N.sums_f),
        scratch=[((768, 768), F32)],
    )
    kernel(
        N.in_grad, in_grad_kernel, [two] * 4, (N.h2, N.gc_f), (), (N.in_ka, N.in_kb, N.in_sa, N.in_sb),
        scratch=[((768, 768), F32)],
    )
    kernel(
        N.out, out_kernel, [half_f, half, ((8, 768), F32)], (N.z, N.wout, N.gc_f, N.gy, N.sums_f), (),
        (N.op_keep, N.op_send, N.sums), scratch=[full_f],
    )
    kernel(
        N.prob, prob_kernel, [((3, 256, 256), F32), ((3, 512, 256), F32)], (N.qkv, N.lse), (), (N.p0, N.p1)
    )
    kernel(N.n2, norm_two_kernel, [full_f, ((512, 1), F32)], (N.x2,), (), (N.n2, N.rate2))
    kernel(
        N.mid, mid_back_kernel, [full_f, full, ((512, 192), BF16), full_f, full_f],
        (N.params, N.d_half, N.dx, N.ds, N.dxc, N.n2, N.rate2, N.gy, N.n_o, N.rate_o, N.wattn), (),
        (N.dx2, N.ga, N.do, N.e2, N.eo),
    )
    kernel(
        N.head, head_back_kernel, [blk2, blk2, blk2, blk2, half_f, half],
        (N.qkv, N.o_t, N.p0, N.p1, N.do, N.a1, N.wqkv, N.n1), (offsets,),
        (N.keep_a, N.keep_b, N.qkv_a, N.qkv_b, N.t_keep, N.t_send), scratch=[full_f, ((768, 640), F32)],
    )
    kernel(N.out_on, pair_kernel, [two], (N.out_ka, N.out_a))
    kernel(N.in_on, pair_kernel, [two], (N.in_ka, N.in_a))
    kernel(N.out_own, pair_kernel, [two_f], (N.out_kb, N.out_b))
    kernel(N.in_own, pair_kernel, [two_f], (N.in_kb, N.in_b))
    kernel(
        N.attn_grad, attn_grad_kernel, [((4, 32, 768), BF16)] * 2, (N.u, N.ga, N.eo, N.n_o, N.e2, N.n2, N.sums), (),
        (N.at_keep, N.at_send), scratch=[((8, 4, 24, 768), F32)],
    )
    kernel(N.split_a, split_kernel, [blk, blk], (N.keep_a, N.qa), (), (N.send_1, N.send_3))
    kernel(N.split_b, split_kernel, [((104, 640), F32), blk], (N.keep_b, N.qb), (), (N.q_sum, N.send_2))
    block = [((96, 768), F32), ((96, 768), BF16)]
    kernel(N.out_last, last_hop_kernel, block, (N.out_own, N.out_z), (), (N.out_mine, N.out_to))
    kernel(N.in_last, last_hop_kernel, block, (N.in_own, N.in_z), (), (N.in_mine, N.in_to))
    kernel(
        N.at_hop, hop_kernel, [((2, 32, 768), F32), ((2, 32, 768), BF16)], (N.at_keep, N.at_y), (), (N.at_own, N.at_on)
    )
    kernel(
        N.at_last, last_hop_kernel, [((32, 768), F32), ((32, 768), BF16)], (N.at_own, N.at_z1), (),
        (N.at_mine, N.at_to),
    )
    kernel(
        N.tail_add, tail_add_kernel, [((128, 1536), F32), ((128, 1536), BF16)],
        (N.op_keep, N.opc, N.t_keep, N.tc_g), (), (N.tail_keep, N.tail_send), scratch=[((256, 1536), F32)],
    )
    kernel(
        N.token, token_kernel, [((128, 768), BF16), ((128, 768), F32)],
        (N.params, N.tail_keep, N.tail, N.tokens, N.x2, N.dx2), (), (N.outputs, N.grad_inputs), final=True,
    )
    kernel(
        N.sum_out, sum_out_kernel, [((96, 768), F32)], (N.out_mine, N.out_z2), (), (N.grad_w_out,), final=True
    )
    small = ((24, 768), BF16)
    kernel(
        N.sum_in, sum_in_kernel, [((24, 768), F32), small, small, small], (N.in_mine, N.in_y), (),
        (N.i_own, N.i1_s, N.i2_s, N.i3_s), scratch=[((4, 24, 768), F32)],
    )
    kernel(
        N.final_in, final_in_kernel, [((24, 3072), F32)], (N.i_own, N.i1, N.i2, N.i3), (), (N.grad_w_in,),
        scratch=[((4, 24, 768), F32)], final=True,
    )
    row = ((32, 640), BF16)
    kernel(
        N.sum_qkv, sum_qkv_kernel, [((32, 640), F32), row, row, row], (N.q_sum, N.qz1, N.qz2, N.qz3), (),
        (N.q_mine, N.n1_s, N.n2_s, N.n3_s), scratch=[((4, 24, 640), F32)],
    )
    kernel(
        N.final, final_kernel,
        [
            ((24, 2304), F32), ((24, 768), F32), ((3, 24), F32), ((7, 24), F32), ((1, 96), F32), ((2, 96), F32),
        ],
        (N.q_mine, N.n1q, N.n2q, N.n3q, N.at_mine, N.at_z2), (),
        (N.grad_w_qkv, N.grad_w_attn, N.grad_gains, N.grad_biases, N.grad_gain_ffn, N.grad_ffn_biases),
        scratch=[((4, 32, 640), F32)], final=True,
    )
    return table


COST = dict(attend=8.0, middle=0.3, ffn_back=4.0, ffn_grad=4.0, in_grad=8.0, out=2.0, mid=1.0, attn_grad=8.0)


def fast_body(
    tokens, cotangent, w_qkv, w_attn, w_in, w_out, gains_model, biases_model, gain_ffn, biases_ffn, offsets
):
    env = {N.offsets: offsets}
    first = (N.tokens, N.cotangent, N.w_out, N.b0, N.b1_s, N.b2_s, N.b3_s)
    outs = call(
        prep_kernel,
        [((128, 768), BF16), ((128, 768), BF16), ((96, 768), BF16)]
        + [((24, 2176 if k % 2 == 0 else 1408), BF16) for k in range(4)],
        w_qkv, w_in, w_attn, gains_model, biases_model, gain_ffn[None], biases_ffn,
        tokens, cotangent, w_out,
        scratch=[((64, 128), F32), ((4, 24, 640), F32), ((4, 24, 768), F32)], held=False,
    )
    env.update(zip(first, outs))
    table = steps(env)
    for slot in range(max(at for _, at, _ in TABLE) + 1):
        now = [name for name, at, _ in TABLE if at == slot]
        tied = [r for name, _, done in TABLE if done == slot and done > 0 for r in table[name][1]]
        tied += [v for name in now for v in table[name][0] if v in env]
        tied = list(dict.fromkeys(tied))
        if slot and tied:
            env.update(zip(tied, lax.optimization_barrier(tuple(env[v] for v in tied))))
        while now:
            name = next(n for n in now if all(v in env for v in table[n][0]))
            now.remove(name)
            ins, results, run = table[name]
            env.update(zip(results, run(*(env[v] for v in ins))))
    return (
        env[N.outputs], env[N.grad_inputs], env[N.grad_w_qkv], env[N.grad_w_attn], env[N.grad_w_in],
        env[N.grad_w_out], env[N.grad_gains], env[N.grad_biases], env[N.grad_gain_ffn][0],
        env[N.grad_ffn_biases],
    )


def solution(mesh):
    fast = dict(mesh.shape) == {"wide": 8, "narrow": 4}
    return jax.shard_map(
        fast_body if fast else body,
        mesh=mesh,
        in_specs=(
            P(("wide", "narrow"), None),
            P(("wide", "narrow"), None),
            P(("wide", "narrow"), None),
            P(("wide", "narrow"), None),
            P(("wide", "narrow"), None),
            P(("wide", "narrow"), None),
            P(None, ("wide", "narrow")),
            P(None, ("wide", "narrow")),
            P(("wide", "narrow")),
            P(None, ("wide", "narrow")),
            P(),
        ),
        out_specs=(
            P(("wide", "narrow"), None),
            P(("wide", "narrow"), None),
            P(("wide", "narrow"), None),
            P(("wide", "narrow"), None),
            P(("wide", "narrow"), None),
            P(("wide", "narrow"), None),
            P(None, ("wide", "narrow")),
            P(None, ("wide", "narrow")),
            P(("wide", "narrow")),
            P(None, ("wide", "narrow")),
        ),
        check_vma=False,
    )
```

```python
import jax
import jax.numpy as jnp
from jax import lax
from jax.experimental import pallas as pl
from jax.experimental.pallas import tpu as pltpu
from jax.sharding import PartitionSpec as P

HEADS = 12
HEAD_DIM = 64
RATE0 = 1
RATE1 = 2
RATE2 = 4


EPSILON = 1e-05
SCORE_SCALE = 0.125
MASKED = -1e30


def layer_norm(values, norm_gain, norm_shift):
    average = jnp.mean(values, axis=-1, keepdims=True)
    centred = values - average
    spread = jnp.mean(centred * centred, axis=-1, keepdims=True)
    return centred * lax.rsqrt(spread + EPSILON) * norm_gain + norm_shift


def gelu_exact(values):
    return jax.nn.gelu(values, approximate=False)


def product(former, latter):
    return jnp.dot(former, latter, preferred_element_type=jnp.float32)


def product_tn(former, latter):
    return lax.dot_general(
        former, latter, (((0,), (0,)), ((), ())), preferred_element_type=jnp.float32
    )


def product_nt(former, latter):
    return lax.dot_general(
        former, latter, (((1,), (1,)), ((), ())), preferred_element_type=jnp.float32
    )


def one_hot(offset_row, dilation):
    return (jnp.arange(dilation)[:, None] == offset_row[None, :]).astype(jnp.float32)


def select_rows(dense_rows, selector, dilation):
    picked_rows = dense_rows.shape[0] // dilation
    shaped = dense_rows.reshape(picked_rows, dilation, HEADS, HEAD_DIM)
    picked = jnp.einsum(
        "trhd,rh->thd",
        shaped,
        selector.astype(dense_rows.dtype),
        preferred_element_type=jnp.float32,
    )
    return picked.reshape(picked_rows, HEADS * HEAD_DIM)


def spread_rows(sparse_rows, selector, dilation):
    shaped = sparse_rows.reshape(sparse_rows.shape[0], 1, HEADS, HEAD_DIM)
    placed = shaped * selector[None, :, :, None]
    return placed.reshape(sparse_rows.shape[0] * dilation, HEADS * HEAD_DIM)


def select_heads(dense_heads, selector, dilation):
    shaped = dense_heads.reshape(dense_heads.shape[0] // dilation, dilation, HEADS)
    return jnp.sum(shaped * selector[None], axis=1)


def spread_heads(sparse_heads, selector, dilation):
    placed = jnp.where(selector[None] > 0, sparse_heads[:, None, :], MASKED)
    return placed.reshape(sparse_heads.shape[0] * dilation, HEADS)


def head_major(values):
    return values.reshape(values.shape[0], HEADS, HEAD_DIM).transpose(1, 0, 2)


def row_major(values):
    return values.transpose(1, 0, 2).reshape(values.shape[1], HEADS * HEAD_DIM)


def key_mask(row_count, block_count, own_block):
    query_pos = jnp.arange(row_count)[:, None]
    position = jnp.arange(row_count * block_count)[None, :]
    key_block = position // row_count
    within = position % row_count
    return (key_block < own_block) | (key_block == own_block) & (within <= query_pos)


def masked_scores(head_query, head_keys, allowed):
    return jnp.where(allowed, product_nt(head_query, head_keys) * SCORE_SCALE, MASKED)


def pattern_lse(queries, keys, allowed):

    def one_head(operands):
        scores = masked_scores(operands[0], operands[1], allowed)
        peak_rows = jnp.max(scores, axis=1, keepdims=True)
        return peak_rows[:, 0] + jnp.log(jnp.sum(jnp.exp(scores - peak_rows), axis=1))

    return lax.map(one_head, (head_major(queries), head_major(keys))).T


def pattern_out(queries, keys, values, allowed, totals):

    def one_head(operands):
        head_query, head_keys, head_values, head_total = operands
        scores = masked_scores(head_query, head_keys, allowed)
        probability = jnp.where(allowed, jnp.exp(scores - head_total[:, None]), 0.0).astype(
            jnp.bfloat16
        )
        return product(probability, head_values)

    return row_major(
        lax.map(one_head, (head_major(queries), head_major(keys), head_major(values), totals.T))
    )


def pattern_back(queries, keys, values, allowed, totals, deltas, grad_out):

    def one_head(operands):
        head_query, head_keys, head_values, head_total, head_delta, head_grad = operands
        scores = masked_scores(head_query, head_keys, allowed)
        probability = jnp.where(allowed, jnp.exp(scores - head_total[:, None]), 0.0)
        grad_probs = product_nt(head_grad, head_values)
        grad_scores = (probability * (grad_probs - head_delta[:, None])).astype(jnp.bfloat16)
        grad_query = product(grad_scores, head_keys) * SCORE_SCALE
        grad_keys = product_tn(grad_scores, head_query) * SCORE_SCALE
        grad_values = product_tn(probability.astype(jnp.bfloat16), head_grad)
        return (grad_query, grad_keys, grad_values)

    results = lax.map(
        one_head,
        (
            head_major(queries),
            head_major(keys),
            head_major(values),
            totals.T,
            deltas.T,
            head_major(grad_out),
        ),
    )
    return (row_major(results[0]), row_major(results[1]), row_major(results[2]))


def body(
    tokens,
    cotangent,
    w_qkv,
    w_attn,
    w_in,
    w_out,
    gains_model,
    biases_model,
    gain_ffn,
    biases_ffn,
    offsets,
):
    gathered = (
        lax.all_gather(w_qkv, ("wide", "narrow"), axis=0, tiled=True),
        lax.all_gather(w_attn, ("wide", "narrow"), axis=0, tiled=True),
        lax.all_gather(w_in, ("wide", "narrow"), axis=0, tiled=True),
        lax.all_gather(w_out, ("wide", "narrow"), axis=0, tiled=True),
        lax.all_gather(gains_model, ("wide", "narrow"), axis=1, tiled=True),
        lax.all_gather(biases_model, ("wide", "narrow"), axis=1, tiled=True),
        lax.all_gather(gain_ffn, ("wide", "narrow"), axis=0, tiled=True),
        lax.all_gather(biases_ffn, ("wide", "narrow"), axis=1, tiled=True),
    )
    qkv_full, attn_full, in_full, out_full = (gathered[0], gathered[1], gathered[2], gathered[3])
    model_gains = gathered[4].astype(jnp.float32)
    model_biases = gathered[5].astype(jnp.float32)
    ffn_gain = gathered[6].astype(jnp.float32)
    ffn_biases = gathered[7].astype(jnp.float32)
    local_rows = tokens.shape[0]
    width = tokens.shape[1]
    inputs = tokens.astype(jnp.float32)
    normed_one, pull_one = jax.vjp(layer_norm, inputs, model_gains[0], model_biases[0])
    normed_low = normed_one.astype(jnp.bfloat16)
    projected = product(normed_low, qkv_full)
    queries = (projected[:, :width] + model_biases[1]).astype(jnp.bfloat16)
    keys = projected[:, width : 2 * width].astype(jnp.bfloat16)
    values = (projected[:, 2 * width :] + model_biases[2]).astype(jnp.bfloat16)
    size_narrow = lax.axis_size("narrow")
    narrow_place = lax.axis_index("narrow")
    dilations = (RATE0, RATE1, RATE2)
    selectors = (one_hot(offsets[0], RATE0), one_hot(offsets[1], RATE1), one_hot(offsets[2], RATE2))
    picked_q = [
        select_rows(queries, selectors[pattern], dilations[pattern]).astype(jnp.bfloat16)
        for pattern in range(3)
    ]
    picked_k = [
        select_rows(keys, selectors[pattern], dilations[pattern]).astype(jnp.bfloat16)
        for pattern in range(3)
    ]
    picked_v = [
        select_rows(values, selectors[pattern], dilations[pattern]).astype(jnp.bfloat16)
        for pattern in range(3)
    ]
    arrived = (
        lax.all_gather(picked_k[0], "narrow", axis=0, tiled=True),
        lax.all_gather(picked_v[0], "narrow", axis=0, tiled=True),
        lax.all_gather(picked_k[1], "narrow", axis=0, tiled=True),
        lax.all_gather(picked_v[1], "narrow", axis=0, tiled=True),
        lax.all_gather(picked_k[2], "narrow", axis=0, tiled=True),
        lax.all_gather(picked_v[2], "narrow", axis=0, tiled=True),
    )
    key_sets = (arrived[0], arrived[2], arrived[4])
    value_sets = (arrived[1], arrived[3], arrived[5])
    allowed_sets = tuple(
        (
            key_mask(local_rows // dilations[pattern], size_narrow, narrow_place)
            for pattern in range(3)
        )
    )
    partial_value = jnp.stack(
        [
            spread_heads(
                pattern_lse(picked_q[pattern], key_sets[pattern], allowed_sets[pattern]),
                selectors[pattern],
                dilations[pattern],
            )
            for pattern in range(3)
        ]
    )
    peak_rows = jnp.max(partial_value, axis=0)
    totals = peak_rows + jnp.log(jnp.sum(jnp.exp(partial_value - peak_rows), axis=0))
    attended = jnp.zeros((local_rows, width), jnp.float32)
    for pattern in range(3):
        pattern_totals = select_heads(totals, selectors[pattern], dilations[pattern])
        result_rows = pattern_out(
            picked_q[pattern],
            key_sets[pattern],
            value_sets[pattern],
            allowed_sets[pattern],
            pattern_totals,
        )
        attended = attended + spread_rows(result_rows, selectors[pattern], dilations[pattern])
    sub_normed, pull_sub = jax.vjp(layer_norm, attended, model_gains[1], model_biases[3])
    sub_low = sub_normed.astype(jnp.bfloat16)
    middle = inputs + product(sub_low, attn_full) + model_biases[4]
    normed_two, pull_two = jax.vjp(layer_norm, middle, model_gains[2], model_biases[5])
    normed_two_low = normed_two.astype(jnp.bfloat16)
    pre_act = product(normed_two_low, in_full) + ffn_biases[0]
    activated, pull_gelu = jax.vjp(gelu_exact, pre_act)
    ffn_normed, pull_ffn = jax.vjp(layer_norm, activated, ffn_gain, ffn_biases[1])
    ffn_low = ffn_normed.astype(jnp.bfloat16)
    outputs = (middle + product(ffn_low, out_full) + model_biases[6]).astype(jnp.bfloat16)
    regathered = (
        lax.all_gather(w_qkv, ("wide", "narrow"), axis=0, tiled=True),
        lax.all_gather(w_attn, ("wide", "narrow"), axis=0, tiled=True),
        lax.all_gather(w_in, ("wide", "narrow"), axis=0, tiled=True),
        lax.all_gather(w_out, ("wide", "narrow"), axis=0, tiled=True),
    )
    qkv_back, attn_back, in_back, out_back = (
        regathered[0],
        regathered[1],
        regathered[2],
        regathered[3],
    )
    grad_out_f = cotangent.astype(jnp.float32)
    grad_w_out = product_tn(ffn_low, cotangent)
    grad_bias_ffo = jnp.sum(cotangent.astype(jnp.float32), axis=0)
    grad_act, grad_gain_ffn, grad_bias_ffn_norm = pull_ffn(product_nt(cotangent, out_back))
    grad_pre = pull_gelu(grad_act)[0].astype(jnp.bfloat16)
    grad_w_in = product_tn(normed_two_low, grad_pre)
    grad_bias_pre = jnp.sum(grad_pre.astype(jnp.float32), axis=0)
    grad_mid_norm, grad_gain_two, grad_bias_two = pull_two(product_nt(grad_pre, in_back))
    grad_middle = grad_out_f + grad_mid_norm
    grad_branch = grad_middle.astype(jnp.bfloat16)
    grad_w_attn = product_tn(sub_low, grad_branch)
    grad_bias_branch = jnp.sum(grad_branch.astype(jnp.float32), axis=0)
    grad_att, grad_gain_sub, grad_bias_sub = pull_sub(product_nt(grad_branch, attn_back))
    grad_att_low = grad_att.astype(jnp.bfloat16)
    deltas = jnp.sum(
        (grad_att_low.astype(jnp.float32) * attended).reshape(local_rows, HEADS, HEAD_DIM), axis=2
    )
    backward_parts = []
    for pattern in range(3):
        backward_parts.append(
            pattern_back(
                picked_q[pattern],
                key_sets[pattern],
                value_sets[pattern],
                allowed_sets[pattern],
                select_heads(totals, selectors[pattern], dilations[pattern]),
                select_heads(deltas, selectors[pattern], dilations[pattern]),
                select_rows(grad_att_low, selectors[pattern], dilations[pattern]).astype(
                    jnp.bfloat16
                ),
            )
        )
    returned = (
        lax.psum_scatter(
            backward_parts[0][1].astype(jnp.bfloat16), "narrow", scatter_dimension=0, tiled=True
        ).astype(jnp.float32),
        lax.psum_scatter(
            backward_parts[0][2].astype(jnp.bfloat16), "narrow", scatter_dimension=0, tiled=True
        ).astype(jnp.float32),
        lax.psum_scatter(
            backward_parts[1][1].astype(jnp.bfloat16), "narrow", scatter_dimension=0, tiled=True
        ).astype(jnp.float32),
        lax.psum_scatter(
            backward_parts[1][2].astype(jnp.bfloat16), "narrow", scatter_dimension=0, tiled=True
        ).astype(jnp.float32),
        lax.psum_scatter(
            backward_parts[2][1].astype(jnp.bfloat16), "narrow", scatter_dimension=0, tiled=True
        ).astype(jnp.float32),
        lax.psum_scatter(
            backward_parts[2][2].astype(jnp.bfloat16), "narrow", scatter_dimension=0, tiled=True
        ).astype(jnp.float32),
    )
    key_grads = (returned[0], returned[2], returned[4])
    value_grads = (returned[1], returned[3], returned[5])
    grad_q = jnp.zeros((local_rows, width), jnp.float32)
    grad_k = jnp.zeros((local_rows, width), jnp.float32)
    grad_v = jnp.zeros((local_rows, width), jnp.float32)
    for pattern in range(3):
        grad_q = grad_q + spread_rows(
            backward_parts[pattern][0], selectors[pattern], dilations[pattern]
        )
        grad_k = grad_k + spread_rows(key_grads[pattern], selectors[pattern], dilations[pattern])
        grad_v = grad_v + spread_rows(value_grads[pattern], selectors[pattern], dilations[pattern])
    grad_q_low = grad_q.astype(jnp.bfloat16)
    grad_v_low = grad_v.astype(jnp.bfloat16)
    grad_qkv = jnp.concatenate([grad_q_low, grad_k.astype(jnp.bfloat16), grad_v_low], axis=1)
    grad_w_qkv = product_tn(normed_low, grad_qkv)
    grad_bias_q = jnp.sum(grad_q_low.astype(jnp.float32), axis=0)
    grad_bias_v = jnp.sum(grad_v_low.astype(jnp.float32), axis=0)
    grad_first, grad_gain_one, grad_bias_one = pull_one(product_nt(grad_qkv, qkv_back))
    grad_inputs = grad_middle + grad_first
    grad_gains = jnp.stack([grad_gain_one, grad_gain_sub, grad_gain_two])
    grad_biases = jnp.stack(
        [
            grad_bias_one,
            grad_bias_q,
            grad_bias_v,
            grad_bias_sub,
            grad_bias_branch,
            grad_bias_two,
            grad_bias_ffo,
        ]
    )
    grad_ffn_biases = jnp.stack([grad_bias_pre, grad_bias_ffn_norm])
    reduced = (
        lax.psum_scatter(grad_w_qkv, ("wide", "narrow"), scatter_dimension=0, tiled=True),
        lax.psum_scatter(grad_w_attn, ("wide", "narrow"), scatter_dimension=0, tiled=True),
        lax.psum_scatter(grad_w_in, ("wide", "narrow"), scatter_dimension=0, tiled=True),
        lax.psum_scatter(grad_w_out, ("wide", "narrow"), scatter_dimension=0, tiled=True),
        lax.psum_scatter(grad_gains, ("wide", "narrow"), scatter_dimension=1, tiled=True),
        lax.psum_scatter(grad_biases, ("wide", "narrow"), scatter_dimension=1, tiled=True),
        lax.psum_scatter(grad_gain_ffn, ("wide", "narrow"), scatter_dimension=0, tiled=True),
        lax.psum_scatter(grad_ffn_biases, ("wide", "narrow"), scatter_dimension=1, tiled=True),
    )
    return (
        outputs,
        grad_inputs,
        reduced[0],
        reduced[1],
        reduced[2],
        reduced[3],
        reduced[4],
        reduced[5],
        reduced[6],
        reduced[7],
    )


BF16 = jnp.bfloat16
F32 = jnp.float32
ALPHA = (
    -2.72614225801306e-10,
    2.77068142495902e-08,
    -2.10102402082508e-06,
    -5.69250639462346e-05,
    -7.34990630326855e-04,
    -2.95459980854025e-03,
    -1.60960333262415e-02,
)
BETA = (
    -1.45660718464996e-05,
    -2.13374055278905e-04,
    -1.68282697438203e-03,
    -7.37332916720468e-03,
    -1.42647390514189e-02,
)


def nn(a, b):
    return lax.dot_general(a, b, (((1,), (0,)), ((), ())), preferred_element_type=F32)


def nt(a, b):
    return lax.dot_general(a, b, (((1,), (1,)), ((), ())), preferred_element_type=F32)


def tn(a, b):
    return lax.dot_general(a, b, (((0,), (0,)), ((), ())), preferred_element_type=F32)


def erf(v):
    v = jnp.clip(v, -4.0, 4.0)
    s = v * v
    top = jnp.full_like(s, ALPHA[0])
    for term in ALPHA[1:]:
        top = top * s + term
    low = jnp.full_like(s, BETA[0])
    for term in BETA[1:]:
        low = low * s + term
    return v * top / low


def normed(v):
    centred = v - jnp.mean(v, axis=-1, keepdims=True)
    rate = lax.rsqrt(jnp.mean(centred * centred, axis=-1, keepdims=True) + EPSILON)
    return centred * rate, rate


def norm_back(e, n, rate, gain):
    t = e * gain
    return rate * (
        t - jnp.mean(t, axis=-1, keepdims=True) - n * jnp.mean(t * n, axis=-1, keepdims=True)
    )


def colsum(v):
    return jnp.sum(v, axis=0, keepdims=True)


def lanes(shape):
    return lax.broadcasted_iota(jnp.int32, shape, len(shape) - 1)


def sublanes(shape):
    return lax.broadcasted_iota(jnp.int32, shape, len(shape) - 2)


def rows_of(parts, count):
    shape = (count, next(part for part in parts if part is not None).shape[1])
    at = sublanes(shape)
    out = jnp.zeros(shape, F32)
    for i, part in enumerate(parts):
        if part is not None:
            out = jnp.where(at == i, part, out)
    return out


def to_rows(columns):
    shape = (columns[0].shape[0], 128)
    at = lanes(shape)
    out = jnp.zeros(shape, F32)
    for i, column in enumerate(columns):
        out = jnp.where(at == i, column, out)
    return out.T[0:8]


def to_columns(rows):
    wide = rows_of(rows, 128).T
    return [wide[:, i : i + 1] for i in range(len(rows))]


def left(v, amount, width):
    return pltpu.roll(v, lax.rem(width - amount, width), 1)


class Place:
    def __getitem__(self, axis):
        return lax.axis_index(("wide", "narrow")[axis])


def call(kernel, outs, *operands, scratch=(), limit=24, final=False, held=True, us=0.0, alias=None):
    whole = pl.BlockSpec(memory_space=pltpu.VMEM)
    space = pltpu.VMEM if held else pltpu.HBM
    placed = [pltpu.with_memory_space_constraint(a, space) for a in operands]
    return pl.pallas_call(
        kernel,
        out_shape=[jax.ShapeDtypeStruct(s, d) if final else pltpu.VMEM(s, d) for s, d in outs],
        in_specs=[whole for _ in operands],
        out_specs=[whole for _ in outs],
        scratch_shapes=[pltpu.VMEM(s, d) for s, d in scratch],
        compiler_params=pltpu.CompilerParams(vmem_limit_bytes=limit << 20),
        cost_estimate=pl.CostEstimate(
            flops=int(us * 1e9), transcendentals=0, bytes_accessed=int(us * 3.6e6)
        ),
        input_output_aliases=alias or {},
        name=kernel.__name__,
    )(*placed)


def offset_of(off, pattern, head):
    row = off[pattern : pattern + 1, :].astype(F32)
    return jnp.sum(jnp.where(lanes(row.shape) == head, row, 0.0), axis=1, keepdims=True)


def prep_kernel(
    wqkv, win, wattn, gains, biases, gffn, bffn, tok, cot, wout, tok_out, cot_out, wout_out,
    b0, b1, b2, b3, small, qs, is_,
):
    idx = Place()
    n = idx[1]
    tok_out[...] = tok[...]
    cot_out[...] = cot[...]
    wout_out[...] = wout[...]
    small[...] = jnp.zeros_like(small)
    small[0:3, 0:24] = gains[...].astype(F32)
    small[3:10, 0:24] = biases[...].astype(F32)
    ffn_g = gffn[...].astype(F32)
    ffn_b = bffn[...].astype(F32)
    for k in range(4):
        small[16 + 8 * k : 17 + 8 * k, 0:24] = ffn_g[:, k * 24 : k * 24 + 24]
        small[17 + 8 * k : 19 + 8 * k, 0:24] = ffn_b[:, k * 24 : k * 24 + 24]
    eye = (sublanes((24, 128)) == lanes((24, 128))).astype(BF16)
    params = nt(eye, small[...].astype(BF16))
    weights = wqkv[...].astype(F32)
    for m in range(4):
        for part in range(3):
            at = part * 768 + m * 192
            qs[m, :, part * 192 : part * 192 + 192] = weights[:, at : at + 192]
        qs[m, :, 576:640] = params
    inner = win[...].astype(F32)
    for m in range(4):
        for w in range(8):
            at = (w * 4 + m) * 96
            is_[m, :, w * 96 : w * 96 + 96] = inner[:, at : at + 96]
    for k, out in enumerate((b0, b1, b2, b3)):
        out[:, 0:640] = qs[n ^ k].astype(BF16)
        out[:, 640:1408] = is_[n ^ k].astype(BF16)
        if k % 2 == 0:
            out[:, 1408:2176] = wattn[...]


def pack_kernel(b0, b1, b2, b3, q_out, r_out, qs, is_, two):
    idx = Place()
    n = idx[1]
    for k, b in enumerate((b0, b1, b2, b3)):
        qs[n ^ k] = b[:, 0:640].astype(F32)
        is_[n ^ k] = b[:, 640:1408].astype(F32)
        if k % 2 == 0:
            two[(n ^ k) // 2] = b[:, 1408:2176].astype(F32)
    q_out[...] = qs[...].reshape(96, 640).astype(BF16)
    r_out[0:96] = is_[...].reshape(96, 768).astype(BF16)
    r_out[96:144] = two[...].reshape(48, 768).astype(BF16)


def place_i_kernel(r0, r1, r2, r3, r4, r5, r6, win, attn):
    idx = Place()
    w = idx[0]
    for j, r in enumerate((r0, r1, r2, r3, r4, r5, r6)):
        win[pl.ds(pl.multiple_of((w ^ j) * 96, 32), 96), :] = r[0:96]
        attn[j] = r[96:144]


def merge_cores(mine, other, core, buf):
    for x_ in range(2):
        buf[x_ * 2 + core] = mine[x_ * 24 : x_ * 24 + 24].astype(F32)
        buf[x_ * 2 + 1 - core] = other[x_ * 24 : x_ * 24 + 24].astype(F32)
    return buf[...].reshape(96, 768).astype(BF16)


def place_a_kernel(mine, other, wattn, buf):
    idx = Place()
    w, core = idx[0], lax.rem(idx[1], 2)
    for j in range(7):
        block = merge_cores(mine[j], other[j], core, buf)
        wattn[pl.ds(pl.multiple_of((w ^ j) * 96, 32), 96), :] = block


def place_last_kernel(win_in, wattn_in, mine, other, win, wattn, buf):
    idx = Place()
    here = pl.ds(pl.multiple_of((idx[0] ^ 7) * 96, 32), 96)
    win[here, :] = mine[0:96]
    block = merge_cores(mine[96:144], other[96:144], lax.rem(idx[1], 2), buf)
    wattn[here, :] = block


def place_c_kernel(r0, r1, r2, r3, r4, r5, r6, wout):
    idx = Place()
    w = idx[0]
    for j, r in enumerate((r0, r1, r2, r3, r4, r5, r6)):
        wout[pl.ds(pl.multiple_of((w ^ j) * 96, 32), 96), :] = r[...]


def place_c_last_kernel(wout_in, block, wout):
    idx = Place()
    wout[pl.ds(pl.multiple_of((idx[0] ^ 7) * 96, 32), 96), :] = block[...]


def place_t_kernel(t0, t1, t2, t3, out):
    idx = Place()
    n = idx[1]
    for k, t in enumerate((t0, t1, t2, t3)):
        out[pl.ds(pl.multiple_of((n ^ k) * 128, 128), 128), :] = t[...]


def norm_kernel(x, n_out):
    n_out[...], _ = normed(x[...].astype(F32))


def attend_kernel(
    off, n1, q0, q1, q2, q3, q4, q5, q6, q7,
    w_out, p_out, a_out, qkv_out, o_t_out, lse_out, o_out,
):
    idx = Place()
    w, n = idx[0], idx[1]
    for j, q in enumerate((q0, q1, q2, q3, q4, q5, q6, q7)):
        w_out[pl.ds(pl.multiple_of((w ^ j) * 96, 32), 96), :] = q[...]
    pick = (sublanes((64, 128)) + 64 == lanes((64, 128))).astype(BF16)
    table = nt(pick, w_out[:, 512:640])
    model = table[0:16]
    ffn = jnp.zeros((8, 768), F32)
    inside = lax.rem(lanes((8, 768)), 96) // 24
    for k in range(4):
        turned = pltpu.roll(table[16 + 8 * k : 24 + 8 * k], lax.rem(768 + (k - n) * 24, 768), 1)
        ffn = jnp.where(inside == k, turned, ffn)
    p_out[0:16] = model
    p_out[16:24] = ffn
    a1 = (n1[...] * model[0:1] + model[3:4]).astype(BF16)
    a_out[...] = a1
    qkv = nn(a1, w_out[...])
    lane = lanes((8, 768))
    bias_q = left(jnp.broadcast_to(model[4:5], (8, 768)), n * 192, 768)
    bias_v = pltpu.roll(
        jnp.broadcast_to(model[5:6], (8, 768)), lax.rem(768 + 384 - n * 192, 768), 1
    )
    bias = jnp.where(
        lane < 192, bias_q, jnp.where((lane >= 384) & (lane < 576), bias_v, 0.0)
    )[0:1, 0:640]
    qkv = jnp.where(lanes((1, 640)) < 576, qkv + bias, 0.0).astype(BF16)
    qkv_out[...] = qkv
    v_t = qkv[:, 384:576].astype(F32).T
    o_parts, lse_rows = [], []
    for h in range(3):
        head = n * 3 + h
        o1, o2 = offset_of(off, 1, head), offset_of(off, 2, head)
        at = lanes((1, 512))
        r1 = (lax.rem(at, 2).astype(F32) == o1).astype(F32)
        r2 = (lax.rem(at, 4).astype(F32) == o2).astype(F32)
        head_v = v_t[h * 64 : h * 64 + 64]
        ones = rows_of([jnp.ones((1, 512), F32), r1, r2], 8)
        left_side = jnp.concatenate([head_v, head_v * r1, head_v * r2, ones], axis=0).astype(BF16)
        head_q = qkv[:, h * 64 : h * 64 + 64] * jnp.asarray(SCORE_SCALE, BF16)
        head_k = qkv[:, 192 + h * 64 : 256 + h * 64]
        blocks, lses = [], []
        for i in range(2):
            keys = 256 * (i + 1)
            scores = nt(head_k[0:keys], head_q[i * 256 : i * 256 + 256])
            shape = (keys, 256)
            scores = jnp.where(sublanes(shape) <= lanes(shape) + i * 256, scores, MASKED)
            peak = jnp.max(scores, axis=0, keepdims=True)
            weight = jnp.exp(scores - peak).astype(BF16)
            both = nn(left_side[:, 0:keys], weight)
            s1, s2 = r1[:, i * 256 : i * 256 + 256], r2[:, i * 256 : i * 256 + 256]
            total = both[192:193] + s1 * both[193:194] + s2 * both[194:195]
            blocks.append((both[0:64] + s1 * both[64:128] + s2 * both[128:192]) / total)
            lses.append(peak + jnp.log(total))
        o_parts.append(jnp.concatenate(blocks, axis=1))
        lse_rows.append(jnp.concatenate(lses, axis=1))
    o_t = jnp.concatenate(o_parts, axis=0)
    o_t_out[...] = o_t
    lse_out[...] = rows_of(lse_rows, 8)
    o_out[...] = o_t.T.astype(BF16)


def sub_norm_kernel(p, o0, o1, o2, o3, n_o_out, rate_o_out, u_out, o_buf):
    idx = Place()
    n = idx[1]
    for k, o in enumerate((o0, o1, o2, o3)):
        o_buf[n ^ k] = o[...].astype(F32)
    o = jnp.concatenate([o_buf[m] for m in range(4)], axis=1)
    n_o, rate_o = normed(o)
    n_o_out[...] = n_o
    rate_o_out[...] = rate_o
    u_out[...] = (n_o * p[1:2] + p[6:7]).astype(BF16)


def middle_kernel(x, p, u, wattn, win, x2_out, h2_out, f_out, dg_out, stat_out):
    x2 = x[...].astype(F32) + nn(u[...], wattn[...]) + p[7:8]
    x2_out[...] = x2
    n2, _ = normed(x2)
    h2 = (n2 * p[2:3] + p[8:9]).astype(BF16)
    h2_out[...] = h2
    c = nn(h2, win[...]) + p[17:18]
    half = 0.5 + 0.5 * erf(c * 0.7071067811865476)
    f = c * half
    f_out[...] = f
    dg_out[...] = half + c * jnp.exp(c * c * -0.5) * 0.3989422804014327
    mean = jnp.mean(f, axis=1, keepdims=True)
    centred = f - mean
    stat_out[...] = to_rows([mean, jnp.sum(centred * centred, axis=1, keepdims=True)])


def cot_kernel(gy, wout, p, f, stat_in, e_out, stat_out):
    e = nt(gy[...], wout[...])
    e_out[...] = e
    t = e * p[16:17]
    mean = to_columns([stat_in[0:1]])[0]
    rows = to_rows(
        [jnp.sum(t, axis=1, keepdims=True), jnp.sum(t * (f[...] - mean), axis=1, keepdims=True)]
    )
    stat_out[...] = jnp.where(sublanes((8, 512)) < 2, stat_in[...], jnp.roll(rows, 2, axis=0))


def ffn_columns(s0, s1, s2, s3):
    parts = [s[...] for s in (s0, s1, s2, s3)]
    count = 768.0 * 4
    mean = sum(s[0:1] for s in parts) * 0.25
    spread = sum(s[1:2] + 768.0 * (s[0:1] - mean) * (s[0:1] - mean) for s in parts) / count
    rate = lax.rsqrt(spread + EPSILON)
    mean_t = sum(s[2:3] for s in parts) / count
    mean_tn = rate * sum(s[3:4] + (s[0:1] - mean) * s[2:3] for s in parts) / count
    return to_columns([mean, rate, mean_t, mean_tn])


def core_halves(value, keep, send, core, buf):
    buf[...] = value
    for x_ in range(2):
        mine = pl.ds(pl.multiple_of((x_ * 2 + core) * 128, 128), 128)
        other = pl.ds(pl.multiple_of((x_ * 2 + 1 - core) * 128, 128), 128)
        keep[x_ * 128 : x_ * 128 + 128, :] = buf[mine, :].astype(keep.dtype)
        send[x_ * 128 : x_ * 128 + 128, :] = buf[other, :].astype(send.dtype)


def ffn_back_kernel(p, s0, s1, s2, s3, f, dg, e, win, gc_out, keep, send, buf):
    idx = Place()
    core = lax.rem(idx[1], 2)
    mean, rate, mean_t, mean_tn = ffn_columns(s0, s1, s2, s3)
    n_f = (f[...] - mean) * rate
    df = rate * (e[...] * p[16:17] - mean_t - n_f * mean_tn)
    gc = (df * dg[...]).astype(BF16)
    gc_out[...] = gc
    core_halves(nt(gc, win[...]), keep, send, core, buf)


def by_wide(value, w, steps, out):
    for i, step in enumerate(steps):
        out[i] = value[pl.ds(pl.multiple_of((w ^ step) * 96, 32), 96), :].astype(BF16)


def ffn_grad_kernel(
    p, s0, s1, s2, s3, f, e, gy, z_out, keep_a, keep_b, send_a, send_b, sums, prod
):
    idx = Place()
    mean, rate, _, _ = ffn_columns(s0, s1, s2, s3)
    n_f = (f[...] - mean) * rate
    z = (n_f * p[16:17] + p[18:19]).astype(BF16)
    z_out[...] = z
    prod[...] = tn(z, gy[...])
    for steps, out in (((2, 6), keep_a), ((0, 4), keep_b), ((3, 7), send_a), ((1, 5), send_b)):
        by_wide(prod, idx[0], steps, out)
    sums[...] = rows_of([colsum(e[...] * n_f), None, colsum(e[...]), None], 8)


def in_grad_kernel(h2, gc, keep_a, keep_b, send_a, send_b, prod):
    idx = Place()
    prod[...] = tn(h2[...], gc[...])
    for steps, out in (((4, 5), keep_a), ((0, 1), keep_b), ((6, 7), send_a), ((2, 3), send_b)):
        by_wide(prod, idx[0], steps, out)


def out_kernel(z, wout, gc, gy, sums_in, keep, send, sums, buf):
    idx = Place()
    core_halves(nn(z[...], wout[...]), keep, send, lax.rem(idx[1], 2), buf)
    extra = rows_of([None, colsum(gc[...].astype(F32)), None, colsum(gy[...].astype(F32))], 8)
    sums[...] = sums_in[...] + extra


def prob_kernel(qkv, lse, *outs):
    for h in range(3):
        low_q = qkv[:, h * 64 : h * 64 + 64] * jnp.asarray(SCORE_SCALE, BF16)
        head_k = qkv[:, 192 + h * 64 : 256 + h * 64]
        for i in range(2):
            keys = 256 * (i + 1)
            here = slice(i * 256, i * 256 + 256)
            shape = (keys, 256)
            scores = nt(head_k[0:keys], low_q[here])
            outs[i][h] = jnp.where(
                sublanes(shape) <= lanes(shape) + i * 256,
                jnp.exp(scores - lse[h : h + 1, here]),
                0.0,
            )


def norm_two_kernel(x2, n2_out, rate_out):
    n2_out[...], rate_out[...] = normed(x2[...])


def add_kernel(keep, got, out):
    out[...] = (keep[...].astype(F32) + got[...].astype(F32)).astype(out.dtype)


def hop_kernel(keep, got, own, send):
    for i in range(2):
        own[i] = keep[2 * i].astype(F32) + got[2 * i].astype(F32)
        send[i] = (keep[2 * i + 1].astype(F32) + got[2 * i + 1].astype(F32)).astype(BF16)


def pair_kernel(keep, got, out):
    for i in range(2):
        out[i] = (keep[i].astype(F32) + got[i].astype(F32)).astype(out.dtype)


def split_kernel(keep, got, first, second):
    first[...] = (keep[0].astype(F32) + got[0].astype(F32)).astype(first.dtype)
    second[...] = (keep[1].astype(F32) + got[1].astype(F32)).astype(second.dtype)


def last_hop_kernel(own, got, mine, send):
    mine[...] = own[0] + got[0].astype(F32)
    send[...] = (own[1] + got[1].astype(F32)).astype(BF16)


def sum_out_kernel(mine, got, out):
    out[...] = mine[...] + got[...].astype(F32)


def mid_back_kernel(
    p, own, own_x, sib, sib_x, n2, rate2, gy, n_o, rate_o, wattn,
    dx2_out, ga_out, do_out, e2_out, eo_out,
):
    idx = Place()
    n = idx[1]
    core = lax.rem(n, 2)
    for x_ in range(2):
        at = slice(x_ * 128, x_ * 128 + 128)
        mine = pl.ds(pl.multiple_of((x_ * 2 + core) * 128, 128), 128)
        other = pl.ds(pl.multiple_of((x_ * 2 + 1 - core) * 128, 128), 128)
        e2_out[mine, :] = own[at].astype(F32) + own_x[at].astype(F32)
        e2_out[other, :] = sib[at].astype(F32) + sib_x[at].astype(F32)
    dx2 = gy[...].astype(F32) + norm_back(e2_out[...], n2[...], rate2[...], p[2:3])
    dx2_out[...] = dx2
    ga = dx2.astype(BF16)
    ga_out[...] = ga
    eo = nt(ga, wattn[...])
    eo_out[...] = eo
    d_o = norm_back(eo, n_o[...], rate_o[...], p[1:2])
    for m in range(4):
        @pl.when(n == m)
        def _():
            do_out[...] = d_o[:, m * 192 : m * 192 + 192].astype(BF16)


def attn_grad_kernel(u, ga, eo, n_o, e2, n2, sums, keep, send, gat):
    idx = Place()
    w, n = idx[0], idx[1]
    e_o, e_2 = eo[...], e2[...]
    model = rows_of(
        [
            None,
            colsum(e_o * n_o[...]),
            colsum(e_2 * n2[...]),
            None,
            None,
            None,
            colsum(e_o),
            colsum(ga[...].astype(F32)),
            colsum(e_2),
            sums[3:4],
        ],
        16,
    )
    gat[...] = tn(u[...], ga[...]).reshape(8, 4, 24, 768)
    for i in range(8):
        to = w ^ i
        block = (keep if i % 2 == 0 else send).at[i // 2]
        mine = left(model, to * 96 + n * 24, 768)
        ffn = left(sums[...], to * 96, 768)
        extra = jnp.concatenate(
            [mine[0:8, 0:128], mine[8:16, 0:128], ffn[:, 0:128], jnp.zeros((8, 384), F32)], axis=1
        )
        block[...] = jnp.concatenate([gat[to, n], extra], axis=0).astype(BF16)


def head_back_kernel(
    off, qkv, o_t, p0, p1, do, a1, wqkv, n1,
    keep_a, keep_b, send_a, send_b, d_keep, d_send, buf, prod,
):
    idx = Place()
    w, n = idx[0], idx[1]
    core = lax.rem(n, 2)
    do_t = do[...].astype(F32).T
    k_t = qkv[:, 192:384].astype(F32).T
    row = lanes((1, 512))
    column = sublanes((512, 1))
    dq_parts, dk_parts, dv_parts = [], [], []
    for h in range(3):
        head = n * 3 + h
        o1, o2 = offset_of(off, 1, head), offset_of(off, 2, head)
        r1 = (lax.rem(row, 2).astype(F32) == o1).astype(F32)
        r2 = (lax.rem(row, 4).astype(F32) == o2).astype(F32)
        c1 = (lax.rem(column, 2).astype(F32) == o1).astype(F32)
        c2 = (lax.rem(column, 4).astype(F32) == o2).astype(F32)
        span = slice(h * 64, h * 64 + 64)
        delta = colsum(do_t[span] * o_t[span, :])
        head_q = qkv[:, h * 64 : h * 64 + 64].astype(F32) * SCORE_SCALE
        head_v = qkv[:, 384 + h * 64 : 448 + h * 64]
        head_do = do[:, h * 64 : h * 64 + 64]
        do_f = head_do.astype(F32)
        q_all = jnp.concatenate([head_q, head_q * c1, head_q * c2], axis=1).astype(BF16)
        do_all = jnp.concatenate([do_f, do_f * c1, do_f * c2], axis=1).astype(BF16)
        kt = k_t[span]
        k_all = jnp.concatenate([kt, kt * r1, kt * r2], axis=0).astype(BF16)
        dk = jnp.zeros((512, 192), F32)
        dv = jnp.zeros((512, 192), F32)
        dq_blocks = []
        for i in range(2):
            keys = 256 * (i + 1)
            here = slice(i * 256, i * 256 + 256)
            prob = (p0, p1)[i][h]
            grad_p = nt(head_v[0:keys], head_do[here])
            grad_s = (prob * (grad_p - delta[:, here])).astype(BF16)
            dv_i = nn(prob.astype(BF16), do_all[here])
            dk_i = nn(grad_s, q_all[here])
            if keys < 512:
                zero = jnp.zeros((512 - keys, 192), F32)
                dv_i = jnp.concatenate([dv_i, zero], axis=0)
                dk_i = jnp.concatenate([dk_i, zero], axis=0)
            dv = dv + dv_i
            dk = dk + dk_i
            dq_i = nn(k_all[:, 0:keys], grad_s)
            dq_blocks.append(dq_i[0:64] + r1[:, here] * dq_i[64:128] + r2[:, here] * dq_i[128:192])
        dq_parts.append(jnp.concatenate(dq_blocks, axis=1) * SCORE_SCALE)
        dk_parts.append(dk[:, 0:64] + c1 * dk[:, 64:128] + c2 * dk[:, 128:192])
        dv_parts.append(dv[:, 0:64] + c1 * dv[:, 64:128] + c2 * dv[:, 128:192])
    dq = jnp.concatenate(dq_parts, axis=0).T
    g = jnp.concatenate([dq] + dk_parts + dv_parts + [jnp.zeros((512, 64), F32)], axis=1)
    g = g.astype(BF16)
    prod[...] = tn(a1[...], g)
    grad = nt(g, wqkv[...])
    outer = rows_of([None, colsum(grad * n1[...]), colsum(grad)], 8)
    g_sum = colsum(g.astype(F32))
    for i in range(8):
        to = w ^ i
        block = ((keep_b, keep_a), (send_b, send_a))[i % 2][i // 2 % 2].at[i // 4]
        turned = left(outer, to * 96, 768)[:, 0:640]
        extra = jnp.where(sublanes((8, 640)) == 0, g_sum, turned)
        mine = prod[pl.ds(pl.multiple_of(to * 96, 32), 96), :]
        block[...] = jnp.concatenate([mine, extra], axis=0).astype(BF16)
    core_halves(grad, d_keep, d_send, core, buf)


def tail_add_kernel(ok, og, dk, dg, keep, send, buf):
    idx = Place()
    x_ = idx[1] // 2
    buf[:, 0:768] = ok[...].astype(F32) + og[...].astype(F32)
    buf[:, 768:1536] = dk[...].astype(F32) + dg[...].astype(F32)
    keep[...] = buf[pl.ds(pl.multiple_of(x_ * 128, 128), 128), :]
    send[...] = buf[pl.ds(pl.multiple_of((1 - x_) * 128, 128), 128), :].astype(BF16)


def token_kernel(p, keep, got, tok, x2, dx2, out, grad):
    idx = Place()
    mine = pl.ds(pl.multiple_of(idx[1] * 128, 128), 128)
    both = keep[...] + got[...].astype(F32)
    out[...] = (x2[mine, :] + both[:, 0:768] + p[9:10]).astype(BF16)
    n1, rate = normed(tok[...].astype(F32))
    grad[...] = dx2[mine, :] + norm_back(both[:, 768:1536], n1, rate, p[0:1])


def sum_in_kernel(mine, got, own, t1, t2, t3, buf):
    idx = Place()
    n = idx[1]
    buf[...] = (mine[...] + got[...].astype(F32)).reshape(4, 24, 768)
    own[...] = buf[n]
    for k, out in enumerate((t1, t2, t3)):
        out[...] = buf[n ^ (k + 1)].astype(BF16)


def sum_qkv_kernel(mine, z1, z2, z3, own, t1, t2, t3, buf):
    idx = Place()
    n = idx[1]
    total = mine[...] + z1[...].astype(F32) + z2[...].astype(F32) + z3[...].astype(F32)
    buf[...] = total[0:96].reshape(4, 24, 640)
    own[0:24] = buf[n]
    own[24:32] = total[96:104]
    for k, out in enumerate((t1, t2, t3)):
        out[...] = jnp.concatenate([buf[n ^ (k + 1)], total[96:104]], axis=0).astype(BF16)


def final_in_kernel(i0, i1, i2, i3, out, buf):
    idx = Place()
    n = idx[1]
    for k, i in enumerate((i0, i1, i2, i3)):
        buf[n ^ k] = i[...].astype(F32)
    for m in range(4):
        block = buf[m]
        for w in range(8):
            at = (w * 4 + m) * 96
            out[:, at : at + 96] = block[:, w * 96 : w * 96 + 96]


def final_kernel(q0, q1, q2, q3, a_mine, a_got, gq, gattn, gains, biases, gffn, bffn, buf):
    idx = Place()
    w, n = idx[0], idx[1]
    total = a_mine[...] + a_got[...].astype(F32)
    gattn[...] = total[0:24]
    extra = total[24:32]
    for k, q in enumerate((q0, q1, q2, q3)):
        buf[n ^ k] = q[...].astype(F32)
    for m in range(4):
        block = buf[m]
        for part in range(3):
            at = part * 768 + m * 192
            gq[:, at : at + 192] = block[0:24, part * 192 : part * 192 + 192]
    tails = [buf[m][24:32] for m in range(4)]
    q_row = jnp.concatenate([t[:, 0:192] for t in tails], axis=1)
    v_row = jnp.concatenate([t[:, 384:576] for t in tails], axis=1)
    place = (w * 4 + n) * 24
    q_row = left(q_row, place, 768)[0:1, 0:24]
    v_row = left(v_row, place, 768)[0:1, 0:24]
    norm = left((tails[0] + tails[1] + tails[2] + tails[3])[:, 0:128], n * 24, 128)[:, 0:24]
    low, high, ffn = extra[:, 0:24], extra[:, 128:152], extra[:, 256:352]
    gains[0:1] = norm[1:2]
    gains[1:3] = low[1:3]
    biases[0:1] = norm[2:3]
    biases[1:2] = q_row
    biases[2:3] = v_row
    biases[3:5] = low[6:8]
    biases[5:7] = high[0:2]
    gffn[...] = ffn[0:1]
    bffn[...] = ffn[1:3]


def swap(values, axis, size, step):
    return lax.ppermute(values, axis, [(i, i ^ step) for i in range(size)])


def Y(v):
    return swap(v, "wide", 8, 1)


def Z1(v):
    return swap(v, "wide", 8, 2)


def Z2(v):
    return swap(v, "wide", 8, 4)


def Z3(v):
    return swap(v, "wide", 8, 6)


def C(v):
    return swap(v, "narrow", 4, 1)


def X(v):
    return swap(v, "narrow", 4, 2)


def XC(v):
    return swap(v, "narrow", 4, 3)


class Names:
    def __getattr__(self, name):
        return name


N = Names()


TABLE = (
    (N.cy, 1, 4), (N.ry, 4, 6), (N.b1, 0, 2), (N.b3, 0, 2), (N.qy, 2, 4), (N.b2, 0, 0), (N.q2y, 4, 6),
    (N.pack, 2, 5), (N.q1, 2, 4), (N.txc, 6, 0), (N.q2, 2, 6), (N.r1, 4, 6), (N.tc, 2, 6), (N.q1y, 4, 5),
    (N.x, 6, 10), (N.gx, 6, 8), (N.tx, 4, 6), (N.r1y, 6, 7), (N.c2y, 6, 9), (N.q3, 4, 6), (N.c2, 6, 0),
    (N.r2, 4, 6), (N.n1, 6, 14), (N.r3, 6, 7), (N.c1, 3, 7), (N.q3y, 4, 6), (N.c3, 6, 10), (N.c1y, 6, 10),
    (N.ox, 8, 10), (N.r3y, 6, 10), (N.oc, 10, 0), (N.c3y, 11, 14), (N.gy, 8, 17), (N.attend, 6, 8),
    (N.place_i, 7, 9), (N.gxc, 8, 0), (N.ac, 10, 0), (N.r2y, 6, 7), (N.gc, 5, 0), (N.sub, 10, 13),
    (N.place_l, 10, 0), (N.oxc, 10, 0), (N.place_a, 10, 0), (N.middle, 10, 18), (N.s3, 14, 0),
    (N.s2, 14, 15), (N.dx, 17, 18), (N.dc, 14, 0), (N.r3yc, 10, 0), (N.place_c, 12, 14),
    (N.place_cl, 14, 15), (N.s1, 14, 0), (N.ffn_back, 14, 0), (N.e, 14, 0), (N.in_grad, 14, 0),
    (N.add, 16, 0), (N.ds, 18, 0), (N.n2, 18, 19), (N.ffn_grad, 15, 0), (N.out, 16, 20), (N.out_b, 18, 20),
    (N.dxc, 18, 0), (N.prob, 19, 0), (N.in_a, 16, 18), (N.mid, 18, 20), (N.opc, 18, 19), (N.out_z, 20, 22),
    (N.in_b, 17, 20), (N.out_a, 16, 0), (N.in_on, 18, 19), (N.qa, 20, 0), (N.out_on, 18, 20), (N.qb, 20, 0),
    (N.qz1, 20, 0), (N.split_b, 20, 21), (N.out_own, 18, 22), (N.in_own, 20, 0), (N.at_y, 19, 22),
    (N.qz3, 20, 0), (N.split_a, 20, 0), (N.attn_grad, 19, 0), (N.head, 19, 0), (N.in_z, 20, 0),
    (N.out_last, 22, 0), (N.tail, 20, 0), (N.qz2, 20, 24), (N.tail_add, 20, 0), (N.in_y, 22, 0),
    (N.out_z2, 22, 0), (N.token, 25, 27), (N.at_hop, 22, 0), (N.tc_g, 20, 0), (N.at_z2, 23, 0),
    (N.n2q, 23, 25), (N.sum_out, 25, 26), (N.at_last, 22, 25), (N.i3, 22, 0), (N.at_z1, 22, 0),
    (N.in_last, 20, 0), (N.n1q, 21, 25), (N.sum_qkv, 21, 0), (N.n3q, 24, 27), (N.sum_in, 22, 0),
    (N.i1, 22, 0), (N.i2, 22, 0), (N.final_in, 22, 28), (N.final, 32, 0),
)


def steps(env):
    offsets = env[N.offsets]
    two, two_f = ((2, 96, 768), BF16), ((2, 96, 768), F32)
    full, full_f, half, half_f = (
        ((512, 768), BF16), ((512, 768), F32), ((256, 768), BF16), ((256, 768), F32),
    )
    sq = ((768, 768), BF16)
    blk, blk2 = ((104, 640), BF16), ((2, 104, 640), BF16)

    def kernel(name, body, outs, ins, lead=(), results=None, **keys):
        results = results or (name,)
        table[name] = (
            tuple(ins), results, lambda *a: call(body, outs, *lead, *a, us=COST.get(name, 0.0), **keys)
        )

    def move(name, how, source):
        table[name] = ((source,), (name,), lambda a: (how(a),))

    table = {}
    for name, how, source in (
        (N.b1, C, N.b1_s), (N.b2, X, N.b2_s), (N.b3, XC, N.b3_s), (N.cy, Y, N.w_out),
        (N.qy, Y, N.q), (N.q1, Z1, N.q), (N.q2, Z2, N.q), (N.q3, Z1, N.q2), (N.q1y, Y, N.q1),
        (N.q2y, Y, N.q2), (N.q3y, Y, N.q3), (N.ry, Y, N.r), (N.r1, Z1, N.r), (N.r2, Z2, N.r),
        (N.r3, Z1, N.r2), (N.r1y, Y, N.r1), (N.r2y, Y, N.r2), (N.r3y, Z1, N.r2y),
        (N.c1, Z1, N.w_out), (N.c2, Z2, N.w_out), (N.c3, Z1, N.c2), (N.c1y, Y, N.c1),
        (N.c2y, Y, N.c2), (N.c3y, Y, N.c3), (N.tc, C, N.tokens), (N.tx, X, N.tokens), (N.txc, C, N.tx),
        (N.gc, C, N.cotangent), (N.gx, X, N.cotangent), (N.gxc, C, N.gx),
        (N.oc, C, N.o_low), (N.ox, X, N.o_low), (N.oxc, C, N.ox), (N.ac, C, N.attn), (N.r3yc, C, N.r3y),
        (N.s1, C, N.stats), (N.s2, X, N.stats), (N.s3, XC, N.stats), (N.dc, C, N.d_send),
        (N.dx, X, N.d_half), (N.ds, C, N.d_half), (N.dxc, C, N.dx), (N.out_a, Y, N.out_sa),
        (N.out_b, Y, N.out_sb), (N.in_a, Z1, N.in_sa), (N.in_b, Z1, N.in_sb), (N.opc, C, N.op_send),
        (N.qa, Y, N.qkv_a), (N.qb, Y, N.qkv_b), (N.out_z, Z1, N.out_on), (N.in_z, Z2, N.in_on),
        (N.tc_g, C, N.t_send), (N.at_y, Y, N.at_send), (N.qz1, Z1, N.send_1), (N.qz2, Z2, N.send_2),
        (N.qz3, Z3, N.send_3), (N.out_z2, Z2, N.out_to), (N.tail, X, N.tail_send), (N.in_y, Y, N.in_to),
        (N.at_z1, Z1, N.at_on), (N.at_z2, Z2, N.at_to), (N.i1, C, N.i1_s), (N.i2, X, N.i2_s),
        (N.i3, XC, N.i3_s), (N.n1q, C, N.n1_s), (N.n2q, X, N.n2_s), (N.n3q, XC, N.n3_s),
    ):
        move(name, how, source)
    kernel(
        N.pack, pack_kernel, [((96, 640), BF16), ((144, 768), BF16)], (N.b0, N.b1, N.b2, N.b3), (), (N.q, N.r),
        scratch=[((4, 24, 640), F32), ((4, 24, 768), F32), ((2, 24, 768), F32)],
    )
    kernel(N.x, place_t_kernel, [full], (N.tokens, N.tc, N.tx, N.txc))
    kernel(N.n1, norm_kernel, [full_f], (N.x,))
    kernel(
        N.attend, attend_kernel,
        [
            ((768, 640), BF16), ((24, 768), F32), full, ((512, 640), BF16), ((192, 512), F32),
            ((8, 512), F32), ((512, 192), BF16),
        ],
        (N.n1, N.q, N.qy, N.q1, N.q1y, N.q2, N.q2y, N.q3, N.q3y), (offsets,),
        (N.wqkv, N.params, N.a1, N.qkv, N.o_t, N.lse, N.o_low),
    )
    kernel(N.gy, place_t_kernel, [full], (N.cotangent, N.gc, N.gx, N.gxc))
    kernel(
        N.place_i, place_i_kernel, [sq, ((7, 48, 768), BF16)], (N.r, N.ry, N.r1, N.r1y, N.r2, N.r2y, N.r3), (),
        (N.win_7, N.attn),
    )
    kernel(N.place_a, place_a_kernel, [sq], (N.attn, N.ac), (), (N.wattn_7,), scratch=[((4, 24, 768), F32)])
    kernel(
        N.place_l, place_last_kernel, [sq, sq], (N.win_7, N.wattn_7, N.r3y, N.r3yc), (), (N.win, N.wattn),
        scratch=[((4, 24, 768), F32)], alias={0: 0, 1: 1},
    )
    kernel(
        N.sub, sub_norm_kernel, [full_f, ((512, 1), F32), full], (N.params, N.o_low, N.oc, N.ox, N.oxc), (),
        (N.n_o, N.rate_o, N.u), scratch=[((4, 512, 192), F32)],
    )
    kernel(
        N.middle, middle_kernel, [full_f, full, full_f, full_f, ((8, 512), F32)],
        (N.x, N.params, N.u, N.wattn, N.win), (), (N.x2, N.h2, N.f, N.dg, N.stat_f),
    )
    kernel(
        N.place_c, place_c_kernel, [sq], (N.w_out, N.cy, N.c1, N.c1y, N.c2, N.c2y, N.c3), (), (N.wout_7,)
    )
    kernel(N.place_cl, place_c_last_kernel, [sq], (N.wout_7, N.c3y), (), (N.wout,), alias={0: 0})
    kernel(
        N.e, cot_kernel, [full_f, ((8, 512), F32)], (N.gy, N.wout, N.params, N.f, N.stat_f), (), (N.e, N.stats)
    )
    stats = (N.params, N.stats, N.s1, N.s2, N.s3)
    kernel(
        N.ffn_back, ffn_back_kernel, [full, half_f, half], (*stats, N.f, N.dg, N.e, N.win), (),
        (N.gc_f, N.d_keep, N.d_send), scratch=[full_f],
    )
    kernel(N.add, add_kernel, [half], (N.d_keep, N.dc), (), (N.d_half,))
    kernel(
        N.ffn_grad, ffn_grad_kernel, [full, two, two, two, two, ((8, 768), F32)],
        (*stats, N.f, N.e, N.gy), (), (N.z, N.out_ka, N.out_kb, N.out_sa, N.out_sb, N.sums_f),
        scratch=[((768, 768), F32)],
    )
    kernel(
        N.in_grad, in_grad_kernel, [two] * 4, (N.h2, N.gc_f), (), (N.in_ka, N.in_kb, N.in_sa, N.in_sb),
        scratch=[((768, 768), F32)],
    )
    kernel(
        N.out, out_kernel, [half_f, half, ((8, 768), F32)], (N.z, N.wout, N.gc_f, N.gy, N.sums_f), (),
        (N.op_keep, N.op_send, N.sums), scratch=[full_f],
    )
    kernel(
        N.prob, prob_kernel, [((3, 256, 256), F32), ((3, 512, 256), F32)], (N.qkv, N.lse), (), (N.p0, N.p1)
    )
    kernel(N.n2, norm_two_kernel, [full_f, ((512, 1), F32)], (N.x2,), (), (N.n2, N.rate2))
    kernel(
        N.mid, mid_back_kernel, [full_f, full, ((512, 192), BF16), full_f, full_f],
        (N.params, N.d_half, N.dx, N.ds, N.dxc, N.n2, N.rate2, N.gy, N.n_o, N.rate_o, N.wattn), (),
        (N.dx2, N.ga, N.do, N.e2, N.eo),
    )
    kernel(
        N.head, head_back_kernel, [blk2, blk2, blk2, blk2, half_f, half],
        (N.qkv, N.o_t, N.p0, N.p1, N.do, N.a1, N.wqkv, N.n1), (offsets,),
        (N.keep_a, N.keep_b, N.qkv_a, N.qkv_b, N.t_keep, N.t_send), scratch=[full_f, ((768, 640), F32)],
    )
    kernel(N.out_on, pair_kernel, [two], (N.out_ka, N.out_a))
    kernel(N.in_on, pair_kernel, [two], (N.in_ka, N.in_a))
    kernel(N.out_own, pair_kernel, [two_f], (N.out_kb, N.out_b))
    kernel(N.in_own, pair_kernel, [two_f], (N.in_kb, N.in_b))
    kernel(
        N.attn_grad, attn_grad_kernel, [((4, 32, 768), BF16)] * 2, (N.u, N.ga, N.eo, N.n_o, N.e2, N.n2, N.sums), (),
        (N.at_keep, N.at_send), scratch=[((8, 4, 24, 768), F32)],
    )
    kernel(N.split_a, split_kernel, [blk, blk], (N.keep_a, N.qa), (), (N.send_1, N.send_3))
    kernel(N.split_b, split_kernel, [((104, 640), F32), blk], (N.keep_b, N.qb), (), (N.q_sum, N.send_2))
    block = [((96, 768), F32), ((96, 768), BF16)]
    kernel(N.out_last, last_hop_kernel, block, (N.out_own, N.out_z), (), (N.out_mine, N.out_to))
    kernel(N.in_last, last_hop_kernel, block, (N.in_own, N.in_z), (), (N.in_mine, N.in_to))
    kernel(
        N.at_hop, hop_kernel, [((2, 32, 768), F32), ((2, 32, 768), BF16)], (N.at_keep, N.at_y), (), (N.at_own, N.at_on)
    )
    kernel(
        N.at_last, last_hop_kernel, [((32, 768), F32), ((32, 768), BF16)], (N.at_own, N.at_z1), (),
        (N.at_mine, N.at_to),
    )
    kernel(
        N.tail_add, tail_add_kernel, [((128, 1536), F32), ((128, 1536), BF16)],
        (N.op_keep, N.opc, N.t_keep, N.tc_g), (), (N.tail_keep, N.tail_send), scratch=[((256, 1536), F32)],
    )
    kernel(
        N.token, token_kernel, [((128, 768), BF16), ((128, 768), F32)],
        (N.params, N.tail_keep, N.tail, N.tokens, N.x2, N.dx2), (), (N.outputs, N.grad_inputs), final=True,
    )
    kernel(
        N.sum_out, sum_out_kernel, [((96, 768), F32)], (N.out_mine, N.out_z2), (), (N.grad_w_out,), final=True
    )
    small = ((24, 768), BF16)
    kernel(
        N.sum_in, sum_in_kernel, [((24, 768), F32), small, small, small], (N.in_mine, N.in_y), (),
        (N.i_own, N.i1_s, N.i2_s, N.i3_s), scratch=[((4, 24, 768), F32)],
    )
    kernel(
        N.final_in, final_in_kernel, [((24, 3072), F32)], (N.i_own, N.i1, N.i2, N.i3), (), (N.grad_w_in,),
        scratch=[((4, 24, 768), F32)], final=True,
    )
    row = ((32, 640), BF16)
    kernel(
        N.sum_qkv, sum_qkv_kernel, [((32, 640), F32), row, row, row], (N.q_sum, N.qz1, N.qz2, N.qz3), (),
        (N.q_mine, N.n1_s, N.n2_s, N.n3_s), scratch=[((4, 24, 640), F32)],
    )
    kernel(
        N.final, final_kernel,
        [
            ((24, 2304), F32), ((24, 768), F32), ((3, 24), F32), ((7, 24), F32), ((1, 96), F32), ((2, 96), F32),
        ],
        (N.q_mine, N.n1q, N.n2q, N.n3q, N.at_mine, N.at_z2), (),
        (N.grad_w_qkv, N.grad_w_attn, N.grad_gains, N.grad_biases, N.grad_gain_ffn, N.grad_ffn_biases),
        scratch=[((4, 32, 640), F32)], final=True,
    )
    return table


COST = dict(attend=8.0, middle=0.3, ffn_back=4.0, ffn_grad=4.0, in_grad=8.0, out=2.0, mid=1.0, attn_grad=8.0)


def fast_body(
    tokens, cotangent, w_qkv, w_attn, w_in, w_out, gains_model, biases_model, gain_ffn, biases_ffn, offsets
):
    env = {N.offsets: offsets}
    first = (N.tokens, N.cotangent, N.w_out, N.b0, N.b1_s, N.b2_s, N.b3_s)
    outs = call(
        prep_kernel,
        [((128, 768), BF16), ((128, 768), BF16), ((96, 768), BF16)]
        + [((24, 2176 if k % 2 == 0 else 1408), BF16) for k in range(4)],
        w_qkv, w_in, w_attn, gains_model, biases_model, gain_ffn[None], biases_ffn,
        tokens, cotangent, w_out,
        scratch=[((64, 128), F32), ((4, 24, 640), F32), ((4, 24, 768), F32)], held=False,
    )
    env.update(zip(first, outs))
    table = steps(env)
    for slot in range(max(at for _, at, _ in TABLE) + 1):
        now = [name for name, at, _ in TABLE if at == slot]
        tied = [r for name, _, done in TABLE if done == slot and done > 0 for r in table[name][1]]
        tied += [v for name in now for v in table[name][0] if v in env]
        tied = list(dict.fromkeys(tied))
        if slot and tied:
            env.update(zip(tied, lax.optimization_barrier(tuple(env[v] for v in tied))))
        while now:
            name = next(n for n in now if all(v in env for v in table[n][0]))
            now.remove(name)
            ins, results, run = table[name]
            env.update(zip(results, run(*(env[v] for v in ins))))
    return (
        env[N.outputs], env[N.grad_inputs], env[N.grad_w_qkv], env[N.grad_w_attn], env[N.grad_w_in],
        env[N.grad_w_out], env[N.grad_gains], env[N.grad_biases], env[N.grad_gain_ffn][0],
        env[N.grad_ffn_biases],
    )


def solution(mesh):
    fast = dict(mesh.shape) == {"wide": 8, "narrow": 4}
    return jax.shard_map(
        fast_body if fast else body,
        mesh=mesh,
        in_specs=(
            P(("wide", "narrow"), None),
            P(("wide", "narrow"), None),
            P(("wide", "narrow"), None),
            P(("wide", "narrow"), None),
            P(("wide", "narrow"), None),
            P(("wide", "narrow"), None),
            P(None, ("wide", "narrow")),
            P(None, ("wide", "narrow")),
            P(("wide", "narrow")),
            P(None, ("wide", "narrow")),
            P(),
        ),
        out_specs=(
            P(("wide", "narrow"), None),
            P(("wide", "narrow"), None),
            P(("wide", "narrow"), None),
            P(("wide", "narrow"), None),
            P(("wide", "narrow"), None),
            P(("wide", "narrow"), None),
            P(None, ("wide", "narrow")),
            P(None, ("wide", "narrow")),
            P(("wide", "narrow")),
            P(None, ("wide", "narrow")),
        ),
        check_vma=False,
    )
```
